32 devices in a mesh: seq: 32 (over z, y, x, core), ch: 1.
Axes of the slice: x: 2, y: 2, z: 4, core: 2. Of those that a mesh axis runs over, the one named last changes fastest.
Arguments:
- q_feat: bfloat16 [8192, 4096], P('seq', 'ch'), may hold values from -6 to 6
- k_feat: bfloat16 [8192, 4096], P('seq', 'ch'), may hold values from -6 to 6
- v_feat: bfloat16 [8192, 4096], P('seq', 'ch'), may hold values from -6 to 6
- short_taps: float32 [3, 3, 4096], P(None, None, 'ch'), may hold values from -3.5 to 3.5
- decay_rate: float32 [16, 4096], P(None, 'ch'), may hold values from 0 to 1, as said below
- residue: float32 [16, 4096], P(None, 'ch'), may hold values from -1 to 1
- skip_gain: float32 [4096], P('ch'), may hold values from -6 to 6
- out_weight: bfloat16 [4096, 4096], P('seq', 'ch'), may hold values from -0.09375 to 0.09375
- doc_starts: int32 [32, 4], P('seq'), may hold values from 0 to 256, as said below
- reset_flags: int32 [32, 4], P('seq'), may hold values from 0 to 1, as said below
Outputs:
- mixer_out: bfloat16 [8192, 4096], P('seq', 'ch')
The draws below stay inside these ranges and needn't reach their ends.
Inputs may be any that keep to these rules, and one draw needn't show every extreme that they name: `doc_starts`: row s lists ascending the offsets within shard s at which documents begin, then unused slots holding 256; a shard holds at most 4 starts, some shard exactly 4, some shard none. `reset_flags`: only used slots hold 1; in each shard at most one slot holds 1, and some shard has one. `decay_rate`: positive rates.
All inputs are finite; a program needn't handle non-finite values.
Results may differ from the reference program's by a relative error of at most 0.018.
Values may be sent and summed in bfloat16 or wider, within the bound.
A program may use at most 256 MiB of HBM per device.

```python
import jax
import jax.numpy as jnp
from jax import lax

D = 4096
MODES = 16
SHORT = 3
BLOCK = 128
SLOTS = 4
TOK = 256
SHARDS = 32
SEQLEN = 8192
GROUP = 4096
N_CH = 1


def rate_table(key):
    picker = jax.random.uniform(jax.random.fold_in(key, 11), (MODES, D))
    fast_rate = jnp.exp(jax.random.uniform(jax.random.fold_in(key, 12), (MODES, D), minval=jnp.log(1.0 / 50.0), maxval=jnp.log(1.0 / 30.0)))
    middle_rate = jnp.exp(jax.random.uniform(jax.random.fold_in(key, 14), (MODES, D), minval=jnp.log(0.25), maxval=jnp.log(2.5))) / TOK
    slow_rate = jnp.exp(jax.random.uniform(jax.random.fold_in(key, 13), (MODES, D), minval=jnp.log(0.1), maxval=jnp.log(2.0))) / SEQLEN
    fast_share = 0.3
    middle_share = 0.3
    chosen = jnp.where(picker < fast_share, fast_rate, jnp.where(picker < fast_share + middle_share, middle_rate, slow_rate))
    return chosen.astype(jnp.float32)


def draw_decay_rate(key, part):
    return rate_table(key)


def draw_residue(key, part):
    rates = rate_table(key)
    base = jnp.clip(jax.random.normal(jax.random.fold_in(key, 22), (MODES, D)), -4.0, 4.0)
    return (0.35 * base * jnp.sqrt(-jnp.expm1(-2.0 * rates))).astype(jnp.float32)


def shard_layout(key):
    base = jax.random.fold_in(key, 7)
    shard_ids = jnp.arange(SHARDS, dtype=jnp.int32)
    full_shard = jax.random.randint(jax.random.fold_in(base, 1), (), 0, SHARDS)
    counts = jax.random.randint(jax.random.fold_in(base, 2), (SHARDS,), 0, SLOTS + 1)
    counts = jnp.where(shard_ids == full_shard, SLOTS, counts)
    counts = jnp.where(shard_ids == (full_shard + 1) % SHARDS, 0, counts)
    scores = jax.random.randint(jax.random.fold_in(base, 3), (SHARDS, TOK), 0, 65536) * TOK + jnp.arange(TOK, dtype=jnp.int32)[None, :]
    _, chosen = lax.top_k(scores, SLOTS)
    chosen = jnp.sort(chosen, axis=1)
    slot_ids = jnp.arange(SLOTS, dtype=jnp.int32)[None, :]
    used_slot = slot_ids < counts[:, None]
    starts = jnp.where(used_slot, chosen, TOK).astype(jnp.int32)
    picked = jax.random.randint(jax.random.fold_in(base, 4), (SHARDS,), 0, 65536) % jnp.maximum(counts, 1)
    coins = (jax.random.randint(jax.random.fold_in(base, 5), (SHARDS,), 0, 16) == 0) | (shard_ids == full_shard)
    flags = ((slot_ids == picked[:, None]) & used_slot & coins[:, None]).astype(jnp.int32)
    return (starts, flags)


def draw_doc_starts(key, part):
    return shard_layout(key)[0]


def draw_reset_flags(key, part):
    return shard_layout(key)[1]


def shard_levels(stream_key, dims, split, least, largest):
    level = 1.0
    for axis_at, shards_of in split:
        steps = jax.random.uniform(jax.random.fold_in(jax.random.fold_in(stream_key, 6), axis_at), (shards_of,), jnp.float32, least / len(split), largest / len(split))
        level = level * jnp.repeat(jnp.exp(steps), dims[axis_at] // shards_of).reshape((-1,) + (1,) * (len(dims) - 1 - axis_at))
    return level


def gaussian(stream_key, dims, width, limit, split=(), kind=jnp.bfloat16):
    gain = shard_levels(stream_key, dims, split, -0.22, 0.18) if split else 1.0
    array = jax.random.normal(stream_key, dims, jnp.float32) * width * gain
    return jnp.minimum(jnp.maximum(array, -limit), limit).astype(kind)


def setup_inputs(seed: int = 0) -> dict:
    key_of = jax.random.split(jax.random.key(seed), 11)
    return {
        "q_feat": gaussian(key_of[0], (SEQLEN, D), 1.0, 6.0, ((0, 32),)),
        "k_feat": gaussian(key_of[1], (SEQLEN, D), 1.0, 6.0, ((0, 32),)),
        "v_feat": gaussian(key_of[2], (SEQLEN, D), 1.0, 6.0, ((0, 32),)),
        "short_taps": gaussian(key_of[3], (3, SHORT, D), 0.6, 3.5, (), jnp.float32),
        "decay_rate": draw_decay_rate(jax.random.fold_in(key_of[10], 71), 0),
        "residue": draw_residue(jax.random.fold_in(key_of[10], 71), 0),
        "skip_gain": gaussian(key_of[6], (D,), 1.0, 6.0, (), jnp.float32),
        "out_weight": gaussian(key_of[7], (D, D), D ** -0.5, 0.09375, ((0, 32),)),
        "doc_starts": draw_doc_starts(jax.random.fold_in(key_of[10], 71), 0),
        "reset_flags": draw_reset_flags(jax.random.fold_in(key_of[10], 71), 0),
    }


def short_filter(features, rim_rows, tap_weights, keep_mask):
    token_rows = features.shape[0]
    tap_count = tap_weights.shape[0]
    joined = jnp.concatenate([rim_rows, features], axis=0)
    summed = tap_weights[0] * features.astype(jnp.float32)
    valid_mask = jnp.ones((token_rows,), jnp.float32)
    for offset in range(1, tap_count):
        valid_mask = valid_mask * jnp.concatenate([jnp.ones((offset - 1,), jnp.float32), keep_mask[:token_rows - offset + 1]])
        lagged = joined[tap_count - 1 - offset:tap_count - 1 - offset + token_rows].astype(jnp.float32)
        summed = summed + tap_weights[offset] * valid_mask[:, None] * lagged
    return summed.astype(jnp.bfloat16)


def document_marks(doc_starts, reset_flags):
    shard_base = (jnp.arange(SHARDS, dtype=jnp.int32) * TOK)[:, None]
    used_slot = doc_starts < TOK
    spots = jnp.where(used_slot, shard_base + doc_starts, SEQLEN).reshape(-1).astype(jnp.int32)
    flagged = ((reset_flags == 1) & used_slot).astype(jnp.float32).reshape(-1)
    starts_at = jnp.zeros((SEQLEN + 1,), jnp.float32).at[spots].max(jnp.ones_like(flagged))[:SEQLEN]
    resets = jnp.zeros((SEQLEN + 1,), jnp.float32).at[spots].max(flagged)[:SEQLEN]
    return starts_at, resets


def modal_filter(gated, resets, decay_rate, residue):
    highest = lax.Precision.HIGHEST
    decay_factor = jnp.exp(-decay_rate)
    steps_axis = jnp.arange(1, BLOCK + 1, dtype=jnp.float32)
    weighted = jnp.exp(-steps_axis[:, None, None] * decay_rate[None]) * residue[None]
    block_pow = jnp.exp(-BLOCK * decay_rate)
    gated_blocks = gated.reshape(SEQLEN // BLOCK, BLOCK, D)
    reset_blocks = resets.reshape(SEQLEN // BLOCK, BLOCK)

    def row_step(carried_state, row_item):
        gated_row, reset_row = row_item
        carried_state = decay_factor * carried_state * (1.0 - reset_row) + gated_row[None, :]
        return carried_state, jnp.sum(residue * carried_state, axis=0)

    def block_step(carried_state, block_item):
        gated_block, reset_block = block_item
        local_end, local_out = lax.scan(row_step, jnp.zeros((MODES, D), jnp.float32), (gated_block, reset_block))
        alive_mask = jnp.cumprod(1.0 - reset_block)
        carried = jnp.einsum("bnc,nc->bc", weighted, carried_state, precision=highest) * alive_mask[:, None]
        next_state = local_end + block_pow * carried_state * alive_mask[-1]
        return next_state, local_out + carried

    _, outputs = lax.scan(block_step, jnp.zeros((MODES, D), jnp.float32), (gated_blocks, reset_blocks))
    return outputs.reshape(SEQLEN, D)


def reference(q_feat, k_feat, v_feat, short_taps, decay_rate, residue, skip_gain, out_weight, doc_starts, reset_flags):
    starts_at, resets = document_marks(doc_starts, reset_flags)
    keep_mask = 1.0 - starts_at
    empty_rim = jnp.zeros((SHORT - 1, D), jnp.bfloat16)
    q_short = short_filter(q_feat, empty_rim, short_taps[0], keep_mask)
    k_short = short_filter(k_feat, empty_rim, short_taps[1], keep_mask)
    v_short = short_filter(v_feat, empty_rim, short_taps[2], keep_mask)
    gated = k_short.astype(jnp.float32) * v_short.astype(jnp.float32)
    filtered = modal_filter(gated, resets, decay_rate, residue)
    mixed = (q_short.astype(jnp.float32) * (filtered + skip_gain[None, :] * gated)).astype(jnp.bfloat16)

    def project_rows(row_block):
        summed = jnp.zeros((TOK, D), jnp.float32)
        for group_index in range(N_CH):
            first = group_index * GROUP
            group_term = jnp.dot(row_block[:, first:first + GROUP], out_weight[:, first:first + GROUP].T, preferred_element_type=jnp.float32)
            rounded = lax.optimization_barrier(group_term.astype(jnp.bfloat16))
            summed = summed + rounded.astype(jnp.float32)
        return summed.astype(jnp.bfloat16)

    projected = lax.map(project_rows, mixed.reshape(SHARDS, TOK, D))
    return projected.reshape(SEQLEN, D)
```

```python
import functools

import jax
import jax.numpy as jnp
from jax import lax
from jax.experimental import pallas as pl
from jax.experimental.pallas import tpu as pltpu
from jax.sharding import PartitionSpec as P

LANES = 128
GROUPS = 8
TILE = LANES * GROUPS
ROWS = 16
UNROLL = 8


def cut_of(starts, flags, tokens):
    cut = jnp.int32(tokens)
    for slot in range(starts.shape[1]):
        cut = jnp.where(flags[0, slot] == 1, jnp.minimum(cut, starts[0, slot]), cut)
    return cut


def local_kernel(starts, flags, q_ref, k_ref, v_ref, rim_ref, taps_ref, rate_ref, res_ref,
                 skip_ref, qs_ref, z_ref, state_ref, fac_ref):
    tokens = q_ref.shape[0]
    modes = rate_ref.shape[0]
    slots = starts.shape[1]
    cut = cut_of(starts, flags, tokens)

    def short_rows(step, carry):
        row = pl.multiple_of(step * ROWS, ROWS)
        back = pl.multiple_of(jnp.maximum(row - ROWS, 0), ROWS)
        at = lax.broadcasted_iota(jnp.int32, (ROWS, LANES), 0) + row
        hit = jnp.zeros((ROWS, LANES), jnp.bool_)
        hit_before = jnp.zeros((ROWS, LANES), jnp.bool_)
        for slot in range(slots):
            hit = hit | (at == starts[0, slot])
            hit_before = hit_before | (at - 1 == starts[0, slot])
        mask1 = jnp.where(hit, 0.0, 1.0)
        mask2 = jnp.where(hit | hit_before, 0.0, 1.0)
        first = step == 0
        for group in range(GROUPS):
            cols = slice(group * LANES, (group + 1) * LANES)

            def short(ref, index):
                x = ref[pl.ds(row, ROWS), cols].astype(jnp.float32)
                before = ref[pl.ds(back, ROWS), cols].astype(jnp.float32)
                rim = rim_ref[index, :, cols].astype(jnp.float32)
                before = jnp.where(first, rim, before)
                both = jnp.concatenate([before, x], axis=0)
                lag1 = pltpu.roll(both, 1, 0)[ROWS:]
                lag2 = pltpu.roll(both, 2, 0)[ROWS:]
                base = 3 * index
                summed = taps_ref[base : base + 1, cols] * x
                summed = summed + taps_ref[base + 1 : base + 2, cols] * mask1 * lag1
                summed = summed + taps_ref[base + 2 : base + 3, cols] * mask2 * lag2
                return summed.astype(jnp.bfloat16)

            qs_ref[pl.ds(row, ROWS), cols] = short(q_ref, 0)
            gated = short(k_ref, 1).astype(jnp.float32) * short(v_ref, 2).astype(jnp.float32)
            z_ref[pl.ds(row * GROUPS + group, ROWS, stride=GROUPS), :] = gated
        return carry

    lax.fori_loop(0, tokens // ROWS, short_rows, 0)

    fac_ref[...] = jnp.exp(-rate_ref[...])
    skip = skip_ref[...]

    def advance(step, states):
        states = list(states)
        for inner in range(UNROLL):
            time = step * UNROLL + inner
            spot = pl.ds(pl.multiple_of(time * GROUPS, GROUPS), GROUPS)
            keep = jnp.where(time == cut, 0.0, 1.0)
            x = z_ref[spot, :]
            sums = [skip * x, None]
            for n in range(modes):
                states[n] = (fac_ref[n] * keep) * states[n] + x
                term = res_ref[n] * states[n]
                sums[n % 2] = term if sums[n % 2] is None else sums[n % 2] + term
            z_ref[spot, :] = sums[0] + sums[1]
        return tuple(states)

    zero = jnp.zeros((GROUPS, LANES), jnp.float32)
    states = lax.fori_loop(0, tokens // UNROLL, advance, (zero,) * modes)
    for n in range(modes):
        state_ref[n] = states[n]
    through = jnp.where(cut < tokens, 0.0, 1.0)
    for n in range(modes, state_ref.shape[0]):
        state_ref[n] = zero + through


def scan_kernel(tokens, pieces_ref, rate_ref, out_ref):
    modes = rate_ref.shape[0]
    factor = jnp.exp(-float(tokens) * rate_ref[...])

    def hop(j, running):
        out_ref[j] = running
        piece = pieces_ref[j]
        return factor * piece[modes : modes + 1] * running + piece[:modes]

    lax.fori_loop(0, pieces_ref.shape[0], hop, jnp.zeros(rate_ref.shape, jnp.float32))


def finish_kernel(starts, flags, qs_ref, z_ref, enter_ref, rate_ref, res_ref, out_ref, fac_ref,
                  y_ref):
    tokens = qs_ref.shape[0]
    modes = rate_ref.shape[0]
    cut = cut_of(starts, flags, tokens)
    fac_ref[...] = jnp.exp(-rate_ref[...])

    def advance(step, weights):
        weights = list(weights)
        for inner in range(UNROLL):
            time = step * UNROLL + inner
            spot = pl.ds(pl.multiple_of(time * GROUPS, GROUPS), GROUPS)
            alive = jnp.where(time < cut, 1.0, 0.0)
            sums = [None, None]
            for n in range(modes):
                sums[n % 2] = weights[n] if sums[n % 2] is None else sums[n % 2] + weights[n]
                weights[n] = weights[n] * fac_ref[n]
            y_ref[spot, :] = z_ref[spot, :] + alive * (sums[0] + sums[1])
        return tuple(weights)

    begin = tuple(res_ref[n] * (fac_ref[n] * enter_ref[n]) for n in range(modes))
    lax.fori_loop(0, tokens // UNROLL, advance, begin)

    def mix_rows(step, carry):
        row = pl.multiple_of(step * ROWS, ROWS)
        for group in range(GROUPS):
            cols = slice(group * LANES, (group + 1) * LANES)
            y = y_ref[pl.ds(row * GROUPS + group, ROWS, stride=GROUPS), :]
            q = qs_ref[pl.ds(row, ROWS), cols].astype(jnp.float32)
            out_ref[pl.ds(row, ROWS), cols] = (q * y).astype(jnp.bfloat16)
        return carry

    lax.fori_loop(0, tokens // ROWS, mix_rows, 0)


PLANE = 8
RB = 32
PARTS = ((0, 64), (64, 48), (112, 16))


def fused_kernel(zs, starts, flags, q_hbm, k_hbm, v_hbm, w_hbm, taps_ref, rate_ref, res_ref,
                 skip_ref, out_hbm, wbuf, xin, tails, rim_out, rim_in, rimx, z_ref, acts, obuf,
                 acc_ref, fac_t, rate_t, res_t, csnd, crcv, tfin, pre, ent, load_sem, tail_sem,
                 rim_sem, wsend, wrecv, own_sem, chain_send_sem, chain_recv_sem, act_sem,
                 out_send_sem, out_recv_sem, out_sem):
    _, tokens, channels = xin.shape
    modes = rate_ref.shape[0]
    slots = starts.shape[1]
    feats = w_hbm.shape[0]
    tiles = channels // TILE
    lane_groups = channels // LANES
    blocks = 2 * zs
    n = PLANE * zs
    f32 = jnp.float32

    me = lax.axis_index("seq")
    core = lax.rem(me, 2)
    x = lax.rem(me // 2, 2)
    y = lax.rem(me // 4, 2)
    z = me // PLANE
    sib = me + 1 - 2 * core
    x_peer = me + 2 - 4 * x
    y_peer = me + 4 - 8 * y
    up, down = me + PLANE, me - PLANE
    has_up, has_down = z < zs - 1, z > 0

    order = [sorted(range(zs), key=lambda s, at=at: (abs(s - at), s)) for at in range(zs)]

    def source(rank):
        at = jnp.int32(order[0][rank])
        for level in range(1, zs):
            at = jnp.where(z == level, order[level][rank], at)
        return at

    def remote(src, dst, send, recv, dev):
        return pltpu.make_async_remote_copy(
            src_ref=src, dst_ref=dst, send_sem=send, recv_sem=recv,
            device_id={"seq": dev}, device_id_type=pl.DeviceIdType.MESH,
        )

    def piece(block, side, part):
        first, rows = PARTS[part]
        row = pl.multiple_of(side * feats + first, 16)
        return wbuf.at[block, pl.ds(row, rows), :]

    def weight_copy(block, part, way, own):
        first, rows = PARTS[part]
        dst = piece(block, core, part)
        src = w_hbm.at[pl.ds(first, rows), :] if own else dst
        return remote(src, dst, wsend.at[block, part, way],
                      wrecv.at[1 if way == 3 else 0, block, part],
                      (up, down, y_peer, sib)[way])

    def wait_weight(block, part):
        first, rows = PARTS[part]
        dst = piece(block, core, part)
        remote(dst, dst, wsend.at[block, part, 0], wrecv.at[0, block, part], sib).wait_recv()

    def wait_sibling(block):
        for part in range(len(PARTS)):
            dst = piece(block, 1 - core, part)
            remote(dst, dst, wsend.at[block, part, 3], wrecv.at[1, block, part], sib).wait_recv()

    def forward(block, part, ways, own, done):
        for way, cond in ways:
            copy = weight_copy(block, part, way, own)
            act = copy.wait_send if done else copy.start
            if cond is None:
                act()
            else:
                pl.when(cond)(act)

    def on_way(src_z):
        return ((0, jnp.logical_and(src_z < z, has_up)), (1, jnp.logical_and(src_z > z, has_down)))

    both = ((0, has_up), (1, has_down))
    here = z * 2 + y
    there = z * 2 + 1 - y
    last = len(PARTS) - 1

    def send_own(done):
        for part in range(last):
            forward(here, part, both + ((2, None), (3, None)), True, done)
        forward(here, last, ((2, None),) + both + ((3, None),), True, done)

    def poll_line(rank, part, done=False):
        src = source(rank)
        block = src * 2 + y
        if not done:
            wait_weight(block, part)
        forward(block, part, on_way(src) + ((2, None), (3, None)), False, done)

    def poll_across(rank, part, done=False):
        block = source(rank) * 2 + 1 - y
        if not done:
            wait_weight(block, part)
        forward(block, part, ((3, None),), False, done)

    def poll_last_across(done=False):
        if not done:
            wait_weight(there, last)
        forward(there, last, both + ((3, None),), False, done)

    def poll_last_line(rank, side, done=False):
        src = source(rank)
        block = src * 2 + (y if side == 0 else 1 - y)
        if not done:
            wait_weight(block, last)
        forward(block, last, on_way(src) + ((3, None),), False, done)

    barrier = pltpu.get_barrier_semaphore()

    def greet(dev):
        pl.semaphore_signal(barrier, inc=1, device_id={"seq": dev},
                            device_id_type=pl.DeviceIdType.MESH)

    for dev in (sib, x_peer, y_peer):
        greet(dev)
    pl.when(has_up)(lambda: greet(up))
    pl.when(has_down)(lambda: greet(down))
    pl.when(me < n - 1)(lambda: greet(me + 1))
    pl.when(me > 0)(lambda: greet(me - 1))

    feeds = (q_hbm, k_hbm, v_hbm)
    tail_copies = [
        pltpu.make_async_copy(feeds[i].at[pl.ds(tokens - 16, 16), :], tails.at[i], tail_sem.at[i])
        for i in range(3)
    ]
    for copy in tail_copies:
        copy.start()

    def load(index, tile):
        cols = pl.ds(tile * TILE, TILE)
        return pltpu.make_async_copy(feeds[index].at[:, cols], xin.at[index, :, cols],
                                     load_sem.at[index, tile])

    for tile in range(tiles):
        load(1, tile).start()
        load(2, tile).start()
    for tile in range(tiles):
        load(0, tile).start()
    own_copy = pltpu.make_async_copy(
        w_hbm, wbuf.at[here, pl.ds(pl.multiple_of(core * feats, 16), feats), :], own_sem)
    own_copy.start()

    cut = cut_of(starts, flags, tokens)
    through_me = jnp.where(cut < tokens, 0.0, 1.0)
    live = jnp.where(cut < tokens, cut, 0)
    final_start = jnp.float32(1.0)
    for slot in range(slots):
        final_start = jnp.where(starts[0, slot] == tokens - 1, 0.0, final_start)

    pl.semaphore_wait(barrier, 3 + jnp.where(has_up, 1, 0) + jnp.where(has_down, 1, 0)
                      + jnp.where(me < n - 1, 1, 0) + jnp.where(me > 0, 1, 0))
    send_own(False)

    for copy in tail_copies:
        copy.wait()
    for index in range(3):
        two = tails[index, 8:16, :].astype(f32)
        rim_out[2 * index : 2 * index + 1, :] = two[6:7] * final_start
        rim_out[2 * index + 1 : 2 * index + 2, :] = two[7:8]
    rim_out[6:8, :] = jnp.zeros((2, channels), f32)
    rim_copy = remote(rim_out, rim_in, rim_sem.at[0], rim_sem.at[1], me + 1)
    pl.when(me < n - 1)(rim_copy.start)

    for half in range(modes // 8):
        for group in range(lane_groups):
            cols = slice(group * LANES, (group + 1) * LANES)
            spot = pl.ds(half * 8 * lane_groups + group, 8, stride=lane_groups)
            rate_t[spot, :] = rate_ref[half * 8 : half * 8 + 8, cols]
            res_t[spot, :] = res_ref[half * 8 : half * 8 + 8, cols]

    def fill_factors(step, carry):
        rows = pl.ds(pl.multiple_of(step * 32, 32), 32)
        fac_t[rows, :] = jnp.exp(-rate_t[rows, :])
        return carry

    lax.fori_loop(0, modes * lane_groups // 32, fill_factors, 0)

    def table(ref, mode, tile):
        first = mode * lane_groups + tile * GROUPS
        return ref[first : first + GROUPS, :]

    @pl.when(z == 0)
    def _():
        for tile in range(tiles):
            crcv[tile, 3] = jnp.zeros(crcv.shape[2:], f32)

    @pl.when(me == 0)
    def _():
        rim_in[...] = jnp.zeros(rim_in.shape, f32)

    def masks(row):
        at = lax.broadcasted_iota(jnp.int32, (RB, LANES), 0) + row
        hit = jnp.zeros((RB, LANES), jnp.bool_)
        hit_before = jnp.zeros((RB, LANES), jnp.bool_)
        for slot in range(slots):
            hit = hit | (at == starts[0, slot])
            hit_before = hit_before | (at - 1 == starts[0, slot])
        return jnp.where(hit, 0.0, 1.0), jnp.where(hit | hit_before, 0.0, 1.0)

    def short(index, row, cols, mask1, mask2, first):
        now = xin[index, pl.ds(row, RB), cols].astype(f32)
        if first:
            before = rimx[index, :, cols]
        else:
            before = xin[index, pl.ds(pl.multiple_of(row - 16, 16), 16), cols].astype(f32)[8:]
        joined = jnp.concatenate([before, now], axis=0)
        lag1 = pltpu.roll(joined, 1, 0)[8:]
        lag2 = pltpu.roll(joined, 2, 0)[8:]
        summed = taps_ref[index, 0:1, cols] * now
        summed = summed + taps_ref[index, 1:2, cols] * mask1 * lag1
        summed = summed + taps_ref[index, 2:3, cols] * mask2 * lag2
        return summed.astype(jnp.bfloat16)

    def gate_rows(tile, row, first):
        mask1, mask2 = masks(row)
        for group in range(GROUPS):
            cols = slice(tile * TILE + group * LANES, tile * TILE + (group + 1) * LANES)
            key = short(1, row, cols, mask1, mask2, first).astype(f32)
            value = short(2, row, cols, mask1, mask2, first).astype(f32)
            z_ref[tile, pl.ds(row * GROUPS + group, RB, stride=GROUPS), :] = key * value

    def gate(tile):
        load(1, tile).wait()
        load(2, tile).wait()

        def rows(step, carry):
            gate_rows(tile, pl.multiple_of(step * RB, RB), False)
            return carry

        lax.fori_loop(1, tokens // RB, rows, 0)

    def end_states(tile):
        zero = jnp.zeros((GROUPS, LANES), f32)

        def advance(step, states):
            states = list(states)
            for inner in range(UNROLL):
                time = step * UNROLL + inner
                spot = pl.ds(pl.multiple_of(time * GROUPS, GROUPS), GROUPS)
                item = z_ref[tile, spot, :] * jnp.where(time >= live, 1.0, 0.0)
                for mode in range(modes):
                    states[mode] = table(fac_t, mode, tile) * states[mode] + item
            return tuple(states)

        states = lax.fori_loop(0, tokens // UNROLL, advance, (zero,) * modes)
        for mode in range(modes):
            csnd[tile, 0, mode] = states[mode]
            pre[tile, mode] = zero
        csnd[tile, 0, modes] = zero + through_me
        pre[tile, modes] = zero + 1.0

    peers = (sib, x_peer, y_peer, up)
    bits = (core, x, y)

    def chain_copy(tile, step):
        return remote(csnd.at[tile, step], crcv.at[tile, step], chain_send_sem.at[tile, step],
                      chain_recv_sem.at[tile, step], peers[step])

    def chain_step(tile, step):
        chain_copy(tile, step).wait_recv()
        upper = bits[step] == 1
        span = float(tokens * 2**step)
        before = (lax.rem(me, 2**step) * tokens).astype(f32)
        through_mine = csnd[tile, step, modes]
        through_other = crcv[tile, step, modes]
        through_pre = pre[tile, modes]
        through_late = jnp.where(upper, through_mine, through_other)
        for mode in range(modes):
            rate = table(rate_t, mode, tile)
            mine = csnd[tile, step, mode]
            other = crcv[tile, step, mode]
            early = jnp.where(upper, other, mine)
            late = jnp.where(upper, mine, other)
            total = late + through_late * jnp.exp(-span * rate) * early
            if step < 2:
                csnd[tile, step + 1, mode] = total
            else:
                tfin[tile, mode] = total
            old = pre[tile, mode]
            pre[tile, mode] = jnp.where(
                upper, old + through_pre * jnp.exp(-before * rate) * other, old)
        through = through_mine * through_other
        if step < 2:
            csnd[tile, step + 1, modes] = through
        else:
            tfin[tile, modes] = through
        pre[tile, modes] = jnp.where(upper, through_pre * through_other, through_pre)
        if step < 2:
            chain_copy(tile, step + 1).start()

    def chain_line(tile):
        pl.when(has_down)(chain_copy(tile, 3).wait_recv)
        before = (lax.rem(me, PLANE) * tokens).astype(f32)
        through_all = tfin[tile, modes]
        through_pre = pre[tile, modes]
        for mode in range(modes):
            rate = table(rate_t, mode, tile)
            entering = crcv[tile, 3, mode]
            csnd[tile, 3, mode] = (
                tfin[tile, mode] + through_all * jnp.exp(-float(tokens * PLANE) * rate) * entering)
        csnd[tile, 3, modes] = through_all
        pl.when(has_up)(chain_copy(tile, 3).start)
        for mode in range(modes):
            rate = table(rate_t, mode, tile)
            entering = crcv[tile, 3, mode]
            ent[tile, mode] = pre[tile, mode] + through_pre * jnp.exp(-before * rate) * entering

    def act_copy(tile):
        cols = pl.ds(tile * TILE, TILE)
        return remote(acts.at[pl.ds(0, tokens), cols], acts.at[pl.ds(tokens, tokens), cols],
                      act_sem.at[0, tile], act_sem.at[1, tile], x_peer)

    def finish(tile):
        skip = skip_ref[tile * GROUPS : (tile + 1) * GROUPS, :]

        def advance(step, states):
            states = list(states)
            for inner in range(UNROLL):
                time = step * UNROLL + inner
                spot = pl.ds(pl.multiple_of(time * GROUPS, GROUPS), GROUPS)
                keep = jnp.where(time == cut, 0.0, 1.0)
                item = z_ref[tile, spot, :]
                sums = [skip * item, None]
                for mode in range(modes):
                    states[mode] = (table(fac_t, mode, tile) * keep) * states[mode] + item
                    term = table(res_t, mode, tile) * states[mode]
                    sums[mode % 2] = term if sums[mode % 2] is None else sums[mode % 2] + term
                z_ref[tile, spot, :] = sums[0] + sums[1]
            return tuple(states)

        begin = tuple(ent[tile, mode] for mode in range(modes))
        lax.fori_loop(0, tokens // UNROLL, advance, begin)
        load(0, tile).wait()

        def mix_rows(row, first):
            mask1, mask2 = masks(row)
            for group in range(GROUPS):
                cols = slice(tile * TILE + group * LANES, tile * TILE + (group + 1) * LANES)
                query = short(0, row, cols, mask1, mask2, first).astype(f32)
                mixed = z_ref[tile, pl.ds(row * GROUPS + group, RB, stride=GROUPS), :]
                acts[pl.ds(row, RB), cols] = (query * mixed).astype(jnp.bfloat16)

        def rows(step, carry):
            mix_rows(pl.multiple_of(step * RB, RB), False)
            return carry

        mix_rows(0, True)
        lax.fori_loop(1, tokens // RB, rows, 0)
        act_copy(tile).start()

    def columns(block, plane):
        return pl.ds(pl.multiple_of((block * 2 + plane) * 2 * feats, LANES), 2 * feats)

    def out_copy(block):
        return remote(obuf.at[block, pl.ds(tokens, tokens), :], out_hbm.at[:, columns(block, x)],
                      out_send_sem.at[block], out_recv_sem.at[block], x_peer)

    def own_out(block):
        return pltpu.make_async_copy(obuf.at[block, pl.ds(0, tokens), :],
                                     out_hbm.at[:, columns(block, x)], out_sem.at[block])

    def project(block):
        wait_sibling(block)

        def depth(step, carry):
            cols = pl.ds(pl.multiple_of(step * TILE, TILE), TILE)
            term = lax.dot_general(acts[:, cols], wbuf[block, :, cols], (((1,), (1,)), ((), ())),
                                   preferred_element_type=f32)

            acc_ref[...] = jnp.where(step == 0, 0.0, acc_ref[...]) + term
            return carry

        acc_ref[...] = jnp.zeros(acc_ref.shape, f32)
        lax.fori_loop(0, tiles, depth, 0)
        obuf[block] = acc_ref[...].astype(jnp.bfloat16)
        out_copy(block).start()
        own_out(block).start()

    gate(0)
    gate(1)
    pl.when(me > 0)(rim_copy.wait_recv)
    for index in range(3):
        rimx[index] = jnp.zeros((8, channels), f32)
        rimx[index, 6:8, :] = rim_in[2 * index : 2 * index + 2, :]
    gate_rows(0, 0, True)
    gate_rows(1, 0, True)
    end_states(0)
    chain_copy(0, 0).start()
    end_states(1)
    chain_step(0, 0)
    chain_copy(1, 0).start()
    gate(2)
    gate_rows(2, 0, True)
    chain_step(0, 1)
    chain_step(1, 0)
    end_states(2)
    chain_copy(2, 0).start()
    chain_step(0, 2)
    chain_step(1, 1)
    gate(3)
    gate_rows(3, 0, True)
    chain_line(0)
    chain_step(1, 2)
    chain_step(2, 0)
    end_states(3)
    chain_copy(3, 0).start()
    chain_line(1)
    chain_step(2, 1)
    finish(0)
    poll_line(1, 0)
    poll_across(0, 0)
    chain_step(2, 2)
    chain_step(3, 0)
    chain_line(2)
    chain_step(3, 1)
    finish(1)
    poll_line(1, 1)
    poll_across(0, 1)
    poll_last_across()
    chain_step(3, 2)
    chain_line(3)
    finish(2)
    poll_last_line(1, 0)
    poll_last_line(1, 1)
    finish(3)
    for rank in range(2, zs):
        for part in range(last):
            poll_line(rank, part)
            poll_across(rank - 1, part)
        poll_last_line(rank, 0)
        poll_last_line(rank, 1)
    for tile in range(tiles):
        act_copy(tile).wait_recv()
    own_copy.wait()
    for rank in range(zs - 1):
        project(source(rank) * 2 + y)
        project(source(rank) * 2 + 1 - y)
    project(source(zs - 1) * 2 + y)
    for part in range(last):
        poll_across(zs - 1, part)
    project(source(zs - 1) * 2 + 1 - y)

    send_own(True)
    for rank in range(1, zs):
        for part in range(last):
            poll_line(rank, part, True)
        poll_last_line(rank, 0, True)
        poll_last_line(rank, 1, True)
    for rank in range(zs):
        for part in range(last):
            poll_across(rank, part, True)
    poll_last_across(True)
    pl.when(me < n - 1)(rim_copy.wait_send)
    for tile in range(tiles):
        for step in range(3):
            chain_copy(tile, step).wait_send()
        pl.when(has_up)(chain_copy(tile, 3).wait_send)
        act_copy(tile).wait_send()
    for block in range(blocks):
        own_out(block).wait()
        out_copy(block).wait()


def fused(q_feat, k_feat, v_feat, short_taps, decay_rate, residue, skip_gain, out_weight,
          doc_starts, reset_flags):
    tokens, channels = q_feat.shape
    modes = decay_rate.shape[0]
    n = lax.axis_size("seq")
    zs = n // PLANE
    tiles = channels // TILE
    feats = out_weight.shape[0]
    f32, bf16 = jnp.float32, jnp.bfloat16
    vmem = pl.BlockSpec(memory_space=pltpu.VMEM)
    smem = pl.BlockSpec(memory_space=pltpu.SMEM)
    hbm = pl.BlockSpec(memory_space=pl.ANY)
    dma = pltpu.SemaphoreType.DMA
    table = pltpu.VMEM((modes * channels // LANES, LANES), f32)
    vec = (GROUPS, LANES)
    return pl.pallas_call(
        functools.partial(fused_kernel, zs),
        in_specs=[smem, smem, hbm, hbm, hbm, hbm, vmem, vmem, vmem, vmem],
        out_specs=hbm,
        out_shape=jax.ShapeDtypeStruct((tokens, n * feats), bf16),
        scratch_shapes=[
            pltpu.VMEM((2 * zs, 2 * feats, channels), bf16),
            pltpu.VMEM((3, tokens, channels), bf16),
            pltpu.VMEM((3, 16, channels), bf16),
            pltpu.VMEM((8, channels), f32),
            pltpu.VMEM((8, channels), f32),
            pltpu.VMEM((3, 8, channels), f32),
            pltpu.VMEM((tiles, tokens * GROUPS, LANES), f32),
            pltpu.VMEM((2 * tokens, channels), bf16),
            pltpu.VMEM((2 * zs, 2 * tokens, 2 * feats), bf16),
            pltpu.VMEM((2 * tokens, 2 * feats), f32),
            table, table, table,
            pltpu.VMEM((tiles, 4, modes + 1) + vec, f32),
            pltpu.VMEM((tiles, 4, modes + 1) + vec, f32),
            pltpu.VMEM((tiles, modes + 1) + vec, f32),
            pltpu.VMEM((tiles, modes + 1) + vec, f32),
            pltpu.VMEM((tiles, modes) + vec, f32),
            dma((3, tiles)), dma((3,)), dma((2,)),
            dma((2 * zs, len(PARTS), 4)), dma((2, 2 * zs, len(PARTS))), dma,
            dma((tiles, 4)), dma((tiles, 4)), dma((2, tiles)),
            dma((2 * zs,)), dma((2 * zs,)), dma((2 * zs,)),
        ],
        compiler_params=pltpu.CompilerParams(
            collective_id=0, has_side_effects=True, vmem_limit_bytes=58 * 2**20
        ),
        name="mixer",
    )(doc_starts, reset_flags, q_feat, k_feat, v_feat, out_weight, short_taps, decay_rate,
      residue, skip_gain.reshape(channels // LANES, LANES))


def local(q_feat, k_feat, v_feat, short_taps, decay_rate, residue, skip_gain, out_weight,
          doc_starts, reset_flags):
    tokens, channels = q_feat.shape
    modes = decay_rate.shape[0]
    kinds, taps = short_taps.shape[:2]
    n = lax.axis_size("seq")
    me = lax.axis_index("seq")
    tiles = channels // TILE
    heads = modes + 8

    weight = lax.all_gather(out_weight, "seq", axis=0, tiled=True)

    last_is_start = jnp.any(doc_starts[0] == tokens - 1)
    scale = jnp.stack([jnp.where(last_is_start, 0.0, 1.0), jnp.float32(1.0)]).astype(jnp.bfloat16)
    tails = jnp.stack([x[tokens - (taps - 1) :] for x in (q_feat, k_feat, v_feat)])
    tails = tails * scale[None, :, None]
    arrived = lax.ppermute(tails, "seq", [(i, i + 1) for i in range(n - 1)])
    rim = jnp.pad(arrived, ((0, 0), (ROWS - (taps - 1), 0), (0, 0)))

    rates = decay_rate.reshape(modes, channels // LANES, LANES)
    residues = residue.reshape(modes, channels // LANES, LANES)
    skips = skip_gain.reshape(channels // LANES, LANES)

    smem = pl.BlockSpec(memory_space=pltpu.SMEM)
    wide = pl.BlockSpec((tokens, TILE), lambda i: (0, i))
    deep = pl.BlockSpec((modes, GROUPS, LANES), lambda i: (0, i, 0))
    flat = pl.BlockSpec((None, tokens * GROUPS, LANES), lambda i: (i, 0, 0))
    f32 = jnp.float32
    qs, z, state = pl.pallas_call(
        local_kernel,
        grid=(tiles,),
        in_specs=[
            smem, smem, wide, wide, wide,
            pl.BlockSpec((kinds, ROWS, TILE), lambda i: (0, 0, i)),
            pl.BlockSpec((kinds * taps, TILE), lambda i: (0, i)),
            deep, deep,
            pl.BlockSpec((GROUPS, LANES), lambda i: (i, 0)),
        ],
        out_specs=[wide, flat, pl.BlockSpec((heads, GROUPS, LANES), lambda i: (0, i, 0))],
        out_shape=[
            jax.ShapeDtypeStruct((tokens, channels), jnp.bfloat16),
            jax.ShapeDtypeStruct((tiles, tokens * GROUPS, LANES), f32),
            jax.ShapeDtypeStruct((heads, channels // LANES, LANES), f32),
        ],
        scratch_shapes=[pltpu.VMEM((modes, GROUPS, LANES), f32)],
        cost_estimate=pl.CostEstimate(
            flops=tokens * channels * 80, bytes_accessed=tokens * channels * 12, transcendentals=0
        ),
        name="local_filter",
    )(doc_starts, reset_flags, q_feat, k_feat, v_feat, rim,
      short_taps.reshape(kinds * taps, channels), rates, residues, skips)

    part = channels // n
    sent = state.reshape(heads, n, part).transpose(1, 0, 2)
    pieces = lax.all_to_all(sent, "seq", 0, 0)
    my_rates = lax.dynamic_slice_in_dim(decay_rate, me * part, part, 1)
    chained = pl.pallas_call(
        functools.partial(scan_kernel, tokens),
        out_shape=jax.ShapeDtypeStruct((n, modes, part), f32),
        name="chain_states",
    )(pieces, my_rates)
    entering = lax.all_to_all(chained, "seq", 0, 0)
    entering = entering.transpose(1, 0, 2).reshape(modes, channels // LANES, LANES)

    mixed = pl.pallas_call(
        finish_kernel,
        grid=(tiles,),
        in_specs=[smem, smem, wide, flat, deep, deep, deep],
        out_specs=wide,
        out_shape=jax.ShapeDtypeStruct((tokens, channels), jnp.bfloat16),
        scratch_shapes=[
            pltpu.VMEM((modes, GROUPS, LANES), f32),
            pltpu.VMEM((tokens * GROUPS, LANES), f32),
        ],
        cost_estimate=pl.CostEstimate(
            flops=tokens * channels * 40, bytes_accessed=tokens * channels * 8, transcendentals=0
        ),
        name="finish_filter",
    )(doc_starts, reset_flags, qs, z, entering, rates, residues)

    projected = lax.dot_general(
        mixed, weight, (((1,), (1,)), ((), ())), preferred_element_type=f32
    ).astype(jnp.bfloat16)
    return lax.psum_scatter(projected, "ch", scatter_dimension=1, tiled=True)


def solution(mesh):
    placed = (
        P("seq", "ch"), P("seq", "ch"), P("seq", "ch"), P(None, None, "ch"), P(None, "ch"),
        P(None, "ch"), P("ch"), P("seq", "ch"), P("seq", None), P("seq", None),
    )
    direct = mesh.shape["ch"] == 1 and mesh.shape["seq"] % (2 * PLANE) == 0
    return jax.shard_map(
        fused if direct else local, mesh=mesh, in_specs=placed, out_specs=P("seq", "ch"), check_vma=False
    )
```

```python
import functools

import jax
import jax.numpy as jnp
from jax import lax
from jax.experimental import pallas as pl
from jax.experimental.pallas import tpu as pltpu
from jax.sharding import PartitionSpec as P

LANES = 128
GROUPS = 8
TILE = LANES * GROUPS
ROWS = 16
UNROLL = 8


def cut_of(starts, flags, tokens):
    cut = jnp.int32(tokens)
    for slot in range(starts.shape[1]):
        cut = jnp.where(flags[0, slot] == 1, jnp.minimum(cut, starts[0, slot]), cut)
    return cut


def local_kernel(starts, flags, q_ref, k_ref, v_ref, rim_ref, taps_ref, rate_ref, res_ref,
                 skip_ref, qs_ref, z_ref, state_ref, fac_ref):
    tokens = q_ref.shape[0]
    modes = rate_ref.shape[0]
    slots = starts.shape[1]
    cut = cut_of(starts, flags, tokens)

    def short_rows(step, carry):
        row = pl.multiple_of(step * ROWS, ROWS)
        back = pl.multiple_of(jnp.maximum(row - ROWS, 0), ROWS)
        at = lax.broadcasted_iota(jnp.int32, (ROWS, LANES), 0) + row
        hit = jnp.zeros((ROWS, LANES), jnp.bool_)
        hit_before = jnp.zeros((ROWS, LANES), jnp.bool_)
        for slot in range(slots):
            hit = hit | (at == starts[0, slot])
            hit_before = hit_before | (at - 1 == starts[0, slot])
        mask1 = jnp.where(hit, 0.0, 1.0)
        mask2 = jnp.where(hit | hit_before, 0.0, 1.0)
        first = step == 0
        for group in range(GROUPS):
            cols = slice(group * LANES, (group + 1) * LANES)

            def short(ref, index):
                x = ref[pl.ds(row, ROWS), cols].astype(jnp.float32)
                before = ref[pl.ds(back, ROWS), cols].astype(jnp.float32)
                rim = rim_ref[index, :, cols].astype(jnp.float32)
                before = jnp.where(first, rim, before)
                both = jnp.concatenate([before, x], axis=0)
                lag1 = pltpu.roll(both, 1, 0)[ROWS:]
                lag2 = pltpu.roll(both, 2, 0)[ROWS:]
                base = 3 * index
                summed = taps_ref[base : base + 1, cols] * x
                summed = summed + taps_ref[base + 1 : base + 2, cols] * mask1 * lag1
                summed = summed + taps_ref[base + 2 : base + 3, cols] * mask2 * lag2
                return summed.astype(jnp.bfloat16)

            qs_ref[pl.ds(row, ROWS), cols] = short(q_ref, 0)
            gated = short(k_ref, 1).astype(jnp.float32) * short(v_ref, 2).astype(jnp.float32)
            z_ref[pl.ds(row * GROUPS + group, ROWS, stride=GROUPS), :] = gated
        return carry

    lax.fori_loop(0, tokens // ROWS, short_rows, 0)

    fac_ref[...] = jnp.exp(-rate_ref[...])
    skip = skip_ref[...]

    def advance(step, states):
        states = list(states)
        for inner in range(UNROLL):
            time = step * UNROLL + inner
            spot = pl.ds(pl.multiple_of(time * GROUPS, GROUPS), GROUPS)
            keep = jnp.where(time == cut, 0.0, 1.0)
            x = z_ref[spot, :]
            sums = [skip * x, None]
            for n in range(modes):
                states[n] = (fac_ref[n] * keep) * states[n] + x
                term = res_ref[n] * states[n]
                sums[n % 2] = term if sums[n % 2] is None else sums[n % 2] + term
            z_ref[spot, :] = sums[0] + sums[1]
        return tuple(states)

    zero = jnp.zeros((GROUPS, LANES), jnp.float32)
    states = lax.fori_loop(0, tokens // UNROLL, advance, (zero,) * modes)
    for n in range(modes):
        state_ref[n] = states[n]
    through = jnp.where(cut < tokens, 0.0, 1.0)
    for n in range(modes, state_ref.shape[0]):
        state_ref[n] = zero + through


def scan_kernel(tokens, pieces_ref, rate_ref, out_ref):
    modes = rate_ref.shape[0]
    factor = jnp.exp(-float(tokens) * rate_ref[...])

    def hop(j, running):
        out_ref[j] = running
        piece = pieces_ref[j]
        return factor * piece[modes : modes + 1] * running + piece[:modes]

    lax.fori_loop(0, pieces_ref.shape[0], hop, jnp.zeros(rate_ref.shape, jnp.float32))


def finish_kernel(starts, flags, qs_ref, z_ref, enter_ref, rate_ref, res_ref, out_ref, fac_ref,
                  y_ref):
    tokens = qs_ref.shape[0]
    modes = rate_ref.shape[0]
    cut = cut_of(starts, flags, tokens)
    fac_ref[...] = jnp.exp(-rate_ref[...])

    def advance(step, weights):
        weights = list(weights)
        for inner in range(UNROLL):
            time = step * UNROLL + inner
            spot = pl.ds(pl.multiple_of(time * GROUPS, GROUPS), GROUPS)
            alive = jnp.where(time < cut, 1.0, 0.0)
            sums = [None, None]
            for n in range(modes):
                sums[n % 2] = weights[n] if sums[n % 2] is None else sums[n % 2] + weights[n]
                weights[n] = weights[n] * fac_ref[n]
            y_ref[spot, :] = z_ref[spot, :] + alive * (sums[0] + sums[1])
        return tuple(weights)

    begin = tuple(res_ref[n] * (fac_ref[n] * enter_ref[n]) for n in range(modes))
    lax.fori_loop(0, tokens // UNROLL, advance, begin)

    def mix_rows(step, carry):
        row = pl.multiple_of(step * ROWS, ROWS)
        for group in range(GROUPS):
            cols = slice(group * LANES, (group + 1) * LANES)
            y = y_ref[pl.ds(row * GROUPS + group, ROWS, stride=GROUPS), :]
            q = qs_ref[pl.ds(row, ROWS), cols].astype(jnp.float32)
            out_ref[pl.ds(row, ROWS), cols] = (q * y).astype(jnp.bfloat16)
        return carry

    lax.fori_loop(0, tokens // ROWS, mix_rows, 0)


PLANE = 8
RB = 32
PARTS = ((0, 64), (64, 48), (112, 16))
PIECE = 16


def fused_kernel(zs, starts, flags, q_hbm, k_hbm, v_hbm, w_hbm, taps_ref, rate_ref, res_ref,
                 skip_ref, out_hbm, wbuf, xin, tails, rim_out, rim_in, rimx, z_ref, acts, obuf,
                 acc_ref, fac_t, rate_t, res_t, csnd, crcv, tot, pre, ent, load_sem, tail_sem,
                 rim_sem, wsend, wrecv, own_sem, chain_send_sem, chain_recv_sem, act_sem,
                 out_send_sem, out_recv_sem, out_sem):
    _, tokens, channels = xin.shape
    modes = rate_ref.shape[0]
    slots = starts.shape[1]
    feats = w_hbm.shape[0]
    tiles = channels // TILE
    lane_groups = channels // LANES
    blocks = 2 * zs
    n = PLANE * zs
    f32 = jnp.float32

    me = lax.axis_index("seq")
    core = lax.rem(me, 2)
    x = lax.rem(me // 2, 2)
    y = lax.rem(me // 4, 2)
    z = me // PLANE
    sib = me + 1 - 2 * core
    x_peer = me + 2 - 4 * x
    y_peer = me + 4 - 8 * y
    up, down = me + PLANE, me - PLANE
    has_up, has_down = z < zs - 1, z > 0

    order = [sorted(range(zs), key=lambda s, at=at: (abs(s - at), s)) for at in range(zs)]

    def source(rank):
        at = jnp.int32(order[0][rank])
        for level in range(1, zs):
            at = jnp.where(z == level, order[level][rank], at)
        return at

    def remote(src, dst, send, recv, dev):
        return pltpu.make_async_remote_copy(
            src_ref=src, dst_ref=dst, send_sem=send, recv_sem=recv,
            device_id={"seq": dev}, device_id_type=pl.DeviceIdType.MESH,
        )

    def piece(block, side, part):
        first, rows = PARTS[part]
        row = pl.multiple_of(side * feats + first, 16)
        return wbuf.at[block, pl.ds(row, rows), :]

    def weight_copy(block, part, way, own):
        first, rows = PARTS[part]
        dst = piece(block, core, part)
        src = w_hbm.at[pl.ds(first, rows), :] if own else dst
        return remote(src, dst, wsend.at[block, part, way],
                      wrecv.at[1 if way == 3 else 0, block, part],
                      (up, down, y_peer, sib)[way])

    def wait_weight(block, part):
        first, rows = PARTS[part]
        dst = piece(block, core, part)
        remote(dst, dst, wsend.at[block, part, 0], wrecv.at[0, block, part], sib).wait_recv()

    def wait_sibling(block):
        for part in range(len(PARTS)):
            dst = piece(block, 1 - core, part)
            remote(dst, dst, wsend.at[block, part, 3], wrecv.at[1, block, part], sib).wait_recv()

    def forward(block, part, ways, own, done):
        for way, cond in ways:
            copy = weight_copy(block, part, way, own)
            act = copy.wait_send if done else copy.start
            if cond is None:
                act()
            else:
                pl.when(cond)(act)

    both = ((0, has_up), (1, has_down))
    here = z * 2 + y
    there = z * 2 + 1 - y
    last = len(PARTS) - 1

    def issue(part, first, count, ways):
        for index in range(first, first + count):
            row = PARTS[part][0] + index * PIECE
            spot = pl.ds(pl.multiple_of(core * feats + row, 16), PIECE)
            for way, cond in ways:
                copy = remote(w_hbm.at[pl.ds(row, PIECE), :], wbuf.at[here, spot, :],
                              wsend.at[here, part, way], wrecv.at[0, here, part],
                              (up, down, y_peer)[way])
                if cond is None:
                    copy.start()
                else:
                    pl.when(cond)(copy.start)

    across = ((2, None),)

    def finish_own():
        for part in range(last + 1):
            forward(here, part, both + ((2, None), (3, None)), True, True)

    def each_side(distance, act):
        pl.when(z >= distance)(lambda: act(z - distance, ((0, has_up),)))
        pl.when(z + distance < zs)(lambda: act(z + distance, ((1, has_down),)))

    def poll_line(distance, part, done=False):
        def act(src, on_way):
            block = src * 2 + y
            if not done:
                wait_weight(block, part)
            forward(block, part, on_way + ((2, None), (3, None)), False, done)

        each_side(distance, act)

    def poll_across(distance, part, done=False):
        def act(src, on_way):
            block = src * 2 + 1 - y
            if not done:
                wait_weight(block, part)
            forward(block, part, ((3, None),), False, done)

        if distance:
            each_side(distance, act)
        else:
            act(z, ())

    def poll_last_across(done=False):
        if not done:
            wait_weight(there, last)
        forward(there, last, both + ((3, None),), False, done)

    def poll_last_line(distance, done=False):
        def act(src, on_way):
            for side in (y, 1 - y):
                block = src * 2 + side
                if not done:
                    wait_weight(block, last)
                forward(block, last, on_way + ((3, None),), False, done)

        each_side(distance, act)

    barrier = pltpu.get_barrier_semaphore()

    def greet(dev):
        pl.semaphore_signal(barrier, inc=1, device_id={"seq": dev},
                            device_id_type=pl.DeviceIdType.MESH)

    for dev in (sib, x_peer, y_peer):
        greet(dev)
    for gap in range(1, zs):
        pl.when(z + gap < zs)(lambda gap=gap: greet(me + gap * PLANE))
        pl.when(z >= gap)(lambda gap=gap: greet(me - gap * PLANE))
    pl.when(me < n - 1)(lambda: greet(me + 1))
    pl.when(me > 0)(lambda: greet(me - 1))

    feeds = (q_hbm, k_hbm, v_hbm)
    tail_copies = [
        pltpu.make_async_copy(feeds[i].at[pl.ds(tokens - 16, 16), :], tails.at[i], tail_sem.at[i])
        for i in range(3)
    ]
    for copy in tail_copies:
        copy.start()

    def load(index, tile):
        cols = pl.ds(tile * TILE, TILE)
        return pltpu.make_async_copy(feeds[index].at[:, cols], xin.at[index, :, cols],
                                     load_sem.at[index, tile])

    for index in (1, 2, 0):
        for tile in range(tiles):
            load(index, tile).start()
    own_copy = pltpu.make_async_copy(
        w_hbm, wbuf.at[here, pl.ds(pl.multiple_of(core * feats, 16), feats), :], own_sem)
    own_copy.start()

    cut = cut_of(starts, flags, tokens)
    through_me = jnp.where(cut < tokens, 0.0, 1.0)
    live = jnp.where(cut < tokens, cut, 0)
    final_start = jnp.float32(1.0)
    for slot in range(slots):
        final_start = jnp.where(starts[0, slot] == tokens - 1, 0.0, final_start)

    for copy in tail_copies:
        copy.wait()
    for index in range(3):
        two = tails[index, 8:16, :].astype(f32)
        rim_out[2 * index : 2 * index + 1, :] = two[6:7] * final_start
        rim_out[2 * index + 1 : 2 * index + 2, :] = two[7:8]
    rim_out[6:8, :] = jnp.zeros((2, channels), f32)
    rim_copy = remote(rim_out, rim_in, rim_sem.at[0], rim_sem.at[1], me + 1)

    pl.semaphore_wait(
        barrier, 3 + zs - 1 + jnp.where(me < n - 1, 1, 0) + jnp.where(me > 0, 1, 0))
    pl.when(me < n - 1)(rim_copy.start)
    issue(last, 0, 1, across)
    issue(0, 0, 1, across)
    issue(0, 0, 2, both)
    for part in range(last + 1):
        forward(here, part, ((3, None),), True, False)

    for half in range(modes // 8):
        for group in range(lane_groups):
            cols = slice(group * LANES, (group + 1) * LANES)
            tile, at = group // GROUPS, group % GROUPS
            spot = pl.ds((tile * modes + half * 8) * GROUPS + at, 8, stride=GROUPS)
            rate_t[spot, :] = rate_ref[half * 8 : half * 8 + 8, cols]
            res_t[spot, :] = res_ref[half * 8 : half * 8 + 8, cols]

    def fill_factors(step, carry):
        rows = pl.ds(pl.multiple_of(step * 32, 32), 32)
        fac_t[rows, :] = jnp.exp(-rate_t[rows, :])
        return carry

    lax.fori_loop(0, modes * lane_groups // 32, fill_factors, 0)

    def table(ref, mode, tile):
        first = (tile * modes + mode) * GROUPS
        return ref[first : first + GROUPS, :]

    for plane in range(zs - 1):

        @pl.when(z <= plane)
        def _(plane=plane):
            for tile in range(tiles):
                crcv[tile, 3 + plane] = jnp.zeros(crcv.shape[2:], crcv.dtype)

    @pl.when(me == 0)
    def _():
        rim_in[...] = jnp.zeros(rim_in.shape, f32)

    def masks(row):
        at = lax.broadcasted_iota(jnp.int32, (RB, LANES), 0) + row
        hit = jnp.zeros((RB, LANES), jnp.bool_)
        hit_before = jnp.zeros((RB, LANES), jnp.bool_)
        for slot in range(slots):
            hit = hit | (at == starts[0, slot])
            hit_before = hit_before | (at - 1 == starts[0, slot])
        return jnp.where(hit, 0.0, 1.0), jnp.where(hit | hit_before, 0.0, 1.0)

    def short(index, row, cols, mask1, mask2, first):
        now = xin[index, pl.ds(row, RB), cols].astype(f32)
        if first:
            before = rimx[index, :, cols]
        else:
            before = xin[index, pl.ds(pl.multiple_of(row - 16, 16), 16), cols].astype(f32)[8:]
        joined = jnp.concatenate([before, now], axis=0)
        lag1 = pltpu.roll(joined, 1, 0)[8:]
        lag2 = pltpu.roll(joined, 2, 0)[8:]
        summed = taps_ref[index, 0:1, cols] * now
        summed = summed + taps_ref[index, 1:2, cols] * mask1 * lag1
        summed = summed + taps_ref[index, 2:3, cols] * mask2 * lag2
        return summed.astype(jnp.bfloat16)

    def gate_rows(tile, row, first):
        mask1, mask2 = masks(row)
        for group in range(GROUPS):
            cols = slice(tile * TILE + group * LANES, tile * TILE + (group + 1) * LANES)
            key = short(1, row, cols, mask1, mask2, first).astype(f32)
            value = short(2, row, cols, mask1, mask2, first).astype(f32)
            z_ref[tile, pl.ds(row * GROUPS + group, RB, stride=GROUPS), :] = key * value

    def gate(tile):
        load(1, tile).wait()
        load(2, tile).wait()

        def rows(step, carry):
            gate_rows(tile, pl.multiple_of(step * RB, RB), False)
            return carry

        lax.fori_loop(1, tokens // RB, rows, 0)

    def end_states(tile):
        zero = jnp.zeros((GROUPS, LANES), f32)

        def advance(step, states):
            states = list(states)
            for inner in range(UNROLL):
                time = step * UNROLL + inner
                spot = pl.ds(pl.multiple_of(time * GROUPS, GROUPS), GROUPS)
                item = z_ref[tile, spot, :] * jnp.where(time >= live, 1.0, 0.0)
                for mode in range(modes):
                    states[mode] = table(fac_t, mode, tile) * states[mode] + item
            return tuple(states)

        states = lax.fori_loop(0, tokens // UNROLL, advance, (zero,) * modes)
        for mode in range(modes):
            tot[tile, mode * GROUPS : (mode + 1) * GROUPS] = states[mode]
        tot[tile, deep:] = zero + through_me
        chain_post(tile, 0)

    peers = (sib, x_peer, y_peer)
    bits = (core, x, y)
    deep = modes * GROUPS
    chunk = 4 * GROUPS

    def chain_pack(tile, step):
        csnd[tile, step, :deep] = tot[tile, :deep].astype(jnp.bfloat16)
        through = tot[tile, deep:]
        csnd[tile, step, deep:] = jnp.concatenate([through, through]).astype(jnp.bfloat16)

    def chain_copy(tile, step):
        return remote(csnd.at[tile, step], crcv.at[tile, step], chain_send_sem.at[tile, step],
                      chain_recv_sem.at[tile, step], peers[step])

    def line_copy(tile, gap, plane):
        return remote(csnd.at[tile, 3], crcv.at[tile, 3 + plane],
                      chain_send_sem.at[tile, 2 + gap], chain_recv_sem.at[tile, 3 + plane],
                      me + gap * PLANE)

    def chain_post(tile, step):
        chain_pack(tile, step)
        if step < 3:
            chain_copy(tile, step).start()
        else:
            for gap in range(1, zs):
                pl.when(z + gap < zs)(line_copy(tile, gap, z).start)

    def message(tile, step, first, rows):
        return crcv[tile, step, first : first + rows].astype(f32)

    def rates(tile, first):
        return rate_t[tile * deep + first : tile * deep + first + chunk]

    def chain_step(tile, step):
        chain_copy(tile, step).wait_recv()
        upper = bits[step] == 1
        span = float(tokens * 2**step)
        before = (lax.rem(me, 2**step) * tokens).astype(f32)
        through_mine = tot[tile, deep:]
        through_other = message(tile, step, deep, 16)[:GROUPS]
        through_late = jnp.where(upper, through_mine, through_other)[0:1]
        if step:
            through_pre = pre[tile, deep:]
        else:
            through_pre = jnp.ones((GROUPS, LANES), f32)
        for first in range(0, deep, chunk):
            rows = slice(first, first + chunk)
            rate = rates(tile, first)
            mine = tot[tile, rows]
            other = message(tile, step, first, chunk)
            early = jnp.where(upper, other, mine)
            late = jnp.where(upper, mine, other)
            tot[tile, rows] = late + through_late * jnp.exp(-span * rate) * early
            if step:
                old = pre[tile, rows]
                fade = through_pre[0:1] * jnp.exp(-before * rate)
                pre[tile, rows] = jnp.where(upper, old + fade * other, old)
            else:
                pre[tile, rows] = jnp.where(upper, other, 0.0)
        tot[tile, deep:] = through_mine * through_other
        pre[tile, deep:] = jnp.where(upper, through_pre * through_other, through_pre)
        chain_post(tile, step + 1)

    def chain_line(tile):
        for plane in range(zs - 1):
            pl.when(plane < z)(line_copy(tile, 1, plane).wait_recv)
        before = (lax.rem(me, PLANE) * tokens).astype(f32)
        through_pre = pre[tile, deep : deep + 1]
        for first in range(0, deep, chunk):
            rate = rates(tile, first)
            fade = jnp.exp(-float(tokens * PLANE) * rate)
            entering = jnp.zeros((chunk, LANES), f32)
            for plane in range(zs - 1):
                through = message(tile, 3 + plane, deep, 16)[0:1]
                item = message(tile, 3 + plane, first, chunk)
                entering = jnp.where(plane < z, item + through * fade * entering, entering)
            ent[tile, first : first + chunk] = (
                pre[tile, first : first + chunk]
                + through_pre * jnp.exp(-before * rate) * entering)

    half = tokens // 2

    def act_copy(tile, part):
        cols = pl.ds(tile * TILE, TILE)
        return remote(acts.at[pl.ds(part * half, half), cols],
                      acts.at[pl.ds(tokens + part * half, half), cols],
                      act_sem.at[0, tile, part], act_sem.at[1, tile, part], x_peer)

    def queries(tile):
        load(0, tile).wait()

        def query_rows(row, first):
            mask1, mask2 = masks(row)
            for group in range(GROUPS):
                cols = slice(tile * TILE + group * LANES, tile * TILE + (group + 1) * LANES)
                acts[pl.ds(row, RB), cols] = short(0, row, cols, mask1, mask2, first)

        def rows(step, carry):
            query_rows(pl.multiple_of(step * RB, RB), False)
            return carry

        query_rows(0, True)
        lax.fori_loop(1, tokens // RB, rows, 0)

    def finish(tile):
        skip = skip_ref[tile * GROUPS : (tile + 1) * GROUPS, :]

        def advance(step, states):
            states = list(states)
            for inner in range(UNROLL):
                time = step * UNROLL + inner
                spot = pl.ds(pl.multiple_of(time * GROUPS, GROUPS), GROUPS)
                keep = jnp.where(time == cut, 0.0, 1.0)
                item = z_ref[tile, spot, :]
                sums = [skip * item, None]
                for mode in range(modes):
                    states[mode] = (table(fac_t, mode, tile) * keep) * states[mode] + item
                    term = table(res_t, mode, tile) * states[mode]
                    sums[mode % 2] = term if sums[mode % 2] is None else sums[mode % 2] + term
                z_ref[tile, spot, :] = sums[0] + sums[1]
            return tuple(states)

        def mix(step, carry):
            row = pl.multiple_of(step * RB, RB)
            for group in range(GROUPS):
                cols = slice(tile * TILE + group * LANES, tile * TILE + (group + 1) * LANES)
                mixed = z_ref[tile, pl.ds(row * GROUPS + group, RB, stride=GROUPS), :]
                query = acts[pl.ds(row, RB), cols].astype(f32)
                acts[pl.ds(row, RB), cols] = (query * mixed).astype(jnp.bfloat16)
            return carry

        states = tuple(ent[tile, mode * GROUPS : (mode + 1) * GROUPS] for mode in range(modes))
        for part in range(2):
            steps = half // UNROLL
            states = lax.fori_loop(part * steps, (part + 1) * steps, advance, states)
            steps = half // RB
            lax.fori_loop(part * steps, (part + 1) * steps, mix, 0)
            act_copy(tile, part).start()

    def columns(block, plane):
        return pl.ds(pl.multiple_of((block * 2 + plane) * 2 * feats, LANES), 2 * feats)

    def out_copy(block):
        return remote(obuf.at[block, pl.ds(tokens, tokens), :], out_hbm.at[:, columns(block, x)],
                      out_send_sem.at[block], out_recv_sem.at[block], x_peer)

    def own_out(block):
        return pltpu.make_async_copy(obuf.at[block, pl.ds(0, tokens), :],
                                     out_hbm.at[:, columns(block, x)], out_sem.at[block])

    def project(block):
        wait_sibling(block)

        def depth(step, carry):
            cols = pl.ds(pl.multiple_of(step * TILE, TILE), TILE)
            term = lax.dot_general(acts[:, cols], wbuf[block, :, cols], (((1,), (1,)), ((), ())),
                                   preferred_element_type=f32)

            acc_ref[...] = jnp.where(step == 0, 0.0, acc_ref[...]) + term
            return carry

        acc_ref[...] = jnp.zeros(acc_ref.shape, f32)
        lax.fori_loop(0, tiles, depth, 0)
        obuf[block] = acc_ref[...].astype(jnp.bfloat16)
        out_copy(block).start()
        own_out(block).start()

    gate(0)
    gate(1)
    pl.when(me > 0)(rim_copy.wait_recv)
    for index in range(3):
        rimx[index] = jnp.zeros((8, channels), f32)
        rimx[index, 6:8, :] = rim_in[2 * index : 2 * index + 2, :]
    gate_rows(0, 0, True)
    gate_rows(1, 0, True)
    end_states(0)
    issue(0, 1, 1, across)
    issue(0, 2, 1, both)
    end_states(1)
    chain_step(0, 0)
    gate(2)
    gate_rows(2, 0, True)
    chain_step(1, 0)
    issue(0, 3, 1, both)
    end_states(2)
    chain_step(0, 1)
    issue(0, 2, 1, across)
    gate(3)
    gate_rows(3, 0, True)
    chain_step(1, 1)
    chain_step(2, 0)
    issue(0, 3, 1, across)
    end_states(3)
    chain_step(0, 2)
    issue(1, 0, 1, both)
    queries(0)
    chain_step(1, 2)
    chain_step(2, 1)
    chain_step(3, 0)
    issue(1, 0, 1, across)
    issue(1, 1, 1, both)
    chain_line(0)
    finish(0)
    chain_step(2, 2)
    chain_step(3, 1)
    issue(1, 1, 2, across)
    issue(1, 2, 1, both)
    issue(last, 0, 1, both)
    poll_last_across()
    queries(1)
    chain_line(1)
    chain_step(3, 2)
    poll_line(1, 0)
    finish(1)
    poll_line(1, 1)
    poll_across(0, 0)
    queries(2)
    chain_line(2)
    finish(2)
    poll_across(0, 1)
    poll_last_line(1)
    queries(3)
    chain_line(3)
    finish(3)
    for distance in range(2, zs):
        poll_line(distance, 0)
        poll_across(distance - 1, 0)
        if distance < zs - 1:
            poll_line(distance, 1)
            poll_across(distance - 1, 1)
            poll_last_line(distance)
    for tile in range(tiles):
        for part in range(2):
            act_copy(tile, part).wait_recv()
    own_copy.wait()
    for rank in range(zs - 1):
        project(source(rank) * 2 + y)
        if rank == 0:
            poll_line(zs - 1, 1)
            poll_across(zs - 2, 1)
        project(source(rank) * 2 + 1 - y)
    poll_last_line(zs - 1)
    project(source(zs - 1) * 2 + y)
    for part in range(last):
        poll_across(zs - 1, part)
    project(source(zs - 1) * 2 + 1 - y)

    finish_own()
    for distance in range(1, zs):
        for part in range(last):
            poll_line(distance, part, True)
        poll_last_line(distance, True)
    for distance in range(zs):
        for part in range(last):
            poll_across(distance, part, True)
    poll_last_across(True)
    pl.when(me < n - 1)(rim_copy.wait_send)
    for tile in range(tiles):
        for step in range(3):
            chain_copy(tile, step).wait_send()
        for gap in range(1, zs):
            pl.when(z + gap < zs)(line_copy(tile, gap, z).wait_send)
        for part in range(2):
            act_copy(tile, part).wait_send()
    for block in range(blocks):
        own_out(block).wait()
        out_copy(block).wait()


def fused(q_feat, k_feat, v_feat, short_taps, decay_rate, residue, skip_gain, out_weight,
          doc_starts, reset_flags):
    tokens, channels = q_feat.shape
    modes = decay_rate.shape[0]
    n = lax.axis_size("seq")
    zs = n // PLANE
    tiles = channels // TILE
    feats = out_weight.shape[0]
    f32, bf16 = jnp.float32, jnp.bfloat16
    vmem = pl.BlockSpec(memory_space=pltpu.VMEM)
    smem = pl.BlockSpec(memory_space=pltpu.SMEM)
    hbm = pl.BlockSpec(memory_space=pl.ANY)
    dma = pltpu.SemaphoreType.DMA
    table = pltpu.VMEM((modes * channels // LANES, LANES), f32)
    return pl.pallas_call(
        functools.partial(fused_kernel, zs),
        in_specs=[smem, smem, hbm, hbm, hbm, hbm, vmem, vmem, vmem, vmem],
        out_specs=hbm,
        out_shape=jax.ShapeDtypeStruct((tokens, n * feats), bf16),
        scratch_shapes=[
            pltpu.VMEM((2 * zs, 2 * feats, channels), bf16),
            pltpu.VMEM((3, tokens, channels), bf16),
            pltpu.VMEM((3, 16, channels), bf16),
            pltpu.VMEM((8, channels), f32),
            pltpu.VMEM((8, channels), f32),
            pltpu.VMEM((3, 8, channels), f32),
            pltpu.VMEM((tiles, tokens * GROUPS, LANES), f32),
            pltpu.VMEM((2 * tokens, channels), bf16),
            pltpu.VMEM((2 * zs, 2 * tokens, 2 * feats), bf16),
            pltpu.VMEM((2 * tokens, 2 * feats), f32),
            table, table, table,
            pltpu.VMEM((tiles, 4, (modes + 2) * GROUPS, LANES), bf16),
            pltpu.VMEM((tiles, 2 + zs, (modes + 2) * GROUPS, LANES), bf16),
            pltpu.VMEM((tiles, (modes + 1) * GROUPS, LANES), f32),
            pltpu.VMEM((tiles, (modes + 1) * GROUPS, LANES), f32),
            pltpu.VMEM((tiles, modes * GROUPS, LANES), f32),
            dma((3, tiles)), dma((3,)), dma((2,)),
            dma((2 * zs, len(PARTS), 4)), dma((2, 2 * zs, len(PARTS))), dma,
            dma((tiles, 2 + zs)), dma((tiles, 2 + zs)), dma((2, tiles, 2)),
            dma((2 * zs,)), dma((2 * zs,)), dma((2 * zs,)),
        ],
        compiler_params=pltpu.CompilerParams(
            collective_id=0, has_side_effects=True, vmem_limit_bytes=58 * 2**20
        ),
        name="mixer",
    )(doc_starts, reset_flags, q_feat, k_feat, v_feat, out_weight, short_taps, decay_rate,
      residue, skip_gain.reshape(channels // LANES, LANES))


def local(q_feat, k_feat, v_feat, short_taps, decay_rate, residue, skip_gain, out_weight,
          doc_starts, reset_flags):
    tokens, channels = q_feat.shape
    modes = decay_rate.shape[0]
    kinds, taps = short_taps.shape[:2]
    n = lax.axis_size("seq")
    me = lax.axis_index("seq")
    tiles = channels // TILE
    heads = modes + 8

    weight = lax.all_gather(out_weight, "seq", axis=0, tiled=True)

    last_is_start = jnp.any(doc_starts[0] == tokens - 1)
    scale = jnp.stack([jnp.where(last_is_start, 0.0, 1.0), jnp.float32(1.0)]).astype(jnp.bfloat16)
    tails = jnp.stack([x[tokens - (taps - 1) :] for x in (q_feat, k_feat, v_feat)])
    tails = tails * scale[None, :, None]
    arrived = lax.ppermute(tails, "seq", [(i, i + 1) for i in range(n - 1)])
    rim = jnp.pad(arrived, ((0, 0), (ROWS - (taps - 1), 0), (0, 0)))

    rates = decay_rate.reshape(modes, channels // LANES, LANES)
    residues = residue.reshape(modes, channels // LANES, LANES)
    skips = skip_gain.reshape(channels // LANES, LANES)

    smem = pl.BlockSpec(memory_space=pltpu.SMEM)
    wide = pl.BlockSpec((tokens, TILE), lambda i: (0, i))
    deep = pl.BlockSpec((modes, GROUPS, LANES), lambda i: (0, i, 0))
    flat = pl.BlockSpec((None, tokens * GROUPS, LANES), lambda i: (i, 0, 0))
    f32 = jnp.float32
    qs, z, state = pl.pallas_call(
        local_kernel,
        grid=(tiles,),
        in_specs=[
            smem, smem, wide, wide, wide,
            pl.BlockSpec((kinds, ROWS, TILE), lambda i: (0, 0, i)),
            pl.BlockSpec((kinds * taps, TILE), lambda i: (0, i)),
            deep, deep,
            pl.BlockSpec((GROUPS, LANES), lambda i: (i, 0)),
        ],
        out_specs=[wide, flat, pl.BlockSpec((heads, GROUPS, LANES), lambda i: (0, i, 0))],
        out_shape=[
            jax.ShapeDtypeStruct((tokens, channels), jnp.bfloat16),
            jax.ShapeDtypeStruct((tiles, tokens * GROUPS, LANES), f32),
            jax.ShapeDtypeStruct((heads, channels // LANES, LANES), f32),
        ],
        scratch_shapes=[pltpu.VMEM((modes, GROUPS, LANES), f32)],
        cost_estimate=pl.CostEstimate(
            flops=tokens * channels * 80, bytes_accessed=tokens * channels * 12, transcendentals=0
        ),
        name="local_filter",
    )(doc_starts, reset_flags, q_feat, k_feat, v_feat, rim,
      short_taps.reshape(kinds * taps, channels), rates, residues, skips)

    part = channels // n
    sent = state.reshape(heads, n, part).transpose(1, 0, 2)
    pieces = lax.all_to_all(sent, "seq", 0, 0)
    my_rates = lax.dynamic_slice_in_dim(decay_rate, me * part, part, 1)
    chained = pl.pallas_call(
        functools.partial(scan_kernel, tokens),
        out_shape=jax.ShapeDtypeStruct((n, modes, part), f32),
        name="chain_states",
    )(pieces, my_rates)
    entering = lax.all_to_all(chained, "seq", 0, 0)
    entering = entering.transpose(1, 0, 2).reshape(modes, channels // LANES, LANES)

    mixed = pl.pallas_call(
        finish_kernel,
        grid=(tiles,),
        in_specs=[smem, smem, wide, flat, deep, deep, deep],
        out_specs=wide,
        out_shape=jax.ShapeDtypeStruct((tokens, channels), jnp.bfloat16),
        scratch_shapes=[
            pltpu.VMEM((modes, GROUPS, LANES), f32),
            pltpu.VMEM((tokens * GROUPS, LANES), f32),
        ],
        cost_estimate=pl.CostEstimate(
            flops=tokens * channels * 40, bytes_accessed=tokens * channels * 8, transcendentals=0
        ),
        name="finish_filter",
    )(doc_starts, reset_flags, qs, z, entering, rates, residues)

    projected = lax.dot_general(
        mixed, weight, (((1,), (1,)), ((), ())), preferred_element_type=f32
    ).astype(jnp.bfloat16)
    return lax.psum_scatter(projected, "ch", scatter_dimension=1, tiled=True)


def solution(mesh):
    placed = (
        P("seq", "ch"), P("seq", "ch"), P("seq", "ch"), P(None, None, "ch"), P(None, "ch"),
        P(None, "ch"), P("ch"), P("seq", "ch"), P("seq", None), P("seq", None),
    )
    direct = mesh.shape["ch"] == 1 and mesh.shape["seq"] % (2 * PLANE) == 0
    return jax.shard_map(
        fused if direct else local, mesh=mesh, in_specs=placed, out_specs=P("seq", "ch"), check_vma=False
    )
```

```python
import functools

import jax
import jax.numpy as jnp
from jax import lax
from jax.experimental import pallas as pl
from jax.experimental.pallas import tpu as pltpu
from jax.sharding import PartitionSpec as P

LANES = 128
GROUPS = 8
TILE = LANES * GROUPS
ROWS = 16
UNROLL = 8


def cut_of(starts, flags, tokens):
    cut = jnp.int32(tokens)
    for slot in range(starts.shape[1]):
        cut = jnp.where(flags[0, slot] == 1, jnp.minimum(cut, starts[0, slot]), cut)
    return cut


def local_kernel(starts, flags, q_ref, k_ref, v_ref, rim_ref, taps_ref, rate_ref, res_ref,
                 skip_ref, qs_ref, z_ref, state_ref, fac_ref):
    tokens = q_ref.shape[0]
    modes = rate_ref.shape[0]
    slots = starts.shape[1]
    cut = cut_of(starts, flags, tokens)

    def short_rows(step, carry):
        row = pl.multiple_of(step * ROWS, ROWS)
        back = pl.multiple_of(jnp.maximum(row - ROWS, 0), ROWS)
        at = lax.broadcasted_iota(jnp.int32, (ROWS, LANES), 0) + row
        hit = jnp.zeros((ROWS, LANES), jnp.bool_)
        hit_before = jnp.zeros((ROWS, LANES), jnp.bool_)
        for slot in range(slots):
            hit = hit | (at == starts[0, slot])
            hit_before = hit_before | (at - 1 == starts[0, slot])
        mask1 = jnp.where(hit, 0.0, 1.0)
        mask2 = jnp.where(hit | hit_before, 0.0, 1.0)
        first = step == 0
        for group in range(GROUPS):
            cols = slice(group * LANES, (group + 1) * LANES)

            def short(ref, index):
                x = ref[pl.ds(row, ROWS), cols].astype(jnp.float32)
                before = ref[pl.ds(back, ROWS), cols].astype(jnp.float32)
                rim = rim_ref[index, :, cols].astype(jnp.float32)
                before = jnp.where(first, rim, before)
                both = jnp.concatenate([before, x], axis=0)
                lag1 = pltpu.roll(both, 1, 0)[ROWS:]
                lag2 = pltpu.roll(both, 2, 0)[ROWS:]
                base = 3 * index
                summed = taps_ref[base : base + 1, cols] * x
                summed = summed + taps_ref[base + 1 : base + 2, cols] * mask1 * lag1
                summed = summed + taps_ref[base + 2 : base + 3, cols] * mask2 * lag2
                return summed.astype(jnp.bfloat16)

            qs_ref[pl.ds(row, ROWS), cols] = short(q_ref, 0)
            gated = short(k_ref, 1).astype(jnp.float32) * short(v_ref, 2).astype(jnp.float32)
            z_ref[pl.ds(row * GROUPS + group, ROWS, stride=GROUPS), :] = gated
        return carry

    lax.fori_loop(0, tokens // ROWS, short_rows, 0)

    fac_ref[...] = jnp.exp(-rate_ref[...])
    skip = skip_ref[...]

    def advance(step, states):
        states = list(states)
        for inner in range(UNROLL):
            time = step * UNROLL + inner
            spot = pl.ds(pl.multiple_of(time * GROUPS, GROUPS), GROUPS)
            keep = jnp.where(time == cut, 0.0, 1.0)
            x = z_ref[spot, :]
            sums = [skip * x, None]
            for n in range(modes):
                states[n] = (fac_ref[n] * keep) * states[n] + x
                term = res_ref[n] * states[n]
                sums[n % 2] = term if sums[n % 2] is None else sums[n % 2] + term
            z_ref[spot, :] = sums[0] + sums[1]
        return tuple(states)

    zero = jnp.zeros((GROUPS, LANES), jnp.float32)
    states = lax.fori_loop(0, tokens // UNROLL, advance, (zero,) * modes)
    for n in range(modes):
        state_ref[n] = states[n]
    through = jnp.where(cut < tokens, 0.0, 1.0)
    for n in range(modes, state_ref.shape[0]):
        state_ref[n] = zero + through


def scan_kernel(tokens, pieces_ref, rate_ref, out_ref):
    modes = rate_ref.shape[0]
    factor = jnp.exp(-float(tokens) * rate_ref[...])

    def hop(j, running):
        out_ref[j] = running
        piece = pieces_ref[j]
        return factor * piece[modes : modes + 1] * running + piece[:modes]

    lax.fori_loop(0, pieces_ref.shape[0], hop, jnp.zeros(rate_ref.shape, jnp.float32))


def finish_kernel(starts, flags, qs_ref, z_ref, enter_ref, rate_ref, res_ref, out_ref, fac_ref,
                  y_ref):
    tokens = qs_ref.shape[0]
    modes = rate_ref.shape[0]
    cut = cut_of(starts, flags, tokens)
    fac_ref[...] = jnp.exp(-rate_ref[...])

    def advance(step, weights):
        weights = list(weights)
        for inner in range(UNROLL):
            time = step * UNROLL + inner
            spot = pl.ds(pl.multiple_of(time * GROUPS, GROUPS), GROUPS)
            alive = jnp.where(time < cut, 1.0, 0.0)
            sums = [None, None]
            for n in range(modes):
                sums[n % 2] = weights[n] if sums[n % 2] is None else sums[n % 2] + weights[n]
                weights[n] = weights[n] * fac_ref[n]
            y_ref[spot, :] = z_ref[spot, :] + alive * (sums[0] + sums[1])
        return tuple(weights)

    begin = tuple(res_ref[n] * (fac_ref[n] * enter_ref[n]) for n in range(modes))
    lax.fori_loop(0, tokens // UNROLL, advance, begin)

    def mix_rows(step, carry):
        row = pl.multiple_of(step * ROWS, ROWS)
        for group in range(GROUPS):
            cols = slice(group * LANES, (group + 1) * LANES)
            y = y_ref[pl.ds(row * GROUPS + group, ROWS, stride=GROUPS), :]
            q = qs_ref[pl.ds(row, ROWS), cols].astype(jnp.float32)
            out_ref[pl.ds(row, ROWS), cols] = (q * y).astype(jnp.bfloat16)
        return carry

    lax.fori_loop(0, tokens // ROWS, mix_rows, 0)


PLANE = 8
RB = 32
PARTS = ((0, 64), (64, 48), (112, 16))
PIECE = 16


def fused_kernel(zs, starts, flags, q_hbm, k_hbm, v_hbm, w_hbm, taps_ref, rate_ref, res_ref,
                 skip_ref, out_hbm, wbuf, xin, tails, rim_out, rim_in, rimx, z_ref, acts, obuf,
                 fac_t, rate_t, span_t, res_t, csnd, crcv, tot, pre, ent, load_sem, tail_sem,
                 rim_sem, wsend, wrecv, own_sem, chain_send_sem, chain_recv_sem, act_sem,
                 out_send_sem, out_recv_sem, out_sem):
    _, tokens, channels = xin.shape
    modes = rate_ref.shape[0]
    slots = starts.shape[1]
    feats = w_hbm.shape[0]
    tiles = channels // TILE
    lane_groups = channels // LANES
    blocks = 2 * zs
    n = PLANE * zs
    f32 = jnp.float32

    me = lax.axis_index("seq")
    core = lax.rem(me, 2)
    x = lax.rem(me // 2, 2)
    y = lax.rem(me // 4, 2)
    z = me // PLANE
    sib = me + 1 - 2 * core
    x_peer = me + 2 - 4 * x
    y_peer = me + 4 - 8 * y
    up, down = me + PLANE, me - PLANE
    has_up, has_down = z < zs - 1, z > 0

    order = [sorted(range(zs), key=lambda s, at=at: (abs(s - at), s)) for at in range(zs)]

    def source(rank):
        at = jnp.int32(order[0][rank])
        for level in range(1, zs):
            at = jnp.where(z == level, order[level][rank], at)
        return at

    def remote(src, dst, send, recv, dev):
        return pltpu.make_async_remote_copy(
            src_ref=src, dst_ref=dst, send_sem=send, recv_sem=recv,
            device_id={"seq": dev}, device_id_type=pl.DeviceIdType.MESH,
        )

    def piece(block, side, part):
        first, rows = PARTS[part]
        row = pl.multiple_of(side * feats + first, 16)
        return wbuf.at[block, pl.ds(row, rows), :]

    def weight_copy(block, part, way, own):
        first, rows = PARTS[part]
        dst = piece(block, core, part)
        src = w_hbm.at[pl.ds(first, rows), :] if own else dst
        return remote(src, dst, wsend.at[block, part, way],
                      wrecv.at[1 if way == 3 else 0, block, part],
                      (up, down, y_peer, sib)[way])

    def wait_weight(block, part):
        first, rows = PARTS[part]
        dst = piece(block, core, part)
        remote(dst, dst, wsend.at[block, part, 0], wrecv.at[0, block, part], sib).wait_recv()

    def wait_sibling(block):
        for part in range(len(PARTS)):
            dst = piece(block, 1 - core, part)
            remote(dst, dst, wsend.at[block, part, 3], wrecv.at[1, block, part], sib).wait_recv()

    def forward(block, part, ways, own, done):
        for way, cond in ways:
            copy = weight_copy(block, part, way, own)
            act = copy.wait_send if done else copy.start
            if cond is None:
                act()
            else:
                pl.when(cond)(act)

    both = ((0, has_up), (1, has_down))
    here = z * 2 + y
    there = z * 2 + 1 - y
    last = len(PARTS) - 1

    def issue(part, first, count, ways):
        for index in range(first, first + count):
            row = PARTS[part][0] + index * PIECE
            spot = pl.ds(pl.multiple_of(core * feats + row, 16), PIECE)
            for way, cond in ways:
                copy = remote(w_hbm.at[pl.ds(row, PIECE), :], wbuf.at[here, spot, :],
                              wsend.at[here, part, way], wrecv.at[0, here, part],
                              (up, down, y_peer)[way])
                if cond is None:
                    copy.start()
                else:
                    pl.when(cond)(copy.start)

    across = ((2, None),)

    def finish_own():
        for part in range(last + 1):
            forward(here, part, both + ((2, None), (3, None)), True, True)

    def each_side(distance, act):
        pl.when(z >= distance)(lambda: act(z - distance, ((0, has_up),)))
        pl.when(z + distance < zs)(lambda: act(z + distance, ((1, has_down),)))

    def poll_line(distance, part, done=False, ways="yz"):
        def act(src, on_way):
            block = src * 2 + y
            if not done and "y" in ways:
                wait_weight(block, part)
            if "z" in ways:
                forward(block, part, on_way, False, done)
            if "y" in ways:
                forward(block, part, ((2, None), (3, None)), False, done)

        each_side(distance, act)

    def poll_across(rank, part, done=False):
        block = source(rank) * 2 + 1 - y
        if not done:
            wait_weight(block, part)
        forward(block, part, ((3, None),), False, done)

    def poll_last_across(done=False):
        if not done:
            wait_weight(there, last)
        forward(there, last, both + ((3, None),), False, done)

    def poll_last_line(distance, done=False):
        def act(src, on_way):
            for side in (y, 1 - y):
                block = src * 2 + side
                if not done:
                    wait_weight(block, last)
                forward(block, last, on_way + ((3, None),), False, done)

        each_side(distance, act)

    barrier = pltpu.get_barrier_semaphore()

    def greet(dev):
        pl.semaphore_signal(barrier, inc=1, device_id={"seq": dev},
                            device_id_type=pl.DeviceIdType.MESH)

    for dev in (sib, x_peer, y_peer):
        greet(dev)
    for gap in range(1, zs):
        pl.when(z + gap < zs)(lambda gap=gap: greet(me + gap * PLANE))
        pl.when(z >= gap)(lambda gap=gap: greet(me - gap * PLANE))
    pl.when(me < n - 1)(lambda: greet(me + 1))
    pl.when(me > 0)(lambda: greet(me - 1))

    feeds = (q_hbm, k_hbm, v_hbm)
    tail_copies = [
        pltpu.make_async_copy(feeds[i].at[pl.ds(tokens - 16, 16), :], tails.at[i], tail_sem.at[i])
        for i in range(3)
    ]
    for copy in tail_copies:
        copy.start()

    def load(index, tile):
        cols = pl.ds(tile * TILE, TILE)
        return pltpu.make_async_copy(feeds[index].at[:, cols], xin.at[index, :, cols],
                                     load_sem.at[index, tile])

    for index in (1, 2, 0):
        for tile in range(tiles):
            load(index, tile).start()
    own_copy = pltpu.make_async_copy(
        w_hbm, wbuf.at[here, pl.ds(pl.multiple_of(core * feats, 16), feats), :], own_sem)
    own_copy.start()

    cut = cut_of(starts, flags, tokens)
    through_me = jnp.where(cut < tokens, 0.0, 1.0)
    live = jnp.where(cut < tokens, cut, 0)
    final_start = jnp.float32(1.0)
    for slot in range(slots):
        final_start = jnp.where(starts[0, slot] == tokens - 1, 0.0, final_start)

    for copy in tail_copies:
        copy.wait()
    for index in range(3):
        two = tails[index, 8:16, :].astype(f32)
        rim_out[2 * index : 2 * index + 1, :] = two[6:7] * final_start
        rim_out[2 * index + 1 : 2 * index + 2, :] = two[7:8]
    rim_out[6:8, :] = jnp.zeros((2, channels), f32)
    rim_copy = remote(rim_out, rim_in, rim_sem.at[0], rim_sem.at[1], me + 1)

    pl.semaphore_wait(
        barrier, 3 + zs - 1 + jnp.where(me < n - 1, 1, 0) + jnp.where(me > 0, 1, 0))
    pl.when(me < n - 1)(rim_copy.start)
    issue(last, 0, 1, across)
    issue(0, 0, 2, across)
    issue(0, 0, 4, both)
    for part in range(last + 1):
        forward(here, part, ((3, None),), True, False)

    for half in range(modes // 8):
        for group in range(lane_groups):
            cols = slice(group * LANES, (group + 1) * LANES)
            tile, at = group // GROUPS, group % GROUPS
            spot = pl.ds((tile * modes + half * 8) * GROUPS + at, 8, stride=GROUPS)
            rate_t[spot, :] = rate_ref[half * 8 : half * 8 + 8, cols]
            res_t[spot, :] = res_ref[half * 8 : half * 8 + 8, cols]

    def fill_factors(step, carry):
        rows = pl.ds(pl.multiple_of(step * 32, 32), 32)
        fac_t[rows, :] = jnp.exp(-rate_t[rows, :])
        span_t[rows, :] = jnp.exp(-float(tokens) * rate_t[rows, :])
        return carry

    lax.fori_loop(0, modes * lane_groups // 32, fill_factors, 0)

    def table(ref, mode, tile):
        first = (tile * modes + mode) * GROUPS
        return ref[first : first + GROUPS, :]

    for plane in range(zs - 1):

        @pl.when(z <= plane)
        def _(plane=plane):
            for tile in range(tiles):
                crcv[tile, 3 + plane] = jnp.zeros(crcv.shape[2:], crcv.dtype)

    @pl.when(me == 0)
    def _():
        rim_in[...] = jnp.zeros(rim_in.shape, f32)

    def masks(row):
        at = lax.broadcasted_iota(jnp.int32, (RB, LANES), 0) + row
        hit = jnp.zeros((RB, LANES), jnp.bool_)
        hit_before = jnp.zeros((RB, LANES), jnp.bool_)
        for slot in range(slots):
            hit = hit | (at == starts[0, slot])
            hit_before = hit_before | (at - 1 == starts[0, slot])
        return jnp.where(hit, 0.0, 1.0), jnp.where(hit | hit_before, 0.0, 1.0)

    def short(index, row, cols, mask1, mask2, first):
        now = xin[index, pl.ds(row, RB), cols].astype(f32)
        if first:
            before = rimx[index, :, cols]
        else:
            before = xin[index, pl.ds(pl.multiple_of(row - 16, 16), 16), cols].astype(f32)[8:]
        joined = jnp.concatenate([before, now], axis=0)
        lag1 = pltpu.roll(joined, 1, 0)[8:]
        lag2 = pltpu.roll(joined, 2, 0)[8:]
        summed = taps_ref[index, 0:1, cols] * now
        summed = summed + taps_ref[index, 1:2, cols] * mask1 * lag1
        summed = summed + taps_ref[index, 2:3, cols] * mask2 * lag2
        return summed.astype(jnp.bfloat16)

    def gate_rows(tile, row, first):
        mask1, mask2 = masks(row)
        for group in range(GROUPS):
            cols = slice(tile * TILE + group * LANES, tile * TILE + (group + 1) * LANES)
            key = short(1, row, cols, mask1, mask2, first).astype(f32)
            value = short(2, row, cols, mask1, mask2, first).astype(f32)
            z_ref[tile, pl.ds(row * GROUPS + group, RB, stride=GROUPS), :] = key * value

    def gate(tile):
        load(1, tile).wait()
        load(2, tile).wait()

        def rows(step, carry):
            gate_rows(tile, pl.multiple_of(step * RB, RB), False)
            return carry

        lax.fori_loop(1, tokens // RB, rows, 0)

    def end_states(tile):
        zero = jnp.zeros((GROUPS, LANES), f32)

        def advance(step, states):
            states = list(states)
            for inner in range(UNROLL):
                time = step * UNROLL + inner
                spot = pl.ds(pl.multiple_of(time * GROUPS, GROUPS), GROUPS)
                item = z_ref[tile, spot, :] * jnp.where(time >= live, 1.0, 0.0)
                for mode in range(modes):
                    states[mode] = table(fac_t, mode, tile) * states[mode] + item
            return tuple(states)

        states = lax.fori_loop(0, tokens // UNROLL, advance, (zero,) * modes)
        for mode in range(modes):
            tot[tile, mode * GROUPS : (mode + 1) * GROUPS] = states[mode]
        tot[tile, deep:] = zero + through_me

    peers = (sib, x_peer, y_peer)
    bits = (core, x, y)
    deep = modes * GROUPS
    chunk = 4 * GROUPS

    def chain_copy(group, step):
        at = pl.ds(group[0], group[1])
        return remote(csnd.at[at, step], crcv.at[at, step], chain_send_sem.at[group[0], step],
                      chain_recv_sem.at[group[0], step], peers[step])

    def line_copy(group, gap, plane):
        at = pl.ds(group[0], group[1])
        return remote(csnd.at[at, 3], crcv.at[at, 3 + plane],
                      chain_send_sem.at[group[0], 2 + gap], chain_recv_sem.at[group[0], 3 + plane],
                      me + gap * PLANE)

    def members(group):
        return range(group[0], group[0] + group[1])

    def chain_post(group, step):
        for tile in members(group):
            csnd[tile, step, :deep] = tot[tile, :deep].astype(jnp.bfloat16)
            through = tot[tile, deep:]
            csnd[tile, step, deep:] = jnp.concatenate([through, through]).astype(jnp.bfloat16)
        if step < 3:
            chain_copy(group, step).start()
        else:
            for gap in range(1, zs):
                pl.when(z + gap < zs)(line_copy(group, gap, z).start)

    def message(tile, step, first, rows):
        return crcv[tile, step, first : first + rows].astype(f32)

    def spans(tile, first, doublings):
        found = [span_t[tile * deep + first : tile * deep + first + chunk]]
        for _ in range(doublings):
            found.append(found[-1] * found[-1])
        return found

    def before_me(found, step):
        product = None
        for bit in range(step):
            factor = jnp.where(bits[bit] == 1, found[bit], 1.0)
            product = factor if product is None else product * factor
        return product

    def chain_step(group, step):
        chain_copy(group, step).wait_recv()
        upper = bits[step] == 1
        for tile in members(group):
            through_mine = tot[tile, deep:]
            through_other = message(tile, step, deep, 16)[:GROUPS]
            through_late = jnp.where(upper, through_mine, through_other)[0:1]
            if step:
                through_pre = pre[tile, deep:]
            else:
                through_pre = jnp.ones((GROUPS, LANES), f32)
            for first in range(0, deep, chunk):
                rows = slice(first, first + chunk)
                found = spans(tile, first, step)
                mine = tot[tile, rows]
                other = message(tile, step, first, chunk)
                early = jnp.where(upper, other, mine)
                late = jnp.where(upper, mine, other)
                tot[tile, rows] = late + through_late * found[step] * early
                if step:
                    old = pre[tile, rows]
                    fade = through_pre[0:1] * before_me(found, step)
                    pre[tile, rows] = jnp.where(upper, old + fade * other, old)
                else:
                    pre[tile, rows] = jnp.where(upper, other, 0.0)
            tot[tile, deep:] = through_mine * through_other
            pre[tile, deep:] = jnp.where(upper, through_pre * through_other, through_pre)
        chain_post(group, step + 1)

    def chain_line(group):
        for plane in range(zs - 1):
            pl.when(plane < z)(line_copy(group, 1, plane).wait_recv)
        for tile in members(group):
            through_pre = pre[tile, deep : deep + 1]
            for first in range(0, deep, chunk):
                found = spans(tile, first, 3)
                entering = jnp.zeros((chunk, LANES), f32)
                for plane in range(zs - 1):
                    through = message(tile, 3 + plane, deep, 16)[0:1]
                    item = message(tile, 3 + plane, first, chunk)
                    entering = jnp.where(
                        plane < z, item + through * found[3] * entering, entering)
                ent[tile, first : first + chunk] = (
                    pre[tile, first : first + chunk]
                    + through_pre * before_me(found, 3) * entering)

    half = tokens // 2

    def act_copy(tile, part):
        cols = pl.ds(tile * TILE, TILE)
        return remote(acts.at[pl.ds(part * half, half), cols],
                      acts.at[pl.ds(tokens + part * half, half), cols],
                      act_sem.at[0, tile, part], act_sem.at[1, tile, part], x_peer)

    def queries(tile):
        load(0, tile).wait()

        def query_rows(row, first):
            mask1, mask2 = masks(row)
            for group in range(GROUPS):
                cols = slice(tile * TILE + group * LANES, tile * TILE + (group + 1) * LANES)
                acts[pl.ds(row, RB), cols] = short(0, row, cols, mask1, mask2, first)

        def rows(step, carry):
            query_rows(pl.multiple_of(step * RB, RB), False)
            return carry

        query_rows(0, True)
        lax.fori_loop(1, tokens // RB, rows, 0)

    def finish(tile):
        skip = skip_ref[tile * GROUPS : (tile + 1) * GROUPS, :]

        def advance(step, states):
            states = list(states)
            for inner in range(UNROLL):
                time = step * UNROLL + inner
                spot = pl.ds(pl.multiple_of(time * GROUPS, GROUPS), GROUPS)
                keep = jnp.where(time == cut, 0.0, 1.0)
                item = z_ref[tile, spot, :]
                sums = [skip * item, None]
                for mode in range(modes):
                    states[mode] = (table(fac_t, mode, tile) * keep) * states[mode] + item
                    term = table(res_t, mode, tile) * states[mode]
                    sums[mode % 2] = term if sums[mode % 2] is None else sums[mode % 2] + term
                z_ref[tile, spot, :] = sums[0] + sums[1]
            return tuple(states)

        def mix(step, carry):
            row = pl.multiple_of(step * RB, RB)
            for group in range(GROUPS):
                cols = slice(tile * TILE + group * LANES, tile * TILE + (group + 1) * LANES)
                mixed = z_ref[tile, pl.ds(row * GROUPS + group, RB, stride=GROUPS), :]
                query = acts[pl.ds(row, RB), cols].astype(f32)
                acts[pl.ds(row, RB), cols] = (query * mixed).astype(jnp.bfloat16)
            return carry

        states = tuple(ent[tile, mode * GROUPS : (mode + 1) * GROUPS] for mode in range(modes))
        for part in range(2):
            steps = half // UNROLL
            states = lax.fori_loop(part * steps, (part + 1) * steps, advance, states)
            steps = half // RB
            lax.fori_loop(part * steps, (part + 1) * steps, mix, 0)
            act_copy(tile, part).start()

    def columns(block, plane):
        return pl.ds(pl.multiple_of((block * 2 + plane) * 2 * feats, LANES), 2 * feats)

    def out_copy(block):
        return remote(obuf.at[block, pl.ds(tokens, tokens), :], out_hbm.at[:, columns(block, x)],
                      out_send_sem.at[block], out_recv_sem.at[block], x_peer)

    def own_out(block):
        return pltpu.make_async_copy(obuf.at[block, pl.ds(0, tokens), :],
                                     out_hbm.at[:, columns(block, x)], out_sem.at[block])

    def project_rows(block, first):
        rows = slice(first, first + tokens)
        obuf[block, rows] = lax.dot_general(
            acts[rows], wbuf[block], (((1,), (1,)), ((), ())), preferred_element_type=f32
        ).astype(jnp.bfloat16)

    def project(block):
        wait_sibling(block)
        project_rows(block, tokens)
        out_copy(block).start()
        project_rows(block, 0)
        own_out(block).start()

    one, two, rest = (0, 1), (1, 1), (2, tiles - 2)
    gate(0)
    gate(1)
    pl.when(me > 0)(rim_copy.wait_recv)
    for index in range(3):
        rimx[index] = jnp.zeros((8, channels), f32)
        rimx[index, 6:8, :] = rim_in[2 * index : 2 * index + 2, :]
    gate_rows(0, 0, True)
    end_states(0)
    chain_post(one, 0)
    gate_rows(1, 0, True)
    end_states(1)
    chain_step(one, 0)
    chain_post(two, 0)
    gate(2)
    gate_rows(2, 0, True)
    chain_step(two, 0)
    end_states(2)
    chain_step(one, 1)
    issue(0, 2, 1, across)
    for tile in range(3, tiles):
        gate(tile)
        gate_rows(tile, 0, True)
    chain_step(two, 1)
    issue(0, 3, 1, across)
    issue(1, 0, 1, across)
    for tile in range(3, tiles):
        end_states(tile)
    chain_step(one, 2)
    issue(1, 0, 2, both)
    chain_post(rest, 0)
    queries(0)
    chain_step(two, 2)
    issue(1, 2, 1, both)
    chain_step(rest, 0)
    chain_line(one)
    finish(0)
    chain_step(rest, 1)
    issue(1, 1, 2, across)
    poll_line(1, 0, ways="y")
    poll_across(0, 0)
    queries(1)
    chain_line(two)
    finish(1)
    chain_step(rest, 2)
    poll_line(1, 0, ways="z")
    poll_line(1, 1)
    poll_across(0, 1)
    queries(2)
    queries(3)
    chain_line(rest)
    for tile in range(2, tiles):
        finish(tile)
    for distance in range(2, zs - 1):
        for part in range(last):
            poll_line(distance, part)
    issue(last, 0, 1, both)
    poll_last_across()
    for part in range(last):
        poll_across(1, part)
        poll_line(zs - 1, part)
    poll_last_line(1)
    for tile in range(tiles):
        for part in range(2):
            act_copy(tile, part).wait_recv()
    own_copy.wait()
    project(source(0) * 2 + y)
    project(source(0) * 2 + 1 - y)
    for rank in range(1, zs):
        if rank > 1:
            poll_last_line(rank)
        project(source(rank) * 2 + y)
        if rank > 1:
            for part in range(last):
                poll_across(rank, part)
        project(source(rank) * 2 + 1 - y)

    finish_own()
    for distance in range(1, zs):
        for part in range(last):
            poll_line(distance, part, True)
        poll_last_line(distance, True)
    for distance in range(zs):
        for part in range(last):
            poll_across(distance, part, True)
    poll_last_across(True)
    pl.when(me < n - 1)(rim_copy.wait_send)
    for group in (one, two, rest):
        for step in range(3):
            chain_copy(group, step).wait_send()
        for gap in range(1, zs):
            pl.when(z + gap < zs)(line_copy(group, gap, z).wait_send)
    for tile in range(tiles):
        for part in range(2):
            act_copy(tile, part).wait_send()
    for block in range(blocks):
        own_out(block).wait()
        out_copy(block).wait()


def fused(q_feat, k_feat, v_feat, short_taps, decay_rate, residue, skip_gain, out_weight,
          doc_starts, reset_flags):
    tokens, channels = q_feat.shape
    modes = decay_rate.shape[0]
    n = lax.axis_size("seq")
    zs = n // PLANE
    tiles = channels // TILE
    feats = out_weight.shape[0]
    f32, bf16 = jnp.float32, jnp.bfloat16
    vmem = pl.BlockSpec(memory_space=pltpu.VMEM)
    smem = pl.BlockSpec(memory_space=pltpu.SMEM)
    hbm = pl.BlockSpec(memory_space=pl.ANY)
    dma = pltpu.SemaphoreType.DMA
    table = pltpu.VMEM((modes * channels // LANES, LANES), f32)
    return pl.pallas_call(
        functools.partial(fused_kernel, zs),
        in_specs=[smem, smem, hbm, hbm, hbm, hbm, vmem, vmem, vmem, vmem],
        out_specs=hbm,
        out_shape=jax.ShapeDtypeStruct((tokens, n * feats), bf16),
        scratch_shapes=[
            pltpu.VMEM((2 * zs, 2 * feats, channels), bf16),
            pltpu.VMEM((3, tokens, channels), bf16),
            pltpu.VMEM((3, 16, channels), bf16),
            pltpu.VMEM((8, channels), f32),
            pltpu.VMEM((8, channels), f32),
            pltpu.VMEM((3, 8, channels), f32),
            pltpu.VMEM((tiles, tokens * GROUPS, LANES), f32),
            pltpu.VMEM((2 * tokens, channels), bf16),
            pltpu.VMEM((2 * zs, 2 * tokens, 2 * feats), bf16),
            table, table, table, table,
            pltpu.VMEM((tiles, 4, (modes + 2) * GROUPS, LANES), bf16),
            pltpu.VMEM((tiles, 2 + zs, (modes + 2) * GROUPS, LANES), bf16),
            pltpu.VMEM((tiles, (modes + 1) * GROUPS, LANES), f32),
            pltpu.VMEM((tiles, (modes + 1) * GROUPS, LANES), f32),
            pltpu.VMEM((tiles, modes * GROUPS, LANES), f32),
            dma((3, tiles)), dma((3,)), dma((2,)),
            dma((2 * zs, len(PARTS), 4)), dma((2, 2 * zs, len(PARTS))), dma,
            dma((tiles, 2 + zs)), dma((tiles, 2 + zs)), dma((2, tiles, 2)),
            dma((2 * zs,)), dma((2 * zs,)), dma((2 * zs,)),
        ],
        compiler_params=pltpu.CompilerParams(
            collective_id=0, has_side_effects=True, vmem_limit_bytes=58 * 2**20
        ),
        name="mixer",
    )(doc_starts, reset_flags, q_feat, k_feat, v_feat, out_weight, short_taps, decay_rate,
      residue, skip_gain.reshape(channels // LANES, LANES))


def local(q_feat, k_feat, v_feat, short_taps, decay_rate, residue, skip_gain, out_weight,
          doc_starts, reset_flags):
    tokens, channels = q_feat.shape
    modes = decay_rate.shape[0]
    kinds, taps = short_taps.shape[:2]
    n = lax.axis_size("seq")
    me = lax.axis_index("seq")
    tiles = channels // TILE
    heads = modes + 8

    weight = lax.all_gather(out_weight, "seq", axis=0, tiled=True)

    last_is_start = jnp.any(doc_starts[0] == tokens - 1)
    scale = jnp.stack([jnp.where(last_is_start, 0.0, 1.0), jnp.float32(1.0)]).astype(jnp.bfloat16)
    tails = jnp.stack([x[tokens - (taps - 1) :] for x in (q_feat, k_feat, v_feat)])
    tails = tails * scale[None, :, None]
    arrived = lax.ppermute(tails, "seq", [(i, i + 1) for i in range(n - 1)])
    rim = jnp.pad(arrived, ((0, 0), (ROWS - (taps - 1), 0), (0, 0)))

    rates = decay_rate.reshape(modes, channels // LANES, LANES)
    residues = residue.reshape(modes, channels // LANES, LANES)
    skips = skip_gain.reshape(channels // LANES, LANES)

    smem = pl.BlockSpec(memory_space=pltpu.SMEM)
    wide = pl.BlockSpec((tokens, TILE), lambda i: (0, i))
    deep = pl.BlockSpec((modes, GROUPS, LANES), lambda i: (0, i, 0))
    flat = pl.BlockSpec((None, tokens * GROUPS, LANES), lambda i: (i, 0, 0))
    f32 = jnp.float32
    qs, z, state = pl.pallas_call(
        local_kernel,
        grid=(tiles,),
        in_specs=[
            smem, smem, wide, wide, wide,
            pl.BlockSpec((kinds, ROWS, TILE), lambda i: (0, 0, i)),
            pl.BlockSpec((kinds * taps, TILE), lambda i: (0, i)),
            deep, deep,
            pl.BlockSpec((GROUPS, LANES), lambda i: (i, 0)),
        ],
        out_specs=[wide, flat, pl.BlockSpec((heads, GROUPS, LANES), lambda i: (0, i, 0))],
        out_shape=[
            jax.ShapeDtypeStruct((tokens, channels), jnp.bfloat16),
            jax.ShapeDtypeStruct((tiles, tokens * GROUPS, LANES), f32),
            jax.ShapeDtypeStruct((heads, channels // LANES, LANES), f32),
        ],
        scratch_shapes=[pltpu.VMEM((modes, GROUPS, LANES), f32)],
        cost_estimate=pl.CostEstimate(
            flops=tokens * channels * 80, bytes_accessed=tokens * channels * 12, transcendentals=0
        ),
        name="local_filter",
    )(doc_starts, reset_flags, q_feat, k_feat, v_feat, rim,
      short_taps.reshape(kinds * taps, channels), rates, residues, skips)

    part = channels // n
    sent = state.reshape(heads, n, part).transpose(1, 0, 2)
    pieces = lax.all_to_all(sent, "seq", 0, 0)
    my_rates = lax.dynamic_slice_in_dim(decay_rate, me * part, part, 1)
    chained = pl.pallas_call(
        functools.partial(scan_kernel, tokens),
        out_shape=jax.ShapeDtypeStruct((n, modes, part), f32),
        name="chain_states",
    )(pieces, my_rates)
    entering = lax.all_to_all(chained, "seq", 0, 0)
    entering = entering.transpose(1, 0, 2).reshape(modes, channels // LANES, LANES)

    mixed = pl.pallas_call(
        finish_kernel,
        grid=(tiles,),
        in_specs=[smem, smem, wide, flat, deep, deep, deep],
        out_specs=wide,
        out_shape=jax.ShapeDtypeStruct((tokens, channels), jnp.bfloat16),
        scratch_shapes=[
            pltpu.VMEM((modes, GROUPS, LANES), f32),
            pltpu.VMEM((tokens * GROUPS, LANES), f32),
        ],
        cost_estimate=pl.CostEstimate(
            flops=tokens * channels * 40, bytes_accessed=tokens * channels * 8, transcendentals=0
        ),
        name="finish_filter",
    )(doc_starts, reset_flags, qs, z, entering, rates, residues)

    projected = lax.dot_general(
        mixed, weight, (((1,), (1,)), ((), ())), preferred_element_type=f32
    ).astype(jnp.bfloat16)
    return lax.psum_scatter(projected, "ch", scatter_dimension=1, tiled=True)


def solution(mesh):
    placed = (
        P("seq", "ch"), P("seq", "ch"), P("seq", "ch"), P(None, None, "ch"), P(None, "ch"),
        P(None, "ch"), P("ch"), P("seq", "ch"), P("seq", None), P("seq", None),
    )
    direct = mesh.shape["ch"] == 1 and mesh.shape["seq"] in range(3 * PLANE, 2**16, PLANE)
    return jax.shard_map(
        fused if direct else local, mesh=mesh, in_specs=placed, out_specs=P("seq", "ch"), check_vma=False
    )
```

```python
import functools

import jax
import jax.numpy as jnp
from jax import lax
from jax.experimental import pallas as pl
from jax.experimental.pallas import tpu as pltpu
from jax.sharding import PartitionSpec as P

LANES = 128
GROUPS = 8
TILE = LANES * GROUPS
ROWS = 16
UNROLL = 8


def cut_of(starts, flags, tokens):
    cut = jnp.int32(tokens)
    for slot in range(starts.shape[1]):
        cut = jnp.where(flags[0, slot] == 1, jnp.minimum(cut, starts[0, slot]), cut)
    return cut


def local_kernel(starts, flags, q_ref, k_ref, v_ref, rim_ref, taps_ref, rate_ref, res_ref,
                 skip_ref, qs_ref, z_ref, state_ref, fac_ref):
    tokens = q_ref.shape[0]
    modes = rate_ref.shape[0]
    slots = starts.shape[1]
    cut = cut_of(starts, flags, tokens)

    def short_rows(step, carry):
        row = pl.multiple_of(step * ROWS, ROWS)
        back = pl.multiple_of(jnp.maximum(row - ROWS, 0), ROWS)
        at = lax.broadcasted_iota(jnp.int32, (ROWS, LANES), 0) + row
        hit = jnp.zeros((ROWS, LANES), jnp.bool_)
        hit_before = jnp.zeros((ROWS, LANES), jnp.bool_)
        for slot in range(slots):
            hit = hit | (at == starts[0, slot])
            hit_before = hit_before | (at - 1 == starts[0, slot])
        mask1 = jnp.where(hit, 0.0, 1.0)
        mask2 = jnp.where(hit | hit_before, 0.0, 1.0)
        first = step == 0
        for group in range(GROUPS):
            cols = slice(group * LANES, (group + 1) * LANES)

            def short(ref, index):
                x = ref[pl.ds(row, ROWS), cols].astype(jnp.float32)
                before = ref[pl.ds(back, ROWS), cols].astype(jnp.float32)
                rim = rim_ref[index, :, cols].astype(jnp.float32)
                before = jnp.where(first, rim, before)
                both = jnp.concatenate([before, x], axis=0)
                lag1 = pltpu.roll(both, 1, 0)[ROWS:]
                lag2 = pltpu.roll(both, 2, 0)[ROWS:]
                base = 3 * index
                summed = taps_ref[base : base + 1, cols] * x
                summed = summed + taps_ref[base + 1 : base + 2, cols] * mask1 * lag1
                summed = summed + taps_ref[base + 2 : base + 3, cols] * mask2 * lag2
                return summed.astype(jnp.bfloat16)

            qs_ref[pl.ds(row, ROWS), cols] = short(q_ref, 0)
            gated = short(k_ref, 1).astype(jnp.float32) * short(v_ref, 2).astype(jnp.float32)
            z_ref[pl.ds(row * GROUPS + group, ROWS, stride=GROUPS), :] = gated
        return carry

    lax.fori_loop(0, tokens // ROWS, short_rows, 0)

    fac_ref[...] = jnp.exp(-rate_ref[...])
    skip = skip_ref[...]

    def advance(step, states):
        states = list(states)
        for inner in range(UNROLL):
            time = step * UNROLL + inner
            spot = pl.ds(pl.multiple_of(time * GROUPS, GROUPS), GROUPS)
            keep = jnp.where(time == cut, 0.0, 1.0)
            x = z_ref[spot, :]
            sums = [skip * x, None]
            for n in range(modes):
                states[n] = (fac_ref[n] * keep) * states[n] + x
                term = res_ref[n] * states[n]
                sums[n % 2] = term if sums[n % 2] is None else sums[n % 2] + term
            z_ref[spot, :] = sums[0] + sums[1]
        return tuple(states)

    zero = jnp.zeros((GROUPS, LANES), jnp.float32)
    states = lax.fori_loop(0, tokens // UNROLL, advance, (zero,) * modes)
    for n in range(modes):
        state_ref[n] = states[n]
    through = jnp.where(cut < tokens, 0.0, 1.0)
    for n in range(modes, state_ref.shape[0]):
        state_ref[n] = zero + through


def scan_kernel(tokens, pieces_ref, rate_ref, out_ref):
    modes = rate_ref.shape[0]
    factor = jnp.exp(-float(tokens) * rate_ref[...])

    def hop(j, running):
        out_ref[j] = running
        piece = pieces_ref[j]
        return factor * piece[modes : modes + 1] * running + piece[:modes]

    lax.fori_loop(0, pieces_ref.shape[0], hop, jnp.zeros(rate_ref.shape, jnp.float32))


def finish_kernel(starts, flags, qs_ref, z_ref, enter_ref, rate_ref, res_ref, out_ref, fac_ref,
                  y_ref):
    tokens = qs_ref.shape[0]
    modes = rate_ref.shape[0]
    cut = cut_of(starts, flags, tokens)
    fac_ref[...] = jnp.exp(-rate_ref[...])

    def advance(step, weights):
        weights = list(weights)
        for inner in range(UNROLL):
            time = step * UNROLL + inner
            spot = pl.ds(pl.multiple_of(time * GROUPS, GROUPS), GROUPS)
            alive = jnp.where(time < cut, 1.0, 0.0)
            sums = [None, None]
            for n in range(modes):
                sums[n % 2] = weights[n] if sums[n % 2] is None else sums[n % 2] + weights[n]
                weights[n] = weights[n] * fac_ref[n]
            y_ref[spot, :] = z_ref[spot, :] + alive * (sums[0] + sums[1])
        return tuple(weights)

    begin = tuple(res_ref[n] * (fac_ref[n] * enter_ref[n]) for n in range(modes))
    lax.fori_loop(0, tokens // UNROLL, advance, begin)

    def mix_rows(step, carry):
        row = pl.multiple_of(step * ROWS, ROWS)
        for group in range(GROUPS):
            cols = slice(group * LANES, (group + 1) * LANES)
            y = y_ref[pl.ds(row * GROUPS + group, ROWS, stride=GROUPS), :]
            q = qs_ref[pl.ds(row, ROWS), cols].astype(jnp.float32)
            out_ref[pl.ds(row, ROWS), cols] = (q * y).astype(jnp.bfloat16)
        return carry

    lax.fori_loop(0, tokens // ROWS, mix_rows, 0)


PLANE = 8
RB = 32
PARTS = ((0, 64), (64, 48), (112, 16))
PIECE = 16


def fused_kernel(zs, starts, flags, q_hbm, k_hbm, v_hbm, w_hbm, taps_ref, rate_ref, res_ref,
                 skip_ref, out_hbm, wbuf, xin, tails, rim_out, rim_in, rimx, z_ref, acts, obuf,
                 fac_t, rate_t, span_t, res_t, csnd, crcv, tot, pre, ent, load_sem, tail_sem,
                 rim_sem, wsend, wrecv, own_sem, chain_send_sem, chain_recv_sem, act_sem,
                 out_send_sem, out_recv_sem, out_sem):
    _, tokens, channels = xin.shape
    modes = rate_ref.shape[0]
    slots = starts.shape[1]
    feats = w_hbm.shape[0]
    tiles = channels // TILE
    lane_groups = channels // LANES
    blocks = 2 * zs
    n = PLANE * zs
    f32 = jnp.float32

    me = lax.axis_index("seq")
    core = lax.rem(me, 2)
    x = lax.rem(me // 2, 2)
    y = lax.rem(me // 4, 2)
    z = me // PLANE
    sib = me + 1 - 2 * core
    x_peer = me + 2 - 4 * x
    y_peer = me + 4 - 8 * y
    up, down = me + PLANE, me - PLANE
    has_up, has_down = z < zs - 1, z > 0

    order = [sorted(range(zs), key=lambda s, at=at: (abs(s - at), s)) for at in range(zs)]

    def source(rank):
        at = jnp.int32(order[0][rank])
        for level in range(1, zs):
            at = jnp.where(z == level, order[level][rank], at)
        return at

    def remote(src, dst, send, recv, dev):
        return pltpu.make_async_remote_copy(
            src_ref=src, dst_ref=dst, send_sem=send, recv_sem=recv,
            device_id={"seq": dev}, device_id_type=pl.DeviceIdType.MESH,
        )

    def piece(block, side, part):
        first, rows = PARTS[part]
        row = pl.multiple_of(side * feats + first, 16)
        return wbuf.at[block, pl.ds(row, rows), :]

    def weight_copy(block, part, way, own):
        first, rows = PARTS[part]
        dst = piece(block, core, part)
        src = w_hbm.at[pl.ds(first, rows), :] if own else dst
        return remote(src, dst, wsend.at[block, part, way],
                      wrecv.at[1 if way == 3 else 0, block, part],
                      (up, down, y_peer, sib)[way])

    def wait_weight(block, part):
        first, rows = PARTS[part]
        dst = piece(block, core, part)
        remote(dst, dst, wsend.at[block, part, 0], wrecv.at[0, block, part], sib).wait_recv()

    def wait_sibling(block):
        for part in range(len(PARTS)):
            dst = piece(block, 1 - core, part)
            remote(dst, dst, wsend.at[block, part, 3], wrecv.at[1, block, part], sib).wait_recv()

    def forward(block, part, ways, own, done):
        for way, cond in ways:
            copy = weight_copy(block, part, way, own)
            act = copy.wait_send if done else copy.start
            if cond is None:
                act()
            else:
                pl.when(cond)(act)

    both = ((0, has_up), (1, has_down))
    here = z * 2 + y
    there = z * 2 + 1 - y
    last = len(PARTS) - 1

    def issue(part, first, count, ways):
        for index in range(first, first + count):
            row = PARTS[part][0] + index * PIECE
            spot = pl.ds(pl.multiple_of(core * feats + row, 16), PIECE)
            for way, cond in ways:
                copy = remote(w_hbm.at[pl.ds(row, PIECE), :], wbuf.at[here, spot, :],
                              wsend.at[here, part, way], wrecv.at[0, here, part],
                              (up, down, y_peer)[way])
                if cond is None:
                    copy.start()
                else:
                    pl.when(cond)(copy.start)

    across = ((2, None),)

    def finish_own():
        for part in range(last + 1):
            forward(here, part, both + ((2, None), (3, None)), True, True)

    def each_side(distance, act):
        pl.when(z >= distance)(lambda: act(z - distance, ((0, has_up),)))
        pl.when(z + distance < zs)(lambda: act(z + distance, ((1, has_down),)))

    def poll_line(distance, part, done=False, ways="yz"):
        def act(src, on_way):
            block = src * 2 + y
            if not done and "y" in ways:
                wait_weight(block, part)
            if "z" in ways:
                forward(block, part, on_way, False, done)
            if "y" in ways:
                forward(block, part, ((2, None), (3, None)), False, done)

        each_side(distance, act)

    def poll_across(rank, part, done=False):
        block = source(rank) * 2 + 1 - y
        if not done:
            wait_weight(block, part)
        forward(block, part, ((3, None),), False, done)

    def poll_last_across(done=False):
        if not done:
            wait_weight(there, last)
        forward(there, last, both + ((3, None),), False, done)

    def poll_last_line(distance, done=False):
        def act(src, on_way):
            for side in (y, 1 - y):
                block = src * 2 + side
                if not done:
                    wait_weight(block, last)
                forward(block, last, on_way + ((3, None),), False, done)

        each_side(distance, act)

    barrier = pltpu.get_barrier_semaphore()

    def greet(dev):
        pl.semaphore_signal(barrier, inc=1, device_id={"seq": dev},
                            device_id_type=pl.DeviceIdType.MESH)

    for dev in (sib, x_peer, y_peer):
        greet(dev)
    for gap in range(1, zs):
        pl.when(z + gap < zs)(lambda gap=gap: greet(me + gap * PLANE))
        pl.when(z >= gap)(lambda gap=gap: greet(me - gap * PLANE))
    pl.when(me < n - 1)(lambda: greet(me + 1))
    pl.when(me > 0)(lambda: greet(me - 1))

    feeds = (q_hbm, k_hbm, v_hbm)
    tail_copies = [
        pltpu.make_async_copy(feeds[i].at[pl.ds(tokens - 16, 16), :], tails.at[i], tail_sem.at[i])
        for i in range(3)
    ]
    for copy in tail_copies:
        copy.start()

    def load(index, tile):
        cols = pl.ds(tile * TILE, TILE)
        return pltpu.make_async_copy(feeds[index].at[:, cols], xin.at[index, :, cols],
                                     load_sem.at[index, tile])

    for index in (1, 2, 0):
        for tile in range(tiles):
            load(index, tile).start()
    own_copy = pltpu.make_async_copy(
        w_hbm, wbuf.at[here, pl.ds(pl.multiple_of(core * feats, 16), feats), :], own_sem)
    own_copy.start()

    cut = cut_of(starts, flags, tokens)
    through_me = jnp.where(cut < tokens, 0.0, 1.0)
    live = jnp.where(cut < tokens, cut, 0)
    final_start = jnp.float32(1.0)
    for slot in range(slots):
        final_start = jnp.where(starts[0, slot] == tokens - 1, 0.0, final_start)

    for copy in tail_copies:
        copy.wait()
    for index in range(3):
        two = tails[index, 8:16, :].astype(f32)
        rim_out[2 * index : 2 * index + 1, :] = two[6:7] * final_start
        rim_out[2 * index + 1 : 2 * index + 2, :] = two[7:8]
    rim_out[6:8, :] = jnp.zeros((2, channels), f32)
    rim_copy = remote(rim_out, rim_in, rim_sem.at[0], rim_sem.at[1], me + 1)

    pl.semaphore_wait(
        barrier, 3 + zs - 1 + jnp.where(me < n - 1, 1, 0) + jnp.where(me > 0, 1, 0))
    pl.when(me < n - 1)(rim_copy.start)
    issue(last, 0, 1, across)
    issue(0, 0, 2, across)
    issue(0, 0, 4, both)
    for part in range(last + 1):
        forward(here, part, ((3, None),), True, False)

    for half in range(modes // 8):
        for group in range(lane_groups):
            cols = slice(group * LANES, (group + 1) * LANES)
            tile, at = group // GROUPS, group % GROUPS
            spot = pl.ds((tile * modes + half * 8) * GROUPS + at, 8, stride=GROUPS)
            rate_t[spot, :] = rate_ref[half * 8 : half * 8 + 8, cols]
            res_t[spot, :] = res_ref[half * 8 : half * 8 + 8, cols]

    def fill_factors(step, carry):
        rows = pl.ds(pl.multiple_of(step * 32, 32), 32)
        fac_t[rows, :] = jnp.exp(-rate_t[rows, :])
        span_t[rows, :] = jnp.exp(-float(tokens) * rate_t[rows, :])
        return carry

    lax.fori_loop(0, modes * lane_groups // 32, fill_factors, 0)

    def table(ref, mode, tile):
        first = (tile * modes + mode) * GROUPS
        return ref[first : first + GROUPS, :]

    for plane in range(zs - 1):

        @pl.when(z <= plane)
        def _(plane=plane):
            for tile in range(tiles):
                crcv[tile, 3 + plane] = jnp.zeros(crcv.shape[2:], crcv.dtype)

    @pl.when(me == 0)
    def _():
        rim_in[...] = jnp.zeros(rim_in.shape, f32)

    def masks(row):
        at = lax.broadcasted_iota(jnp.int32, (RB, LANES), 0) + row
        hit = jnp.zeros((RB, LANES), jnp.bool_)
        hit_before = jnp.zeros((RB, LANES), jnp.bool_)
        for slot in range(slots):
            hit = hit | (at == starts[0, slot])
            hit_before = hit_before | (at - 1 == starts[0, slot])
        return jnp.where(hit, 0.0, 1.0), jnp.where(hit | hit_before, 0.0, 1.0)

    def short(index, row, cols, mask1, mask2, first):
        now = xin[index, pl.ds(row, RB), cols].astype(f32)
        if first:
            before = rimx[index, :, cols]
        else:
            before = xin[index, pl.ds(pl.multiple_of(row - 16, 16), 16), cols].astype(f32)[8:]
        joined = jnp.concatenate([before, now], axis=0)
        lag1 = pltpu.roll(joined, 1, 0)[8:]
        lag2 = pltpu.roll(joined, 2, 0)[8:]
        summed = taps_ref[index, 0:1, cols] * now
        summed = summed + taps_ref[index, 1:2, cols] * mask1 * lag1
        summed = summed + taps_ref[index, 2:3, cols] * mask2 * lag2
        return summed.astype(jnp.bfloat16)

    def gate_rows(tile, row, first):
        mask1, mask2 = masks(row)
        for group in range(GROUPS):
            cols = slice(tile * TILE + group * LANES, tile * TILE + (group + 1) * LANES)
            key = short(1, row, cols, mask1, mask2, first).astype(f32)
            value = short(2, row, cols, mask1, mask2, first).astype(f32)
            z_ref[tile, pl.ds(row * GROUPS + group, RB, stride=GROUPS), :] = key * value

    def gate(tile):
        load(1, tile).wait()
        load(2, tile).wait()

        def rows(step, carry):
            gate_rows(tile, pl.multiple_of(step * RB, RB), False)
            return carry

        lax.fori_loop(1, tokens // RB, rows, 0)

    def end_states(tile):
        zero = jnp.zeros((GROUPS, LANES), f32)

        def advance(step, states):
            states = list(states)
            for inner in range(UNROLL):
                time = step * UNROLL + inner
                spot = pl.ds(pl.multiple_of(time * GROUPS, GROUPS), GROUPS)
                item = z_ref[tile, spot, :] * jnp.where(time >= live, 1.0, 0.0)
                for mode in range(modes):
                    states[mode] = table(fac_t, mode, tile) * states[mode] + item
            return tuple(states)

        states = lax.fori_loop(0, tokens // UNROLL, advance, (zero,) * modes)
        for mode in range(modes):
            tot[tile, mode * GROUPS : (mode + 1) * GROUPS] = states[mode]
        tot[tile, deep:] = zero + through_me

    peers = (sib, x_peer, y_peer)
    bits = (core, x, y)
    deep = modes * GROUPS
    chunk = 4 * GROUPS

    def chain_copy(group, step):
        at = pl.ds(group[0], group[1])
        return remote(csnd.at[at, step], crcv.at[at, step], chain_send_sem.at[group[0], step],
                      chain_recv_sem.at[group[0], step], peers[step])

    def line_copy(group, gap, plane):
        at = pl.ds(group[0], group[1])
        return remote(csnd.at[at, 3], crcv.at[at, 3 + plane],
                      chain_send_sem.at[group[0], 2 + gap], chain_recv_sem.at[group[0], 3 + plane],
                      me + gap * PLANE)

    def members(group):
        return range(group[0], group[0] + group[1])

    def chain_post(group, step):
        for tile in members(group):
            csnd[tile, step, :deep] = tot[tile, :deep].astype(jnp.bfloat16)
            through = tot[tile, deep:]
            csnd[tile, step, deep:] = jnp.concatenate([through, through]).astype(jnp.bfloat16)
        if step < 3:
            chain_copy(group, step).start()
        else:
            for gap in range(1, zs):
                pl.when(z + gap < zs)(line_copy(group, gap, z).start)

    def message(tile, step, first, rows):
        return crcv[tile, step, first : first + rows].astype(f32)

    def spans(tile, first, doublings):
        found = [span_t[tile * deep + first : tile * deep + first + chunk]]
        for _ in range(doublings):
            found.append(found[-1] * found[-1])
        return found

    def before_me(found, step):
        product = None
        for bit in range(step):
            factor = jnp.where(bits[bit] == 1, found[bit], 1.0)
            product = factor if product is None else product * factor
        return product

    def chain_step(group, step):
        chain_copy(group, step).wait_recv()
        upper = bits[step] == 1
        for tile in members(group):
            through_mine = tot[tile, deep:]
            through_other = message(tile, step, deep, 16)[:GROUPS]
            through_late = jnp.where(upper, through_mine, through_other)[0:1]
            if step:
                through_pre = pre[tile, deep:]
            else:
                through_pre = jnp.ones((GROUPS, LANES), f32)
            for first in range(0, deep, chunk):
                rows = slice(first, first + chunk)
                found = spans(tile, first, step)
                mine = tot[tile, rows]
                other = message(tile, step, first, chunk)
                early = jnp.where(upper, other, mine)
                late = jnp.where(upper, mine, other)
                tot[tile, rows] = late + through_late * found[step] * early
                if step:
                    old = pre[tile, rows]
                    fade = through_pre[0:1] * before_me(found, step)
                    pre[tile, rows] = jnp.where(upper, old + fade * other, old)
                else:
                    pre[tile, rows] = jnp.where(upper, other, 0.0)
            tot[tile, deep:] = through_mine * through_other
            pre[tile, deep:] = jnp.where(upper, through_pre * through_other, through_pre)
        chain_post(group, step + 1)

    def chain_line(group):
        for plane in range(zs - 1):
            pl.when(plane < z)(line_copy(group, 1, plane).wait_recv)
        for tile in members(group):
            through_pre = pre[tile, deep : deep + 1]
            for first in range(0, deep, chunk):
                found = spans(tile, first, 3)
                entering = jnp.zeros((chunk, LANES), f32)
                for plane in range(zs - 1):
                    through = message(tile, 3 + plane, deep, 16)[0:1]
                    item = message(tile, 3 + plane, first, chunk)
                    entering = jnp.where(
                        plane < z, item + through * found[3] * entering, entering)
                ent[tile, first : first + chunk] = (
                    pre[tile, first : first + chunk]
                    + through_pre * before_me(found, 3) * entering)

    half = tokens // 2

    def act_copy(tile, part):
        cols = pl.ds(tile * TILE, TILE)
        return remote(acts.at[pl.ds(part * half, half), cols],
                      acts.at[pl.ds(tokens + part * half, half), cols],
                      act_sem.at[0, tile, part], act_sem.at[1, tile, part], x_peer)

    def queries(tile):
        load(0, tile).wait()

        def query_rows(row, first):
            mask1, mask2 = masks(row)
            for group in range(GROUPS):
                cols = slice(tile * TILE + group * LANES, tile * TILE + (group + 1) * LANES)
                acts[pl.ds(row, RB), cols] = short(0, row, cols, mask1, mask2, first)

        def rows(step, carry):
            query_rows(pl.multiple_of(step * RB, RB), False)
            return carry

        query_rows(0, True)
        lax.fori_loop(1, tokens // RB, rows, 0)

    def finish(tile, part):
        skip = skip_ref[tile * GROUPS : (tile + 1) * GROUPS, :]

        def advance(step, states):
            states = list(states)
            for inner in range(UNROLL):
                time = step * UNROLL + inner
                spot = pl.ds(pl.multiple_of(time * GROUPS, GROUPS), GROUPS)
                keep = jnp.where(time == cut, 0.0, 1.0)
                item = z_ref[tile, spot, :]
                sums = [skip * item, None]
                for mode in range(modes):
                    states[mode] = (table(fac_t, mode, tile) * keep) * states[mode] + item
                    term = table(res_t, mode, tile) * states[mode]
                    sums[mode % 2] = term if sums[mode % 2] is None else sums[mode % 2] + term
                z_ref[tile, spot, :] = sums[0] + sums[1]
            return tuple(states)

        def mix(step, carry):
            row = pl.multiple_of(step * RB, RB)
            for group in range(GROUPS):
                cols = slice(tile * TILE + group * LANES, tile * TILE + (group + 1) * LANES)
                mixed = z_ref[tile, pl.ds(row * GROUPS + group, RB, stride=GROUPS), :]
                query = acts[pl.ds(row, RB), cols].astype(f32)
                acts[pl.ds(row, RB), cols] = (query * mixed).astype(jnp.bfloat16)
            return carry

        spots = [slice(mode * GROUPS, (mode + 1) * GROUPS) for mode in range(modes)]
        states = tuple(ent[tile, spot] for spot in spots)
        steps = half // UNROLL
        states = lax.fori_loop(part * steps, (part + 1) * steps, advance, states)
        for spot, state in zip(spots, states):
            ent[tile, spot] = state
        steps = half // RB
        lax.fori_loop(part * steps, (part + 1) * steps, mix, 0)
        act_copy(tile, part).start()

    def columns(block, plane):
        return pl.ds(pl.multiple_of((block * 2 + plane) * 2 * feats, LANES), 2 * feats)

    def out_copy(block):
        return remote(obuf.at[block, pl.ds(tokens, tokens), :], out_hbm.at[:, columns(block, x)],
                      out_send_sem.at[block], out_recv_sem.at[block], x_peer)

    def own_out(block):
        return pltpu.make_async_copy(obuf.at[block, pl.ds(0, tokens), :],
                                     out_hbm.at[:, columns(block, x)], out_sem.at[block])

    def project_rows(block, first):
        rows = slice(first, first + tokens)
        obuf[block, rows] = lax.dot_general(
            acts[rows], wbuf[block], (((1,), (1,)), ((), ())), preferred_element_type=f32
        ).astype(jnp.bfloat16)

    def project_own(block):
        project_rows(block, 0)
        own_out(block).start()

    def project_other(block):
        project_rows(block, tokens)
        out_copy(block).start()

    def project(block):
        wait_sibling(block)
        project_other(block)

    one, two, rest = (0, 1), (1, 1), (2, tiles - 2)
    gate(0)
    gate(1)
    pl.when(me > 0)(rim_copy.wait_recv)
    for index in range(3):
        rimx[index] = jnp.zeros((8, channels), f32)
        rimx[index, 6:8, :] = rim_in[2 * index : 2 * index + 2, :]
    gate_rows(0, 0, True)
    end_states(0)
    chain_post(one, 0)
    gate_rows(1, 0, True)
    end_states(1)
    chain_step(one, 0)
    chain_post(two, 0)
    gate(2)
    gate_rows(2, 0, True)
    chain_step(two, 0)
    end_states(2)
    chain_step(one, 1)
    issue(0, 2, 1, across)
    for tile in range(3, tiles):
        gate(tile)
        gate_rows(tile, 0, True)
    chain_step(two, 1)
    issue(0, 3, 1, across)
    issue(1, 0, 1, across)
    for tile in range(3, tiles):
        end_states(tile)
    chain_step(one, 2)
    issue(1, 0, 2, both)
    chain_post(rest, 0)
    queries(0)
    chain_step(two, 2)
    issue(1, 2, 1, both)
    chain_step(rest, 0)
    issue(1, 1, 1, across)
    issue(last, 0, 1, both)
    poll_last_across()
    chain_line(one)
    finish(0, 0)
    queries(1)
    chain_step(rest, 1)
    issue(1, 2, 1, across)
    poll_line(1, 0, ways="y")
    finish(0, 1)
    poll_across(0, 0)
    chain_line(two)
    finish(1, 0)
    chain_step(rest, 2)
    poll_line(1, 0, ways="z")
    poll_line(1, 1)
    finish(1, 1)
    queries(2)
    queries(3)
    chain_line(rest)
    for tile in range(2, tiles):
        finish(tile, 0)
        finish(tile, 1)
    poll_across(0, 1)
    own_copy.wait()
    for distance in range(2, zs - 1):
        poll_line(distance, 0)
        for side in (0, 1):
            block = source(0) * 2 + (y if side == 0 else 1 - y)
            wait_sibling(block)
            project_own(block)
        poll_line(distance, 1)
    poll_last_line(1)
    poll_across(1, 0)
    poll_line(zs - 1, 0)
    for tile in range(tiles):
        for part in range(2):
            act_copy(tile, part).wait_recv()
    project_other(source(0) * 2 + y)
    project_other(source(0) * 2 + 1 - y)
    poll_line(zs - 1, 1)
    project(source(1) * 2 + y)
    poll_across(1, 1)
    project(source(1) * 2 + 1 - y)
    for rank in range(2, zs):
        poll_last_line(rank)
        project(source(rank) * 2 + y)
        for part in range(last):
            poll_across(rank, part)
        project(source(rank) * 2 + 1 - y)

    for rank in range(1, zs):
        project_own(source(rank) * 2 + y)
        project_own(source(rank) * 2 + 1 - y)

    finish_own()
    for distance in range(1, zs):
        for part in range(last):
            poll_line(distance, part, True)
        poll_last_line(distance, True)
    for distance in range(zs):
        for part in range(last):
            poll_across(distance, part, True)
    poll_last_across(True)
    pl.when(me < n - 1)(rim_copy.wait_send)
    for group in (one, two, rest):
        for step in range(3):
            chain_copy(group, step).wait_send()
        for gap in range(1, zs):
            pl.when(z + gap < zs)(line_copy(group, gap, z).wait_send)
    for tile in range(tiles):
        for part in range(2):
            act_copy(tile, part).wait_send()
    for block in range(blocks):
        own_out(block).wait()
        out_copy(block).wait()


def fused(q_feat, k_feat, v_feat, short_taps, decay_rate, residue, skip_gain, out_weight,
          doc_starts, reset_flags):
    tokens, channels = q_feat.shape
    modes = decay_rate.shape[0]
    n = lax.axis_size("seq")
    zs = n // PLANE
    tiles = channels // TILE
    feats = out_weight.shape[0]
    f32, bf16 = jnp.float32, jnp.bfloat16
    vmem = pl.BlockSpec(memory_space=pltpu.VMEM)
    smem = pl.BlockSpec(memory_space=pltpu.SMEM)
    hbm = pl.BlockSpec(memory_space=pl.ANY)
    dma = pltpu.SemaphoreType.DMA
    table = pltpu.VMEM((modes * channels // LANES, LANES), f32)
    return pl.pallas_call(
        functools.partial(fused_kernel, zs),
        in_specs=[smem, smem, hbm, hbm, hbm, hbm, vmem, vmem, vmem, vmem],
        out_specs=hbm,
        out_shape=jax.ShapeDtypeStruct((tokens, n * feats), bf16),
        scratch_shapes=[
            pltpu.VMEM((2 * zs, 2 * feats, channels), bf16),
            pltpu.VMEM((3, tokens, channels), bf16),
            pltpu.VMEM((3, 16, channels), bf16),
            pltpu.VMEM((8, channels), f32),
            pltpu.VMEM((8, channels), f32),
            pltpu.VMEM((3, 8, channels), f32),
            pltpu.VMEM((tiles, tokens * GROUPS, LANES), f32),
            pltpu.VMEM((2 * tokens, channels), bf16),
            pltpu.VMEM((2 * zs, 2 * tokens, 2 * feats), bf16),
            table, table, table, table,
            pltpu.VMEM((tiles, 4, (modes + 2) * GROUPS, LANES), bf16),
            pltpu.VMEM((tiles, 2 + zs, (modes + 2) * GROUPS, LANES), bf16),
            pltpu.VMEM((tiles, (modes + 1) * GROUPS, LANES), f32),
            pltpu.VMEM((tiles, (modes + 1) * GROUPS, LANES), f32),
            pltpu.VMEM((tiles, modes * GROUPS, LANES), f32),
            dma((3, tiles)), dma((3,)), dma((2,)),
            dma((2 * zs, len(PARTS), 4)), dma((2, 2 * zs, len(PARTS))), dma,
            dma((tiles, 2 + zs)), dma((tiles, 2 + zs)), dma((2, tiles, 2)),
            dma((2 * zs,)), dma((2 * zs,)), dma((2 * zs,)),
        ],
        compiler_params=pltpu.CompilerParams(
            collective_id=0, has_side_effects=True, vmem_limit_bytes=58 * 2**20
        ),
        name="mixer",
    )(doc_starts, reset_flags, q_feat, k_feat, v_feat, out_weight, short_taps, decay_rate,
      residue, skip_gain.reshape(channels // LANES, LANES))


def local(q_feat, k_feat, v_feat, short_taps, decay_rate, residue, skip_gain, out_weight,
          doc_starts, reset_flags):
    tokens, channels = q_feat.shape
    modes = decay_rate.shape[0]
    kinds, taps = short_taps.shape[:2]
    n = lax.axis_size("seq")
    me = lax.axis_index("seq")
    tiles = channels // TILE
    heads = modes + 8

    weight = lax.all_gather(out_weight, "seq", axis=0, tiled=True)

    last_is_start = jnp.any(doc_starts[0] == tokens - 1)
    scale = jnp.stack([jnp.where(last_is_start, 0.0, 1.0), jnp.float32(1.0)]).astype(jnp.bfloat16)
    tails = jnp.stack([x[tokens - (taps - 1) :] for x in (q_feat, k_feat, v_feat)])
    tails = tails * scale[None, :, None]
    arrived = lax.ppermute(tails, "seq", [(i, i + 1) for i in range(n - 1)])
    rim = jnp.pad(arrived, ((0, 0), (ROWS - (taps - 1), 0), (0, 0)))

    rates = decay_rate.reshape(modes, channels // LANES, LANES)
    residues = residue.reshape(modes, channels // LANES, LANES)
    skips = skip_gain.reshape(channels // LANES, LANES)

    smem = pl.BlockSpec(memory_space=pltpu.SMEM)
    wide = pl.BlockSpec((tokens, TILE), lambda i: (0, i))
    deep = pl.BlockSpec((modes, GROUPS, LANES), lambda i: (0, i, 0))
    flat = pl.BlockSpec((None, tokens * GROUPS, LANES), lambda i: (i, 0, 0))
    f32 = jnp.float32
    qs, z, state = pl.pallas_call(
        local_kernel,
        grid=(tiles,),
        in_specs=[
            smem, smem, wide, wide, wide,
            pl.BlockSpec((kinds, ROWS, TILE), lambda i: (0, 0, i)),
            pl.BlockSpec((kinds * taps, TILE), lambda i: (0, i)),
            deep, deep,
            pl.BlockSpec((GROUPS, LANES), lambda i: (i, 0)),
        ],
        out_specs=[wide, flat, pl.BlockSpec((heads, GROUPS, LANES), lambda i: (0, i, 0))],
        out_shape=[
            jax.ShapeDtypeStruct((tokens, channels), jnp.bfloat16),
            jax.ShapeDtypeStruct((tiles, tokens * GROUPS, LANES), f32),
            jax.ShapeDtypeStruct((heads, channels // LANES, LANES), f32),
        ],
        scratch_shapes=[pltpu.VMEM((modes, GROUPS, LANES), f32)],
        cost_estimate=pl.CostEstimate(
            flops=tokens * channels * 80, bytes_accessed=tokens * channels * 12, transcendentals=0
        ),
        name="local_filter",
    )(doc_starts, reset_flags, q_feat, k_feat, v_feat, rim,
      short_taps.reshape(kinds * taps, channels), rates, residues, skips)

    part = channels // n
    sent = state.reshape(heads, n, part).transpose(1, 0, 2)
    pieces = lax.all_to_all(sent, "seq", 0, 0)
    my_rates = lax.dynamic_slice_in_dim(decay_rate, me * part, part, 1)
    chained = pl.pallas_call(
        functools.partial(scan_kernel, tokens),
        out_shape=jax.ShapeDtypeStruct((n, modes, part), f32),
        name="chain_states",
    )(pieces, my_rates)
    entering = lax.all_to_all(chained, "seq", 0, 0)
    entering = entering.transpose(1, 0, 2).reshape(modes, channels // LANES, LANES)

    mixed = pl.pallas_call(
        finish_kernel,
        grid=(tiles,),
        in_specs=[smem, smem, wide, flat, deep, deep, deep],
        out_specs=wide,
        out_shape=jax.ShapeDtypeStruct((tokens, channels), jnp.bfloat16),
        scratch_shapes=[
            pltpu.VMEM((modes, GROUPS, LANES), f32),
            pltpu.VMEM((tokens * GROUPS, LANES), f32),
        ],
        cost_estimate=pl.CostEstimate(
            flops=tokens * channels * 40, bytes_accessed=tokens * channels * 8, transcendentals=0
        ),
        name="finish_filter",
    )(doc_starts, reset_flags, qs, z, entering, rates, residues)

    projected = lax.dot_general(
        mixed, weight, (((1,), (1,)), ((), ())), preferred_element_type=f32
    ).astype(jnp.bfloat16)
    return lax.psum_scatter(projected, "ch", scatter_dimension=1, tiled=True)


def solution(mesh):
    placed = (
        P("seq", "ch"), P("seq", "ch"), P("seq", "ch"), P(None, None, "ch"), P(None, "ch"),
        P(None, "ch"), P("ch"), P("seq", "ch"), P("seq", None), P("seq", None),
    )
    direct = mesh.shape["ch"] == 1 and mesh.shape["seq"] in range(3 * PLANE, 2**16, PLANE)
    return jax.shard_map(
        fused if direct else local, mesh=mesh, in_specs=placed, out_specs=P("seq", "ch"), check_vma=False
    )
```

```python
import functools

import jax
import jax.numpy as jnp
from jax import lax
from jax.experimental import pallas as pl
from jax.experimental.pallas import tpu as pltpu
from jax.sharding import PartitionSpec as P

LANES = 128
GROUPS = 8
TILE = LANES * GROUPS
ROWS = 16
UNROLL = 8


def cut_of(starts, flags, tokens):
    cut = jnp.int32(tokens)
    for slot in range(starts.shape[1]):
        cut = jnp.where(flags[0, slot] == 1, jnp.minimum(cut, starts[0, slot]), cut)
    return cut


def local_kernel(starts, flags, q_ref, k_ref, v_ref, rim_ref, taps_ref, rate_ref, res_ref,
                 skip_ref, qs_ref, z_ref, state_ref, fac_ref):
    tokens = q_ref.shape[0]
    modes = rate_ref.shape[0]
    slots = starts.shape[1]
    cut = cut_of(starts, flags, tokens)

    def short_rows(step, carry):
        row = pl.multiple_of(step * ROWS, ROWS)
        back = pl.multiple_of(jnp.maximum(row - ROWS, 0), ROWS)
        at = lax.broadcasted_iota(jnp.int32, (ROWS, LANES), 0) + row
        hit = jnp.zeros((ROWS, LANES), jnp.bool_)
        hit_before = jnp.zeros((ROWS, LANES), jnp.bool_)
        for slot in range(slots):
            hit = hit | (at == starts[0, slot])
            hit_before = hit_before | (at - 1 == starts[0, slot])
        mask1 = jnp.where(hit, 0.0, 1.0)
        mask2 = jnp.where(hit | hit_before, 0.0, 1.0)
        first = step == 0
        for group in range(GROUPS):
            cols = slice(group * LANES, (group + 1) * LANES)

            def short(ref, index):
                x = ref[pl.ds(row, ROWS), cols].astype(jnp.float32)
                before = ref[pl.ds(back, ROWS), cols].astype(jnp.float32)
                rim = rim_ref[index, :, cols].astype(jnp.float32)
                before = jnp.where(first, rim, before)
                both = jnp.concatenate([before, x], axis=0)
                lag1 = pltpu.roll(both, 1, 0)[ROWS:]
                lag2 = pltpu.roll(both, 2, 0)[ROWS:]
                base = 3 * index
                summed = taps_ref[base : base + 1, cols] * x
                summed = summed + taps_ref[base + 1 : base + 2, cols] * mask1 * lag1
                summed = summed + taps_ref[base + 2 : base + 3, cols] * mask2 * lag2
                return summed.astype(jnp.bfloat16)

            qs_ref[pl.ds(row, ROWS), cols] = short(q_ref, 0)
            gated = short(k_ref, 1).astype(jnp.float32) * short(v_ref, 2).astype(jnp.float32)
            z_ref[pl.ds(row * GROUPS + group, ROWS, stride=GROUPS), :] = gated
        return carry

    lax.fori_loop(0, tokens // ROWS, short_rows, 0)

    fac_ref[...] = jnp.exp(-rate_ref[...])
    skip = skip_ref[...]

    def advance(step, states):
        states = list(states)
        for inner in range(UNROLL):
            time = step * UNROLL + inner
            spot = pl.ds(pl.multiple_of(time * GROUPS, GROUPS), GROUPS)
            keep = jnp.where(time == cut, 0.0, 1.0)
            x = z_ref[spot, :]
            sums = [skip * x, None]
            for n in range(modes):
                states[n] = (fac_ref[n] * keep) * states[n] + x
                term = res_ref[n] * states[n]
                sums[n % 2] = term if sums[n % 2] is None else sums[n % 2] + term
            z_ref[spot, :] = sums[0] + sums[1]
        return tuple(states)

    zero = jnp.zeros((GROUPS, LANES), jnp.float32)
    states = lax.fori_loop(0, tokens // UNROLL, advance, (zero,) * modes)
    for n in range(modes):
        state_ref[n] = states[n]
    through = jnp.where(cut < tokens, 0.0, 1.0)
    for n in range(modes, state_ref.shape[0]):
        state_ref[n] = zero + through


def scan_kernel(tokens, pieces_ref, rate_ref, out_ref):
    modes = rate_ref.shape[0]
    factor = jnp.exp(-float(tokens) * rate_ref[...])

    def hop(j, running):
        out_ref[j] = running
        piece = pieces_ref[j]
        return factor * piece[modes : modes + 1] * running + piece[:modes]

    lax.fori_loop(0, pieces_ref.shape[0], hop, jnp.zeros(rate_ref.shape, jnp.float32))


def finish_kernel(starts, flags, qs_ref, z_ref, enter_ref, rate_ref, res_ref, out_ref, fac_ref,
                  y_ref):
    tokens = qs_ref.shape[0]
    modes = rate_ref.shape[0]
    cut = cut_of(starts, flags, tokens)
    fac_ref[...] = jnp.exp(-rate_ref[...])

    def advance(step, weights):
        weights = list(weights)
        for inner in range(UNROLL):
            time = step * UNROLL + inner
            spot = pl.ds(pl.multiple_of(time * GROUPS, GROUPS), GROUPS)
            alive = jnp.where(time < cut, 1.0, 0.0)
            sums = [None, None]
            for n in range(modes):
                sums[n % 2] = weights[n] if sums[n % 2] is None else sums[n % 2] + weights[n]
                weights[n] = weights[n] * fac_ref[n]
            y_ref[spot, :] = z_ref[spot, :] + alive * (sums[0] + sums[1])
        return tuple(weights)

    begin = tuple(res_ref[n] * (fac_ref[n] * enter_ref[n]) for n in range(modes))
    lax.fori_loop(0, tokens // UNROLL, advance, begin)

    def mix_rows(step, carry):
        row = pl.multiple_of(step * ROWS, ROWS)
        for group in range(GROUPS):
            cols = slice(group * LANES, (group + 1) * LANES)
            y = y_ref[pl.ds(row * GROUPS + group, ROWS, stride=GROUPS), :]
            q = qs_ref[pl.ds(row, ROWS), cols].astype(jnp.float32)
            out_ref[pl.ds(row, ROWS), cols] = (q * y).astype(jnp.bfloat16)
        return carry

    lax.fori_loop(0, tokens // ROWS, mix_rows, 0)


PLANE = 8
RB = 32
PARTS = ((0, 64), (64, 48), (112, 16))
PIECE = 16


def fused_kernel(zs, starts, flags, q_hbm, k_hbm, v_hbm, w_hbm, taps_ref, rate_ref, res_ref,
                 skip_ref, out_hbm, wbuf, xin, tails, rim_out, rim_in, rimx, z_ref, acts, obuf,
                 fac_t, rate_t, span_t, res_t, csnd, crcv, tot, pre, ent, load_sem, tail_sem,
                 rim_sem, wsend, wrecv, own_sem, chain_send_sem, chain_recv_sem, act_sem,
                 out_send_sem, out_recv_sem, out_sem):
    _, tokens, channels = xin.shape
    modes = rate_ref.shape[0]
    slots = starts.shape[1]
    feats = w_hbm.shape[0]
    tiles = channels // TILE
    lane_groups = channels // LANES
    blocks = 2 * zs
    n = PLANE * zs
    f32 = jnp.float32

    me = lax.axis_index("seq")
    core = lax.rem(me, 2)
    x = lax.rem(me // 2, 2)
    y = lax.rem(me // 4, 2)
    z = me // PLANE
    sib = me + 1 - 2 * core
    x_peer = me + 2 - 4 * x
    y_peer = me + 4 - 8 * y
    up, down = me + PLANE, me - PLANE
    has_up, has_down = z < zs - 1, z > 0

    order = [sorted(range(zs), key=lambda s, at=at: (abs(s - at), s)) for at in range(zs)]

    def source(rank):
        at = jnp.int32(order[0][rank])
        for level in range(1, zs):
            at = jnp.where(z == level, order[level][rank], at)
        return at

    def remote(src, dst, send, recv, dev):
        return pltpu.make_async_remote_copy(
            src_ref=src, dst_ref=dst, send_sem=send, recv_sem=recv,
            device_id={"seq": dev}, device_id_type=pl.DeviceIdType.MESH,
        )

    def piece(block, side, part):
        first, rows = PARTS[part]
        row = pl.multiple_of(side * feats + first, 16)
        return wbuf.at[block, pl.ds(row, rows), :]

    def weight_copy(block, part, way, own):
        first, rows = PARTS[part]
        dst = piece(block, core, part)
        src = w_hbm.at[pl.ds(first, rows), :] if own else dst
        return remote(src, dst, wsend.at[block, part, way],
                      wrecv.at[1 if way == 3 else 0, block, part],
                      (up, down, y_peer, sib)[way])

    def wait_weight(block, part):
        first, rows = PARTS[part]
        dst = piece(block, core, part)
        remote(dst, dst, wsend.at[block, part, 0], wrecv.at[0, block, part], sib).wait_recv()

    def wait_sibling(block):
        for part in range(len(PARTS)):
            dst = piece(block, 1 - core, part)
            remote(dst, dst, wsend.at[block, part, 3], wrecv.at[1, block, part], sib).wait_recv()

    def forward(block, part, ways, own, done):
        for way, cond in ways:
            copy = weight_copy(block, part, way, own)
            act = copy.wait_send if done else copy.start
            if cond is None:
                act()
            else:
                pl.when(cond)(act)

    both = ((0, has_up), (1, has_down))
    here = z * 2 + y
    there = z * 2 + 1 - y
    last = len(PARTS) - 1

    def issue(part, first, count, ways):
        for index in range(first, first + count):
            row = PARTS[part][0] + index * PIECE
            spot = pl.ds(pl.multiple_of(core * feats + row, 16), PIECE)
            for way, cond in ways:
                copy = remote(w_hbm.at[pl.ds(row, PIECE), :], wbuf.at[here, spot, :],
                              wsend.at[here, part, way], wrecv.at[0, here, part],
                              (up, down, y_peer)[way])
                if cond is None:
                    copy.start()
                else:
                    pl.when(cond)(copy.start)

    across = ((2, None),)

    def finish_own():
        for part in range(last + 1):
            forward(here, part, both + ((2, None), (3, None)), True, True)

    def each_side(distance, act):
        pl.when(z >= distance)(lambda: act(z - distance, ((0, has_up),)))
        pl.when(z + distance < zs)(lambda: act(z + distance, ((1, has_down),)))

    def poll_line(distance, part, done=False, ways="yz"):
        def act(src, on_way):
            block = src * 2 + y
            if not done and "y" in ways:
                wait_weight(block, part)
            if "z" in ways:
                forward(block, part, on_way, False, done)
            if "y" in ways:
                forward(block, part, ((2, None), (3, None)), False, done)

        each_side(distance, act)

    def poll_across(rank, part, done=False):
        block = source(rank) * 2 + 1 - y
        if not done:
            wait_weight(block, part)
        forward(block, part, ((3, None),), False, done)

    def poll_last_across(done=False):
        if not done:
            wait_weight(there, last)
        forward(there, last, both + ((3, None),), False, done)

    def poll_last_line(distance, done=False):
        def act(src, on_way):
            for side in (y, 1 - y):
                block = src * 2 + side
                if not done:
                    wait_weight(block, last)
                forward(block, last, on_way + ((3, None),), False, done)

        each_side(distance, act)

    barrier = pltpu.get_barrier_semaphore()

    def greet(dev):
        pl.semaphore_signal(barrier, inc=1, device_id={"seq": dev},
                            device_id_type=pl.DeviceIdType.MESH)

    for dev in (sib, x_peer, y_peer):
        greet(dev)
    for gap in range(1, zs):
        pl.when(z + gap < zs)(lambda gap=gap: greet(me + gap * PLANE))
        pl.when(z >= gap)(lambda gap=gap: greet(me - gap * PLANE))
    pl.when(me < n - 1)(lambda: greet(me + 1))
    pl.when(me > 0)(lambda: greet(me - 1))

    feeds = (q_hbm, k_hbm, v_hbm)
    tail_copies = [
        pltpu.make_async_copy(feeds[i].at[pl.ds(tokens - 16, 16), :], tails.at[i], tail_sem.at[i])
        for i in range(3)
    ]
    for copy in tail_copies:
        copy.start()

    def load(index, tile):
        cols = pl.ds(tile * TILE, TILE)
        return pltpu.make_async_copy(feeds[index].at[:, cols], xin.at[index, :, cols],
                                     load_sem.at[index, tile])

    for index in (1, 2, 0):
        for tile in range(tiles):
            load(index, tile).start()
    own_copy = pltpu.make_async_copy(
        w_hbm, wbuf.at[here, pl.ds(pl.multiple_of(core * feats, 16), feats), :], own_sem)
    own_copy.start()

    cut = cut_of(starts, flags, tokens)
    through_me = jnp.where(cut < tokens, 0.0, 1.0)
    live = jnp.where(cut < tokens, cut, 0)
    final_start = jnp.float32(1.0)
    for slot in range(slots):
        final_start = jnp.where(starts[0, slot] == tokens - 1, 0.0, final_start)

    for copy in tail_copies:
        copy.wait()
    for index in range(3):
        two = tails[index, 8:16, :].astype(f32)
        rim_out[2 * index : 2 * index + 1, :] = two[6:7] * final_start
        rim_out[2 * index + 1 : 2 * index + 2, :] = two[7:8]
    rim_out[6:8, :] = jnp.zeros((2, channels), f32)
    rim_copy = remote(rim_out, rim_in, rim_sem.at[0], rim_sem.at[1], me + 1)

    pl.semaphore_wait(
        barrier, 3 + zs - 1 + jnp.where(me < n - 1, 1, 0) + jnp.where(me > 0, 1, 0))
    pl.when(me < n - 1)(rim_copy.start)
    issue(last, 0, 1, across)
    issue(0, 0, 2, across)
    issue(0, 0, 4, both)
    for part in range(last + 1):
        forward(here, part, ((3, None),), True, False)

    for half in range(modes // 8):
        for group in range(lane_groups):
            cols = slice(group * LANES, (group + 1) * LANES)
            tile, at = group // GROUPS, group % GROUPS
            spot = pl.ds((tile * modes + half * 8) * GROUPS + at, 8, stride=GROUPS)
            rate_t[spot, :] = rate_ref[half * 8 : half * 8 + 8, cols]
            res_t[spot, :] = res_ref[half * 8 : half * 8 + 8, cols]

    def fill_factors(step, carry):
        rows = pl.ds(pl.multiple_of(step * 32, 32), 32)
        fac_t[rows, :] = jnp.exp(-rate_t[rows, :])
        span_t[rows, :] = jnp.exp(-float(tokens) * rate_t[rows, :])
        return carry

    lax.fori_loop(0, modes * lane_groups // 32, fill_factors, 0)

    def table(ref, mode, tile):
        first = (tile * modes + mode) * GROUPS
        return ref[first : first + GROUPS, :]

    for plane in range(zs - 1):

        @pl.when(z <= plane)
        def _(plane=plane):
            for tile in range(tiles):
                crcv[tile, 3 + plane] = jnp.zeros(crcv.shape[2:], crcv.dtype)

    @pl.when(me == 0)
    def _():
        rim_in[...] = jnp.zeros(rim_in.shape, f32)

    def masks(row):
        at = lax.broadcasted_iota(jnp.int32, (RB, LANES), 0) + row
        hit = jnp.zeros((RB, LANES), jnp.bool_)
        hit_before = jnp.zeros((RB, LANES), jnp.bool_)
        for slot in range(slots):
            hit = hit | (at == starts[0, slot])
            hit_before = hit_before | (at - 1 == starts[0, slot])
        return jnp.where(hit, 0.0, 1.0), jnp.where(hit | hit_before, 0.0, 1.0)

    def short(index, row, cols, mask1, mask2, first):
        now = xin[index, pl.ds(row, RB), cols].astype(f32)
        if first:
            before = rimx[index, :, cols]
        else:
            before = xin[index, pl.ds(pl.multiple_of(row - 16, 16), 16), cols].astype(f32)[8:]
        joined = jnp.concatenate([before, now], axis=0)
        lag1 = pltpu.roll(joined, 1, 0)[8:]
        lag2 = pltpu.roll(joined, 2, 0)[8:]
        summed = taps_ref[index, 0:1, cols] * now
        summed = summed + taps_ref[index, 1:2, cols] * mask1 * lag1
        summed = summed + taps_ref[index, 2:3, cols] * mask2 * lag2
        return summed.astype(jnp.bfloat16)

    def gate_rows(tile, row, first):
        mask1, mask2 = masks(row)
        for group in range(GROUPS):
            cols = slice(tile * TILE + group * LANES, tile * TILE + (group + 1) * LANES)
            key = short(1, row, cols, mask1, mask2, first).astype(f32)
            value = short(2, row, cols, mask1, mask2, first).astype(f32)
            z_ref[tile, pl.ds(row * GROUPS + group, RB, stride=GROUPS), :] = key * value

    def gate(tile):
        load(1, tile).wait()
        load(2, tile).wait()

        def rows(step, carry):
            gate_rows(tile, pl.multiple_of(step * RB, RB), False)
            return carry

        lax.fori_loop(1, tokens // RB, rows, 0)

    def end_states(tile):
        zero = jnp.zeros((GROUPS, LANES), f32)

        def advance(step, states):
            states = list(states)
            for inner in range(UNROLL):
                time = step * UNROLL + inner
                spot = pl.ds(pl.multiple_of(time * GROUPS, GROUPS), GROUPS)
                item = z_ref[tile, spot, :] * jnp.where(time >= live, 1.0, 0.0)
                for mode in range(modes):
                    states[mode] = table(fac_t, mode, tile) * states[mode] + item
            return tuple(states)

        states = lax.fori_loop(0, tokens // UNROLL, advance, (zero,) * modes)
        for mode in range(modes):
            tot[tile, mode * GROUPS : (mode + 1) * GROUPS] = states[mode]
        tot[tile, deep:] = zero + through_me

    peers = (sib, x_peer, y_peer)
    bits = (core, x, y)
    deep = modes * GROUPS
    chunk = 4 * GROUPS

    def chain_copy(group, step):
        at = pl.ds(group[0], group[1])
        return remote(csnd.at[at, step], crcv.at[at, step], chain_send_sem.at[group[0], step],
                      chain_recv_sem.at[group[0], step], peers[step])

    def line_copy(group, gap, plane):
        at = pl.ds(group[0], group[1])
        return remote(csnd.at[at, 3], crcv.at[at, 3 + plane],
                      chain_send_sem.at[group[0], 2 + gap], chain_recv_sem.at[group[0], 3 + plane],
                      me + gap * PLANE)

    def members(group):
        return range(group[0], group[0] + group[1])

    def chain_post(group, step):
        for tile in members(group):
            csnd[tile, step, :deep] = tot[tile, :deep].astype(jnp.bfloat16)
            through = tot[tile, deep:]
            csnd[tile, step, deep:] = jnp.concatenate([through, through]).astype(jnp.bfloat16)
        if step < 3:
            chain_copy(group, step).start()
        else:
            for gap in range(1, zs):
                pl.when(z + gap < zs)(line_copy(group, gap, z).start)

    def message(tile, step, first, rows):
        return crcv[tile, step, first : first + rows].astype(f32)

    def spans(tile, first, doublings):
        found = [span_t[tile * deep + first : tile * deep + first + chunk]]
        for _ in range(doublings):
            found.append(found[-1] * found[-1])
        return found

    def before_me(found, step):
        product = None
        for bit in range(step):
            factor = jnp.where(bits[bit] == 1, found[bit], 1.0)
            product = factor if product is None else product * factor
        return product

    def chain_step(group, step):
        chain_copy(group, step).wait_recv()
        upper = bits[step] == 1
        for tile in members(group):
            through_mine = tot[tile, deep:]
            through_other = message(tile, step, deep, 16)[:GROUPS]
            through_late = jnp.where(upper, through_mine, through_other)[0:1]
            if step:
                through_pre = pre[tile, deep:]
            else:
                through_pre = jnp.ones((GROUPS, LANES), f32)
            for first in range(0, deep, chunk):
                rows = slice(first, first + chunk)
                found = spans(tile, first, step)
                mine = tot[tile, rows]
                other = message(tile, step, first, chunk)
                early = jnp.where(upper, other, mine)
                late = jnp.where(upper, mine, other)
                tot[tile, rows] = late + through_late * found[step] * early
                if step:
                    old = pre[tile, rows]
                    fade = through_pre[0:1] * before_me(found, step)
                    pre[tile, rows] = jnp.where(upper, old + fade * other, old)
                else:
                    pre[tile, rows] = jnp.where(upper, other, 0.0)
            tot[tile, deep:] = through_mine * through_other
            pre[tile, deep:] = jnp.where(upper, through_pre * through_other, through_pre)
        chain_post(group, step + 1)

    def chain_line(group):
        for plane in range(zs - 1):
            pl.when(plane < z)(line_copy(group, 1, plane).wait_recv)
        for tile in members(group):
            through_pre = pre[tile, deep : deep + 1]
            for first in range(0, deep, chunk):
                found = spans(tile, first, 3)
                entering = jnp.zeros((chunk, LANES), f32)
                for plane in range(zs - 1):
                    through = message(tile, 3 + plane, deep, 16)[0:1]
                    item = message(tile, 3 + plane, first, chunk)
                    entering = jnp.where(
                        plane < z, item + through * found[3] * entering, entering)
                ent[tile, first : first + chunk] = (
                    pre[tile, first : first + chunk]
                    + through_pre * before_me(found, 3) * entering)

    half = tokens // 2

    def act_copy(tile, part):
        cols = pl.ds(tile * TILE, TILE)
        return remote(acts.at[pl.ds(part * half, half), cols],
                      acts.at[pl.ds(tokens + part * half, half), cols],
                      act_sem.at[0, tile, part], act_sem.at[1, tile, part], x_peer)

    def queries(tile):
        load(0, tile).wait()

        def query_rows(row, first):
            mask1, mask2 = masks(row)
            for group in range(GROUPS):
                cols = slice(tile * TILE + group * LANES, tile * TILE + (group + 1) * LANES)
                acts[pl.ds(row, RB), cols] = short(0, row, cols, mask1, mask2, first)

        def rows(step, carry):
            query_rows(pl.multiple_of(step * RB, RB), False)
            return carry

        query_rows(0, True)
        lax.fori_loop(1, tokens // RB, rows, 0)

    def finish(tile, part):
        skip = skip_ref[tile * GROUPS : (tile + 1) * GROUPS, :]

        def advance(step, states):
            states = list(states)
            for inner in range(UNROLL):
                time = step * UNROLL + inner
                spot = pl.ds(pl.multiple_of(time * GROUPS, GROUPS), GROUPS)
                keep = jnp.where(time == cut, 0.0, 1.0)
                item = z_ref[tile, spot, :]
                sums = [skip * item, None]
                for mode in range(modes):
                    states[mode] = (table(fac_t, mode, tile) * keep) * states[mode] + item
                    term = table(res_t, mode, tile) * states[mode]
                    sums[mode % 2] = term if sums[mode % 2] is None else sums[mode % 2] + term
                z_ref[tile, spot, :] = sums[0] + sums[1]
            return tuple(states)

        def mix(step, carry):
            row = pl.multiple_of(step * RB, RB)
            for group in range(GROUPS):
                cols = slice(tile * TILE + group * LANES, tile * TILE + (group + 1) * LANES)
                mixed = z_ref[tile, pl.ds(row * GROUPS + group, RB, stride=GROUPS), :]
                query = acts[pl.ds(row, RB), cols].astype(f32)
                acts[pl.ds(row, RB), cols] = (query * mixed).astype(jnp.bfloat16)
            return carry

        spots = [slice(mode * GROUPS, (mode + 1) * GROUPS) for mode in range(modes)]
        states = tuple(ent[tile, spot] for spot in spots)
        steps = half // UNROLL
        states = lax.fori_loop(part * steps, (part + 1) * steps, advance, states)
        for spot, state in zip(spots, states):
            ent[tile, spot] = state
        steps = half // RB
        lax.fori_loop(part * steps, (part + 1) * steps, mix, 0)
        act_copy(tile, part).start()

    def columns(block, plane):
        return pl.ds(pl.multiple_of((block * 2 + plane) * 2 * feats, LANES), 2 * feats)

    def out_copy(block):
        return remote(obuf.at[block, pl.ds(tokens, tokens), :], out_hbm.at[:, columns(block, x)],
                      out_send_sem.at[block], out_recv_sem.at[block], x_peer)

    def own_out(block):
        return pltpu.make_async_copy(obuf.at[block, pl.ds(0, tokens), :],
                                     out_hbm.at[:, columns(block, x)], out_sem.at[block])

    def project_rows(block, first):
        rows = slice(first, first + tokens)
        obuf[block, rows] = lax.dot_general(
            acts[rows], wbuf[block], (((1,), (1,)), ((), ())), preferred_element_type=f32
        ).astype(jnp.bfloat16)

    def project_own(block):
        project_rows(block, 0)
        own_out(block).start()

    def project_other(block):
        project_rows(block, tokens)
        out_copy(block).start()

    def project(block):
        wait_sibling(block)
        project_other(block)

    one, two, rest = (0, 1), (1, 1), (2, tiles - 2)
    gate(0)
    gate(1)
    pl.when(me > 0)(rim_copy.wait_recv)
    for index in range(3):
        rimx[index] = jnp.zeros((8, channels), f32)
        rimx[index, 6:8, :] = rim_in[2 * index : 2 * index + 2, :]
    gate_rows(0, 0, True)
    end_states(0)
    chain_post(one, 0)
    gate_rows(1, 0, True)
    end_states(1)
    chain_step(one, 0)
    chain_post(two, 0)
    gate(2)
    gate_rows(2, 0, True)
    chain_step(two, 0)
    end_states(2)
    chain_step(one, 1)
    issue(0, 2, 1, across)
    for tile in range(3, tiles):
        gate(tile)
        gate_rows(tile, 0, True)
    chain_step(two, 1)
    issue(0, 3, 1, across)
    issue(1, 0, 1, across)
    for tile in range(3, tiles):
        end_states(tile)
    chain_step(one, 2)
    issue(1, 0, 2, both)
    chain_post(rest, 0)
    queries(0)
    chain_step(two, 2)
    issue(1, 2, 1, both)
    chain_step(rest, 0)
    issue(1, 1, 1, across)
    issue(last, 0, 1, both)
    poll_last_across()
    chain_line(one)
    finish(0, 0)
    queries(1)
    chain_step(rest, 1)
    issue(1, 2, 1, across)
    poll_line(1, 0, ways="y")
    finish(0, 1)
    poll_across(0, 0)
    chain_line(two)
    finish(1, 0)
    chain_step(rest, 2)
    poll_line(1, 0, ways="z")
    poll_line(1, 1)
    finish(1, 1)
    queries(2)
    queries(3)
    chain_line(rest)
    for tile in range(2, tiles):
        finish(tile, 0)
        finish(tile, 1)
    poll_across(0, 1)
    own_copy.wait()
    for distance in range(2, zs - 1):
        poll_line(distance, 0)
        for side in (0, 1):
            block = source(0) * 2 + (y if side == 0 else 1 - y)
            wait_sibling(block)
            project_own(block)
        poll_line(distance, 1)
    poll_last_line(1)
    poll_across(1, 0)
    poll_line(zs - 1, 0)
    for tile in range(tiles):
        for part in range(2):
            act_copy(tile, part).wait_recv()
    project_other(source(0) * 2 + y)
    project_other(source(0) * 2 + 1 - y)
    poll_line(zs - 1, 1)
    project(source(1) * 2 + y)
    poll_across(1, 1)
    project(source(1) * 2 + 1 - y)
    for rank in range(2, zs):
        poll_across(rank, 0)
        poll_last_line(rank)
        project(source(rank) * 2 + y)
        poll_across(rank, 1)
        project(source(rank) * 2 + 1 - y)

    for rank in range(1, zs):
        project_own(source(rank) * 2 + y)
        project_own(source(rank) * 2 + 1 - y)

    finish_own()
    for distance in range(1, zs):
        for part in range(last):
            poll_line(distance, part, True)
        poll_last_line(distance, True)
    for distance in range(zs):
        for part in range(last):
            poll_across(distance, part, True)
    poll_last_across(True)
    pl.when(me < n - 1)(rim_copy.wait_send)
    for group in (one, two, rest):
        for step in range(3):
            chain_copy(group, step).wait_send()
        for gap in range(1, zs):
            pl.when(z + gap < zs)(line_copy(group, gap, z).wait_send)
    for tile in range(tiles):
        for part in range(2):
            act_copy(tile, part).wait_send()
    for block in range(blocks):
        own_out(block).wait()
        out_copy(block).wait()


def fused(q_feat, k_feat, v_feat, short_taps, decay_rate, residue, skip_gain, out_weight,
          doc_starts, reset_flags):
    tokens, channels = q_feat.shape
    modes = decay_rate.shape[0]
    n = lax.axis_size("seq")
    zs = n // PLANE
    tiles = channels // TILE
    feats = out_weight.shape[0]
    f32, bf16 = jnp.float32, jnp.bfloat16
    vmem = pl.BlockSpec(memory_space=pltpu.VMEM)
    smem = pl.BlockSpec(memory_space=pltpu.SMEM)
    hbm = pl.BlockSpec(memory_space=pl.ANY)
    dma = pltpu.SemaphoreType.DMA
    table = pltpu.VMEM((modes * channels // LANES, LANES), f32)
    return pl.pallas_call(
        functools.partial(fused_kernel, zs),
        in_specs=[smem, smem, hbm, hbm, hbm, hbm, vmem, vmem, vmem, vmem],
        out_specs=hbm,
        out_shape=jax.ShapeDtypeStruct((tokens, n * feats), bf16),
        scratch_shapes=[
            pltpu.VMEM((2 * zs, 2 * feats, channels), bf16),
            pltpu.VMEM((3, tokens, channels), bf16),
            pltpu.VMEM((3, 16, channels), bf16),
            pltpu.VMEM((8, channels), f32),
            pltpu.VMEM((8, channels), f32),
            pltpu.VMEM((3, 8, channels), f32),
            pltpu.VMEM((tiles, tokens * GROUPS, LANES), f32),
            pltpu.VMEM((2 * tokens, channels), bf16),
            pltpu.VMEM((2 * zs, 2 * tokens, 2 * feats), bf16),
            table, table, table, table,
            pltpu.VMEM((tiles, 4, (modes + 2) * GROUPS, LANES), bf16),
            pltpu.VMEM((tiles, 2 + zs, (modes + 2) * GROUPS, LANES), bf16),
            pltpu.VMEM((tiles, (modes + 1) * GROUPS, LANES), f32),
            pltpu.VMEM((tiles, (modes + 1) * GROUPS, LANES), f32),
            pltpu.VMEM((tiles, modes * GROUPS, LANES), f32),
            dma((3, tiles)), dma((3,)), dma((2,)),
            dma((2 * zs, len(PARTS), 4)), dma((2, 2 * zs, len(PARTS))), dma,
            dma((tiles, 2 + zs)), dma((tiles, 2 + zs)), dma((2, tiles, 2)),
            dma((2 * zs,)), dma((2 * zs,)), dma((2 * zs,)),
        ],
        compiler_params=pltpu.CompilerParams(
            collective_id=0, has_side_effects=True, vmem_limit_bytes=58 * 2**20
        ),
        name="mixer",
    )(doc_starts, reset_flags, q_feat, k_feat, v_feat, out_weight, short_taps, decay_rate,
      residue, skip_gain.reshape(channels // LANES, LANES))


def local(q_feat, k_feat, v_feat, short_taps, decay_rate, residue, skip_gain, out_weight,
          doc_starts, reset_flags):
    tokens, channels = q_feat.shape
    modes = decay_rate.shape[0]
    kinds, taps = short_taps.shape[:2]
    n = lax.axis_size("seq")
    me = lax.axis_index("seq")
    tiles = channels // TILE
    heads = modes + 8

    weight = lax.all_gather(out_weight, "seq", axis=0, tiled=True)

    last_is_start = jnp.any(doc_starts[0] == tokens - 1)
    scale = jnp.stack([jnp.where(last_is_start, 0.0, 1.0), jnp.float32(1.0)]).astype(jnp.bfloat16)
    tails = jnp.stack([x[tokens - (taps - 1) :] for x in (q_feat, k_feat, v_feat)])
    tails = tails * scale[None, :, None]
    arrived = lax.ppermute(tails, "seq", [(i, i + 1) for i in range(n - 1)])
    rim = jnp.pad(arrived, ((0, 0), (ROWS - (taps - 1), 0), (0, 0)))

    rates = decay_rate.reshape(modes, channels // LANES, LANES)
    residues = residue.reshape(modes, channels // LANES, LANES)
    skips = skip_gain.reshape(channels // LANES, LANES)

    smem = pl.BlockSpec(memory_space=pltpu.SMEM)
    wide = pl.BlockSpec((tokens, TILE), lambda i: (0, i))
    deep = pl.BlockSpec((modes, GROUPS, LANES), lambda i: (0, i, 0))
    flat = pl.BlockSpec((None, tokens * GROUPS, LANES), lambda i: (i, 0, 0))
    f32 = jnp.float32
    qs, z, state = pl.pallas_call(
        local_kernel,
        grid=(tiles,),
        in_specs=[
            smem, smem, wide, wide, wide,
            pl.BlockSpec((kinds, ROWS, TILE), lambda i: (0, 0, i)),
            pl.BlockSpec((kinds * taps, TILE), lambda i: (0, i)),
            deep, deep,
            pl.BlockSpec((GROUPS, LANES), lambda i: (i, 0)),
        ],
        out_specs=[wide, flat, pl.BlockSpec((heads, GROUPS, LANES), lambda i: (0, i, 0))],
        out_shape=[
            jax.ShapeDtypeStruct((tokens, channels), jnp.bfloat16),
            jax.ShapeDtypeStruct((tiles, tokens * GROUPS, LANES), f32),
            jax.ShapeDtypeStruct((heads, channels // LANES, LANES), f32),
        ],
        scratch_shapes=[pltpu.VMEM((modes, GROUPS, LANES), f32)],
        cost_estimate=pl.CostEstimate(
            flops=tokens * channels * 80, bytes_accessed=tokens * channels * 12, transcendentals=0
        ),
        name="local_filter",
    )(doc_starts, reset_flags, q_feat, k_feat, v_feat, rim,
      short_taps.reshape(kinds * taps, channels), rates, residues, skips)

    part = channels // n
    sent = state.reshape(heads, n, part).transpose(1, 0, 2)
    pieces = lax.all_to_all(sent, "seq", 0, 0)
    my_rates = lax.dynamic_slice_in_dim(decay_rate, me * part, part, 1)
    chained = pl.pallas_call(
        functools.partial(scan_kernel, tokens),
        out_shape=jax.ShapeDtypeStruct((n, modes, part), f32),
        name="chain_states",
    )(pieces, my_rates)
    entering = lax.all_to_all(chained, "seq", 0, 0)
    entering = entering.transpose(1, 0, 2).reshape(modes, channels // LANES, LANES)

    mixed = pl.pallas_call(
        finish_kernel,
        grid=(tiles,),
        in_specs=[smem, smem, wide, flat, deep, deep, deep],
        out_specs=wide,
        out_shape=jax.ShapeDtypeStruct((tokens, channels), jnp.bfloat16),
        scratch_shapes=[
            pltpu.VMEM((modes, GROUPS, LANES), f32),
            pltpu.VMEM((tokens * GROUPS, LANES), f32),
        ],
        cost_estimate=pl.CostEstimate(
            flops=tokens * channels * 40, bytes_accessed=tokens * channels * 8, transcendentals=0
        ),
        name="finish_filter",
    )(doc_starts, reset_flags, qs, z, entering, rates, residues)

    projected = lax.dot_general(
        mixed, weight, (((1,), (1,)), ((), ())), preferred_element_type=f32
    ).astype(jnp.bfloat16)
    return lax.psum_scatter(projected, "ch", scatter_dimension=1, tiled=True)


def solution(mesh):
    placed = (
        P("seq", "ch"), P("seq", "ch"), P("seq", "ch"), P(None, None, "ch"), P(None, "ch"),
        P(None, "ch"), P("ch"), P("seq", "ch"), P("seq", None), P("seq", None),
    )
    direct = mesh.shape["ch"] == 1 and mesh.shape["seq"] in range(3 * PLANE, 2**16, PLANE)
    return jax.shard_map(
        fused if direct else local, mesh=mesh, in_specs=placed, out_specs=P("seq", "ch"), check_vma=False
    )
```

```python
import functools

import jax
import jax.numpy as jnp
from jax import lax
from jax.experimental import pallas as pl
from jax.experimental.pallas import tpu as pltpu
from jax.sharding import PartitionSpec as P

LANES = 128
GROUPS = 8
TILE = LANES * GROUPS
ROWS = 16
UNROLL = 8


def cut_of(starts, flags, tokens):
    cut = jnp.int32(tokens)
    for slot in range(starts.shape[1]):
        cut = jnp.where(flags[0, slot] == 1, jnp.minimum(cut, starts[0, slot]), cut)
    return cut


def local_kernel(starts, flags, q_ref, k_ref, v_ref, rim_ref, taps_ref, rate_ref, res_ref,
                 skip_ref, qs_ref, z_ref, state_ref, fac_ref):
    tokens = q_ref.shape[0]
    modes = rate_ref.shape[0]
    slots = starts.shape[1]
    cut = cut_of(starts, flags, tokens)

    def short_rows(step, carry):
        row = pl.multiple_of(step * ROWS, ROWS)
        back = pl.multiple_of(jnp.maximum(row - ROWS, 0), ROWS)
        at = lax.broadcasted_iota(jnp.int32, (ROWS, LANES), 0) + row
        hit = jnp.zeros((ROWS, LANES), jnp.bool_)
        hit_before = jnp.zeros((ROWS, LANES), jnp.bool_)
        for slot in range(slots):
            hit = hit | (at == starts[0, slot])
            hit_before = hit_before | (at - 1 == starts[0, slot])
        mask1 = jnp.where(hit, 0.0, 1.0)
        mask2 = jnp.where(hit | hit_before, 0.0, 1.0)
        first = step == 0
        for group in range(GROUPS):
            cols = slice(group * LANES, (group + 1) * LANES)

            def short(ref, index):
                x = ref[pl.ds(row, ROWS), cols].astype(jnp.float32)
                before = ref[pl.ds(back, ROWS), cols].astype(jnp.float32)
                rim = rim_ref[index, :, cols].astype(jnp.float32)
                before = jnp.where(first, rim, before)
                both = jnp.concatenate([before, x], axis=0)
                lag1 = pltpu.roll(both, 1, 0)[ROWS:]
                lag2 = pltpu.roll(both, 2, 0)[ROWS:]
                base = 3 * index
                summed = taps_ref[base : base + 1, cols] * x
                summed = summed + taps_ref[base + 1 : base + 2, cols] * mask1 * lag1
                summed = summed + taps_ref[base + 2 : base + 3, cols] * mask2 * lag2
                return summed.astype(jnp.bfloat16)

            qs_ref[pl.ds(row, ROWS), cols] = short(q_ref, 0)
            gated = short(k_ref, 1).astype(jnp.float32) * short(v_ref, 2).astype(jnp.float32)
            z_ref[pl.ds(row * GROUPS + group, ROWS, stride=GROUPS), :] = gated
        return carry

    lax.fori_loop(0, tokens // ROWS, short_rows, 0)

    fac_ref[...] = jnp.exp(-rate_ref[...])
    skip = skip_ref[...]

    def advance(step, states):
        states = list(states)
        for inner in range(UNROLL):
            time = step * UNROLL + inner
            spot = pl.ds(pl.multiple_of(time * GROUPS, GROUPS), GROUPS)
            keep = jnp.where(time == cut, 0.0, 1.0)
            x = z_ref[spot, :]
            sums = [skip * x, None]
            for n in range(modes):
                states[n] = (fac_ref[n] * keep) * states[n] + x
                term = res_ref[n] * states[n]
                sums[n % 2] = term if sums[n % 2] is None else sums[n % 2] + term
            z_ref[spot, :] = sums[0] + sums[1]
        return tuple(states)

    zero = jnp.zeros((GROUPS, LANES), jnp.float32)
    states = lax.fori_loop(0, tokens // UNROLL, advance, (zero,) * modes)
    for n in range(modes):
        state_ref[n] = states[n]
    through = jnp.where(cut < tokens, 0.0, 1.0)
    for n in range(modes, state_ref.shape[0]):
        state_ref[n] = zero + through


def scan_kernel(tokens, pieces_ref, rate_ref, out_ref):
    modes = rate_ref.shape[0]
    factor = jnp.exp(-float(tokens) * rate_ref[...])

    def hop(j, running):
        out_ref[j] = running
        piece = pieces_ref[j]
        return factor * piece[modes : modes + 1] * running + piece[:modes]

    lax.fori_loop(0, pieces_ref.shape[0], hop, jnp.zeros(rate_ref.shape, jnp.float32))


def finish_kernel(starts, flags, qs_ref, z_ref, enter_ref, rate_ref, res_ref, out_ref, fac_ref,
                  y_ref):
    tokens = qs_ref.shape[0]
    modes = rate_ref.shape[0]
    cut = cut_of(starts, flags, tokens)
    fac_ref[...] = jnp.exp(-rate_ref[...])

    def advance(step, weights):
        weights = list(weights)
        for inner in range(UNROLL):
            time = step * UNROLL + inner
            spot = pl.ds(pl.multiple_of(time * GROUPS, GROUPS), GROUPS)
            alive = jnp.where(time < cut, 1.0, 0.0)
            sums = [None, None]
            for n in range(modes):
                sums[n % 2] = weights[n] if sums[n % 2] is None else sums[n % 2] + weights[n]
                weights[n] = weights[n] * fac_ref[n]
            y_ref[spot, :] = z_ref[spot, :] + alive * (sums[0] + sums[1])
        return tuple(weights)

    begin = tuple(res_ref[n] * (fac_ref[n] * enter_ref[n]) for n in range(modes))
    lax.fori_loop(0, tokens // UNROLL, advance, begin)

    def mix_rows(step, carry):
        row = pl.multiple_of(step * ROWS, ROWS)
        for group in range(GROUPS):
            cols = slice(group * LANES, (group + 1) * LANES)
            y = y_ref[pl.ds(row * GROUPS + group, ROWS, stride=GROUPS), :]
            q = qs_ref[pl.ds(row, ROWS), cols].astype(jnp.float32)
            out_ref[pl.ds(row, ROWS), cols] = (q * y).astype(jnp.bfloat16)
        return carry

    lax.fori_loop(0, tokens // ROWS, mix_rows, 0)


PLANE = 8
RB = 32
PARTS = ((0, 64), (64, 48), (112, 16))
PIECE = 16


def fused_kernel(zs, starts, flags, q_hbm, k_hbm, v_hbm, w_hbm, taps_ref, rate_ref, res_ref,
                 skip_ref, out_hbm, wbuf, xin, tails, rim_out, rim_in, rimx, z_ref, acts, obuf,
                 fac_t, rate_t, span_t, res_t, csnd, crcv, tot, pre, ent, load_sem, tail_sem,
                 rim_sem, wsend, wrecv, own_sem, chain_send_sem, chain_recv_sem, act_sem,
                 out_send_sem, out_recv_sem, out_sem):
    _, tokens, channels = xin.shape
    modes = rate_ref.shape[0]
    slots = starts.shape[1]
    feats = w_hbm.shape[0]
    tiles = channels // TILE
    lane_groups = channels // LANES
    blocks = 2 * zs
    n = PLANE * zs
    f32 = jnp.float32

    me = lax.axis_index("seq")
    core = lax.rem(me, 2)
    x = lax.rem(me // 2, 2)
    y = lax.rem(me // 4, 2)
    z = me // PLANE
    sib = me + 1 - 2 * core
    x_peer = me + 2 - 4 * x
    y_peer = me + 4 - 8 * y
    up, down = me + PLANE, me - PLANE
    has_up, has_down = z < zs - 1, z > 0

    order = [sorted(range(zs), key=lambda s, at=at: (abs(s - at), s)) for at in range(zs)]

    def source(rank):
        at = jnp.int32(order[0][rank])
        for level in range(1, zs):
            at = jnp.where(z == level, order[level][rank], at)
        return at

    def remote(src, dst, send, recv, dev):
        return pltpu.make_async_remote_copy(
            src_ref=src, dst_ref=dst, send_sem=send, recv_sem=recv,
            device_id={"seq": dev}, device_id_type=pl.DeviceIdType.MESH,
        )

    def piece(block, side, part):
        first, rows = PARTS[part]
        row = pl.multiple_of(side * feats + first, 16)
        return wbuf.at[block, pl.ds(row, rows), :]

    def weight_copy(block, part, way, own):
        first, rows = PARTS[part]
        dst = piece(block, core, part)
        src = w_hbm.at[pl.ds(first, rows), :] if own else dst
        return remote(src, dst, wsend.at[block, part, way],
                      wrecv.at[1 if way == 3 else 0, block, part],
                      (up, down, y_peer, sib)[way])

    def wait_weight(block, part):
        first, rows = PARTS[part]
        dst = piece(block, core, part)
        remote(dst, dst, wsend.at[block, part, 0], wrecv.at[0, block, part], sib).wait_recv()

    def wait_sibling(block):
        for part in range(len(PARTS)):
            dst = piece(block, 1 - core, part)
            remote(dst, dst, wsend.at[block, part, 3], wrecv.at[1, block, part], sib).wait_recv()

    def forward(block, part, ways, own, done):
        for way, cond in ways:
            copy = weight_copy(block, part, way, own)
            act = copy.wait_send if done else copy.start
            if cond is None:
                act()
            else:
                pl.when(cond)(act)

    both = ((0, has_up), (1, has_down))
    here = z * 2 + y
    there = z * 2 + 1 - y
    last = len(PARTS) - 1

    def issue(part, first, count, ways):
        for index in range(first, first + count):
            row = PARTS[part][0] + index * PIECE
            spot = pl.ds(pl.multiple_of(core * feats + row, 16), PIECE)
            for way, cond in ways:
                copy = remote(w_hbm.at[pl.ds(row, PIECE), :], wbuf.at[here, spot, :],
                              wsend.at[here, part, way], wrecv.at[0, here, part],
                              (up, down, y_peer)[way])
                if cond is None:
                    copy.start()
                else:
                    pl.when(cond)(copy.start)

    across = ((2, None),)

    def finish_own():
        for part in range(last + 1):
            forward(here, part, both + ((2, None), (3, None)), True, True)

    def each_side(distance, act):
        pl.when(z >= distance)(lambda: act(z - distance, ((0, has_up),)))
        pl.when(z + distance < zs)(lambda: act(z + distance, ((1, has_down),)))

    def poll_line(distance, part, done=False, ways="yz"):
        def act(src, on_way):
            block = src * 2 + y
            if not done and "y" in ways:
                wait_weight(block, part)
            if "z" in ways:
                forward(block, part, on_way, False, done)
            if "y" in ways:
                forward(block, part, ((2, None), (3, None)), False, done)

        each_side(distance, act)

    def poll_across(rank, part, done=False):
        block = source(rank) * 2 + 1 - y
        if not done:
            wait_weight(block, part)
        forward(block, part, ((3, None),), False, done)

    def poll_last_across(done=False):
        if not done:
            wait_weight(there, last)
        forward(there, last, both + ((3, None),), False, done)

    def poll_last_line(distance, done=False):
        def act(src, on_way):
            for side in (y, 1 - y):
                block = src * 2 + side
                if not done:
                    wait_weight(block, last)
                forward(block, last, on_way + ((3, None),), False, done)

        each_side(distance, act)

    barrier = pltpu.get_barrier_semaphore()

    def greet(dev):
        pl.semaphore_signal(barrier, inc=1, device_id={"seq": dev},
                            device_id_type=pl.DeviceIdType.MESH)

    for dev in (sib, x_peer, y_peer):
        greet(dev)
    for gap in range(1, zs):
        pl.when(z + gap < zs)(lambda gap=gap: greet(me + gap * PLANE))
        pl.when(z >= gap)(lambda gap=gap: greet(me - gap * PLANE))
    pl.when(me < n - 1)(lambda: greet(me + 1))
    pl.when(me > 0)(lambda: greet(me - 1))

    feeds = (q_hbm, k_hbm, v_hbm)
    tail_copies = [
        pltpu.make_async_copy(feeds[i].at[pl.ds(tokens - 16, 16), :], tails.at[i], tail_sem.at[i])
        for i in range(3)
    ]
    for copy in tail_copies:
        copy.start()

    def load(index, tile):
        cols = pl.ds(tile * TILE, TILE)
        return pltpu.make_async_copy(feeds[index].at[:, cols], xin.at[index, :, cols],
                                     load_sem.at[index, tile])

    for index in (1, 2, 0):
        for tile in range(tiles):
            load(index, tile).start()
    own_copy = pltpu.make_async_copy(
        w_hbm, wbuf.at[here, pl.ds(pl.multiple_of(core * feats, 16), feats), :], own_sem)
    own_copy.start()

    cut = cut_of(starts, flags, tokens)
    through_me = jnp.where(cut < tokens, 0.0, 1.0)
    live = jnp.where(cut < tokens, cut, 0)
    final_start = jnp.float32(1.0)
    for slot in range(slots):
        final_start = jnp.where(starts[0, slot] == tokens - 1, 0.0, final_start)

    for copy in tail_copies:
        copy.wait()
    for index in range(3):
        two = tails[index, 8:16, :].astype(f32)
        rim_out[2 * index : 2 * index + 1, :] = two[6:7] * final_start
        rim_out[2 * index + 1 : 2 * index + 2, :] = two[7:8]
    rim_out[6:8, :] = jnp.zeros((2, channels), f32)
    rim_copy = remote(rim_out, rim_in, rim_sem.at[0], rim_sem.at[1], me + 1)

    pl.semaphore_wait(
        barrier, 3 + zs - 1 + jnp.where(me < n - 1, 1, 0) + jnp.where(me > 0, 1, 0))
    pl.when(me < n - 1)(rim_copy.start)
    issue(last, 0, 1, across)
    issue(0, 0, 2, across)
    issue(0, 0, 4, both)
    for part in range(last + 1):
        forward(here, part, ((3, None),), True, False)

    for half in range(modes // 8):
        for group in range(lane_groups):
            cols = slice(group * LANES, (group + 1) * LANES)
            tile, at = group // GROUPS, group % GROUPS
            spot = pl.ds((tile * modes + half * 8) * GROUPS + at, 8, stride=GROUPS)
            rate_t[spot, :] = rate_ref[half * 8 : half * 8 + 8, cols]
            res_t[spot, :] = res_ref[half * 8 : half * 8 + 8, cols]

    def fill_factors(step, carry):
        rows = pl.ds(pl.multiple_of(step * 32, 32), 32)
        fac_t[rows, :] = jnp.exp(-rate_t[rows, :])
        span_t[rows, :] = jnp.exp(-float(tokens) * rate_t[rows, :])
        return carry

    lax.fori_loop(0, modes * lane_groups // 32, fill_factors, 0)

    def table(ref, mode, tile):
        first = (tile * modes + mode) * GROUPS
        return ref[first : first + GROUPS, :]

    for plane in range(zs - 1):

        @pl.when(z <= plane)
        def _(plane=plane):
            for tile in range(tiles):
                crcv[tile, 3 + plane] = jnp.zeros(crcv.shape[2:], crcv.dtype)

    @pl.when(me == 0)
    def _():
        rim_in[...] = jnp.zeros(rim_in.shape, f32)

    def masks(row):
        at = lax.broadcasted_iota(jnp.int32, (RB, LANES), 0) + row
        hit = jnp.zeros((RB, LANES), jnp.bool_)
        hit_before = jnp.zeros((RB, LANES), jnp.bool_)
        for slot in range(slots):
            hit = hit | (at == starts[0, slot])
            hit_before = hit_before | (at - 1 == starts[0, slot])
        return jnp.where(hit, 0.0, 1.0), jnp.where(hit | hit_before, 0.0, 1.0)

    def short(index, row, cols, mask1, mask2, first):
        now = xin[index, pl.ds(row, RB), cols].astype(f32)
        if first:
            before = rimx[index, :, cols]
        else:
            before = xin[index, pl.ds(pl.multiple_of(row - 16, 16), 16), cols].astype(f32)[8:]
        joined = jnp.concatenate([before, now], axis=0)
        lag1 = pltpu.roll(joined, 1, 0)[8:]
        lag2 = pltpu.roll(joined, 2, 0)[8:]
        summed = taps_ref[index, 0:1, cols] * now
        summed = summed + taps_ref[index, 1:2, cols] * mask1 * lag1
        summed = summed + taps_ref[index, 2:3, cols] * mask2 * lag2
        return summed.astype(jnp.bfloat16)

    def gate_rows(tile, row, first):
        mask1, mask2 = masks(row)
        for group in range(GROUPS):
            cols = slice(tile * TILE + group * LANES, tile * TILE + (group + 1) * LANES)
            key = short(1, row, cols, mask1, mask2, first).astype(f32)
            value = short(2, row, cols, mask1, mask2, first).astype(f32)
            z_ref[tile, pl.ds(row * GROUPS + group, RB, stride=GROUPS), :] = key * value

    def gate(tile):
        load(1, tile).wait()
        load(2, tile).wait()

        def rows(step, carry):
            gate_rows(tile, pl.multiple_of(step * RB, RB), False)
            return carry

        lax.fori_loop(1, tokens // RB, rows, 0)

    def end_states(tile):
        zero = jnp.zeros((GROUPS, LANES), f32)

        def advance(step, states):
            states = list(states)
            for inner in range(UNROLL):
                time = step * UNROLL + inner
                spot = pl.ds(pl.multiple_of(time * GROUPS, GROUPS), GROUPS)
                item = z_ref[tile, spot, :] * jnp.where(time >= live, 1.0, 0.0)
                for mode in range(modes):
                    states[mode] = table(fac_t, mode, tile) * states[mode] + item
            return tuple(states)

        states = lax.fori_loop(0, tokens // UNROLL, advance, (zero,) * modes)
        for mode in range(modes):
            tot[tile, mode * GROUPS : (mode + 1) * GROUPS] = states[mode]
        tot[tile, deep:] = zero + through_me

    peers = (sib, x_peer, y_peer)
    bits = (core, x, y)
    deep = modes * GROUPS
    chunk = 4 * GROUPS

    def chain_copy(group, step):
        at = pl.ds(group[0], group[1])
        return remote(csnd.at[at, step], crcv.at[at, step], chain_send_sem.at[group[0], step],
                      chain_recv_sem.at[group[0], step], peers[step])

    def line_copy(group, gap, plane):
        at = pl.ds(group[0], group[1])
        return remote(csnd.at[at, 3], crcv.at[at, 3 + plane],
                      chain_send_sem.at[group[0], 2 + gap], chain_recv_sem.at[group[0], 3 + plane],
                      me + gap * PLANE)

    def members(group):
        return range(group[0], group[0] + group[1])

    def chain_post(group, step):
        for tile in members(group):
            csnd[tile, step, :deep] = tot[tile, :deep].astype(jnp.bfloat16)
            through = tot[tile, deep:]
            csnd[tile, step, deep:] = jnp.concatenate([through, through]).astype(jnp.bfloat16)
        if step < 3:
            chain_copy(group, step).start()
        else:
            for gap in range(1, zs):
                pl.when(z + gap < zs)(line_copy(group, gap, z).start)

    def message(tile, step, first, rows):
        return crcv[tile, step, first : first + rows].astype(f32)

    def spans(tile, first, doublings):
        found = [span_t[tile * deep + first : tile * deep + first + chunk]]
        for _ in range(doublings):
            found.append(found[-1] * found[-1])
        return found

    def before_me(found, step):
        product = None
        for bit in range(step):
            factor = jnp.where(bits[bit] == 1, found[bit], 1.0)
            product = factor if product is None else product * factor
        return product

    def chain_step(group, step):
        chain_copy(group, step).wait_recv()
        upper = bits[step] == 1
        for tile in members(group):
            through_mine = tot[tile, deep:]
            through_other = message(tile, step, deep, 16)[:GROUPS]
            through_late = jnp.where(upper, through_mine, through_other)[0:1]
            if step:
                through_pre = pre[tile, deep:]
            else:
                through_pre = jnp.ones((GROUPS, LANES), f32)
            for first in range(0, deep, chunk):
                rows = slice(first, first + chunk)
                found = spans(tile, first, step)
                mine = tot[tile, rows]
                other = message(tile, step, first, chunk)
                early = jnp.where(upper, other, mine)
                late = jnp.where(upper, mine, other)
                tot[tile, rows] = late + through_late * found[step] * early
                if step:
                    old = pre[tile, rows]
                    fade = through_pre[0:1] * before_me(found, step)
                    pre[tile, rows] = jnp.where(upper, old + fade * other, old)
                else:
                    pre[tile, rows] = jnp.where(upper, other, 0.0)
            tot[tile, deep:] = through_mine * through_other
            pre[tile, deep:] = jnp.where(upper, through_pre * through_other, through_pre)
        chain_post(group, step + 1)

    def chain_line(group):
        for plane in range(zs - 1):
            pl.when(plane < z)(line_copy(group, 1, plane).wait_recv)
        for tile in members(group):
            through_pre = pre[tile, deep : deep + 1]
            for first in range(0, deep, chunk):
                found = spans(tile, first, 3)
                entering = jnp.zeros((chunk, LANES), f32)
                for plane in range(zs - 1):
                    through = message(tile, 3 + plane, deep, 16)[0:1]
                    item = message(tile, 3 + plane, first, chunk)
                    entering = jnp.where(
                        plane < z, item + through * found[3] * entering, entering)
                ent[tile, first : first + chunk] = (
                    pre[tile, first : first + chunk]
                    + through_pre * before_me(found, 3) * entering)

    half = tokens // 2

    def act_copy(tile, part):
        cols = pl.ds(tile * TILE, TILE)
        return remote(acts.at[pl.ds(part * half, half), cols],
                      acts.at[pl.ds(tokens + part * half, half), cols],
                      act_sem.at[0, tile, part], act_sem.at[1, tile, part], x_peer)

    def queries(tile):
        load(0, tile).wait()

        def query_rows(row, first):
            mask1, mask2 = masks(row)
            for group in range(GROUPS):
                cols = slice(tile * TILE + group * LANES, tile * TILE + (group + 1) * LANES)
                acts[pl.ds(row, RB), cols] = short(0, row, cols, mask1, mask2, first)

        def rows(step, carry):
            query_rows(pl.multiple_of(step * RB, RB), False)
            return carry

        query_rows(0, True)
        lax.fori_loop(1, tokens // RB, rows, 0)

    def finish(tile, part):
        skip = skip_ref[tile * GROUPS : (tile + 1) * GROUPS, :]

        def advance(step, states):
            states = list(states)
            for inner in range(UNROLL):
                time = step * UNROLL + inner
                spot = pl.ds(pl.multiple_of(time * GROUPS, GROUPS), GROUPS)
                keep = jnp.where(time == cut, 0.0, 1.0)
                item = z_ref[tile, spot, :]
                sums = [skip * item, None]
                for mode in range(modes):
                    states[mode] = (table(fac_t, mode, tile) * keep) * states[mode] + item
                    term = table(res_t, mode, tile) * states[mode]
                    sums[mode % 2] = term if sums[mode % 2] is None else sums[mode % 2] + term
                z_ref[tile, spot, :] = sums[0] + sums[1]
            return tuple(states)

        def mix(step, carry):
            row = pl.multiple_of(step * RB, RB)
            for group in range(GROUPS):
                cols = slice(tile * TILE + group * LANES, tile * TILE + (group + 1) * LANES)
                mixed = z_ref[tile, pl.ds(row * GROUPS + group, RB, stride=GROUPS), :]
                query = acts[pl.ds(row, RB), cols].astype(f32)
                acts[pl.ds(row, RB), cols] = (query * mixed).astype(jnp.bfloat16)
            return carry

        spots = [slice(mode * GROUPS, (mode + 1) * GROUPS) for mode in range(modes)]
        states = tuple(ent[tile, spot] for spot in spots)
        steps = half // UNROLL
        states = lax.fori_loop(part * steps, (part + 1) * steps, advance, states)
        for spot, state in zip(spots, states):
            ent[tile, spot] = state
        steps = half // RB
        lax.fori_loop(part * steps, (part + 1) * steps, mix, 0)
        act_copy(tile, part).start()

    def columns(block, plane):
        return pl.ds(pl.multiple_of((block * 2 + plane) * 2 * feats, LANES), 2 * feats)

    def out_copy(block):
        return remote(obuf.at[block, pl.ds(tokens, tokens), :], out_hbm.at[:, columns(block, x)],
                      out_send_sem.at[block], out_recv_sem.at[block], x_peer)

    def own_out(block):
        return pltpu.make_async_copy(obuf.at[block, pl.ds(0, tokens), :],
                                     out_hbm.at[:, columns(block, x)], out_sem.at[block])

    def project_rows(block, first):
        rows = slice(first, first + tokens)
        obuf[block, rows] = lax.dot_general(
            acts[rows], wbuf[block], (((1,), (1,)), ((), ())), preferred_element_type=f32
        ).astype(jnp.bfloat16)

    def project_own(block):
        project_rows(block, 0)
        own_out(block).start()

    def project_other(block):
        project_rows(block, tokens)
        out_copy(block).start()

    def project(block):
        wait_sibling(block)
        project_other(block)

    one, two, rest = (0, 1), (1, 1), (2, tiles - 2)
    gate(0)
    gate(1)
    pl.when(me > 0)(rim_copy.wait_recv)
    for index in range(3):
        rimx[index] = jnp.zeros((8, channels), f32)
        rimx[index, 6:8, :] = rim_in[2 * index : 2 * index + 2, :]
    gate_rows(0, 0, True)
    end_states(0)
    chain_post(one, 0)
    gate_rows(1, 0, True)
    end_states(1)
    chain_step(one, 0)
    chain_post(two, 0)
    gate(2)
    gate_rows(2, 0, True)
    chain_step(two, 0)
    end_states(2)
    chain_step(one, 1)
    issue(0, 2, 1, across)
    for tile in range(3, tiles):
        gate(tile)
        gate_rows(tile, 0, True)
    chain_step(two, 1)
    issue(0, 3, 1, across)
    issue(1, 0, 1, across)
    for tile in range(3, tiles):
        end_states(tile)
    chain_step(one, 2)
    issue(1, 0, 2, both)
    chain_post(rest, 0)
    queries(0)
    chain_step(two, 2)
    issue(1, 2, 1, both)
    chain_step(rest, 0)
    issue(1, 1, 1, across)
    issue(last, 0, 1, both)
    poll_last_across()
    chain_line(one)
    finish(0, 0)
    queries(1)
    chain_step(rest, 1)
    issue(1, 2, 1, across)
    poll_line(1, 0, ways="y")
    finish(0, 1)
    poll_across(0, 0)
    chain_line(two)
    finish(1, 0)
    chain_step(rest, 2)
    poll_line(1, 0, ways="z")
    poll_line(1, 1)
    finish(1, 1)
    queries(2)
    queries(3)
    chain_line(rest)
    for tile in range(2, tiles):
        finish(tile, 0)
        finish(tile, 1)
    poll_across(0, 1)
    own_copy.wait()
    for distance in range(2, zs - 1):
        poll_line(distance, 0)
        for side in (0, 1):
            block = source(0) * 2 + (y if side == 0 else 1 - y)
            wait_sibling(block)
            project_own(block)
        poll_line(distance, 1)
    poll_last_line(1)
    poll_across(1, 0)
    poll_line(zs - 1, 0)
    for tile in range(tiles):
        for part in range(2):
            act_copy(tile, part).wait_recv()
    project_other(source(0) * 2 + y)
    project_other(source(0) * 2 + 1 - y)
    project(source(1) * 2 + y)
    poll_line(zs - 1, 1)
    poll_across(1, 1)
    project(source(1) * 2 + 1 - y)
    for rank in range(2, zs):
        poll_across(rank, 0)
        poll_last_line(rank)
        project(source(rank) * 2 + y)
        poll_across(rank, 1)
        project(source(rank) * 2 + 1 - y)

    for rank in range(1, zs):
        project_own(source(rank) * 2 + y)
        project_own(source(rank) * 2 + 1 - y)

    finish_own()
    for distance in range(1, zs):
        for part in range(last):
            poll_line(distance, part, True)
        poll_last_line(distance, True)
    for distance in range(zs):
        for part in range(last):
            poll_across(distance, part, True)
    poll_last_across(True)
    pl.when(me < n - 1)(rim_copy.wait_send)
    for group in (one, two, rest):
        for step in range(3):
            chain_copy(group, step).wait_send()
        for gap in range(1, zs):
            pl.when(z + gap < zs)(line_copy(group, gap, z).wait_send)
    for tile in range(tiles):
        for part in range(2):
            act_copy(tile, part).wait_send()
    for block in range(blocks):
        own_out(block).wait()
        out_copy(block).wait()


def fused(q_feat, k_feat, v_feat, short_taps, decay_rate, residue, skip_gain, out_weight,
          doc_starts, reset_flags):
    tokens, channels = q_feat.shape
    modes = decay_rate.shape[0]
    n = lax.axis_size("seq")
    zs = n // PLANE
    tiles = channels // TILE
    feats = out_weight.shape[0]
    f32, bf16 = jnp.float32, jnp.bfloat16
    vmem = pl.BlockSpec(memory_space=pltpu.VMEM)
    smem = pl.BlockSpec(memory_space=pltpu.SMEM)
    hbm = pl.BlockSpec(memory_space=pl.ANY)
    dma = pltpu.SemaphoreType.DMA
    table = pltpu.VMEM((modes * channels // LANES, LANES), f32)
    return pl.pallas_call(
        functools.partial(fused_kernel, zs),
        in_specs=[smem, smem, hbm, hbm, hbm, hbm, vmem, vmem, vmem, vmem],
        out_specs=hbm,
        out_shape=jax.ShapeDtypeStruct((tokens, n * feats), bf16),
        scratch_shapes=[
            pltpu.VMEM((2 * zs, 2 * feats, channels), bf16),
            pltpu.VMEM((3, tokens, channels), bf16),
            pltpu.VMEM((3, 16, channels), bf16),
            pltpu.VMEM((8, channels), f32),
            pltpu.VMEM((8, channels), f32),
            pltpu.VMEM((3, 8, channels), f32),
            pltpu.VMEM((tiles, tokens * GROUPS, LANES), f32),
            pltpu.VMEM((2 * tokens, channels), bf16),
            pltpu.VMEM((2 * zs, 2 * tokens, 2 * feats), bf16),
            table, table, table, table,
            pltpu.VMEM((tiles, 4, (modes + 2) * GROUPS, LANES), bf16),
            pltpu.VMEM((tiles, 2 + zs, (modes + 2) * GROUPS, LANES), bf16),
            pltpu.VMEM((tiles, (modes + 1) * GROUPS, LANES), f32),
            pltpu.VMEM((tiles, (modes + 1) * GROUPS, LANES), f32),
            pltpu.VMEM((tiles, modes * GROUPS, LANES), f32),
            dma((3, tiles)), dma((3,)), dma((2,)),
            dma((2 * zs, len(PARTS), 4)), dma((2, 2 * zs, len(PARTS))), dma,
            dma((tiles, 2 + zs)), dma((tiles, 2 + zs)), dma((2, tiles, 2)),
            dma((2 * zs,)), dma((2 * zs,)), dma((2 * zs,)),
        ],
        compiler_params=pltpu.CompilerParams(
            collective_id=0, has_side_effects=True, vmem_limit_bytes=58 * 2**20
        ),
        name="mixer",
    )(doc_starts, reset_flags, q_feat, k_feat, v_feat, out_weight, short_taps, decay_rate,
      residue, skip_gain.reshape(channels // LANES, LANES))


def local(q_feat, k_feat, v_feat, short_taps, decay_rate, residue, skip_gain, out_weight,
          doc_starts, reset_flags):
    tokens, channels = q_feat.shape
    modes = decay_rate.shape[0]
    kinds, taps = short_taps.shape[:2]
    n = lax.axis_size("seq")
    me = lax.axis_index("seq")
    tiles = channels // TILE
    heads = modes + 8

    weight = lax.all_gather(out_weight, "seq", axis=0, tiled=True)

    last_is_start = jnp.any(doc_starts[0] == tokens - 1)
    scale = jnp.stack([jnp.where(last_is_start, 0.0, 1.0), jnp.float32(1.0)]).astype(jnp.bfloat16)
    tails = jnp.stack([x[tokens - (taps - 1) :] for x in (q_feat, k_feat, v_feat)])
    tails = tails * scale[None, :, None]
    arrived = lax.ppermute(tails, "seq", [(i, i + 1) for i in range(n - 1)])
    rim = jnp.pad(arrived, ((0, 0), (ROWS - (taps - 1), 0), (0, 0)))

    rates = decay_rate.reshape(modes, channels // LANES, LANES)
    residues = residue.reshape(modes, channels // LANES, LANES)
    skips = skip_gain.reshape(channels // LANES, LANES)

    smem = pl.BlockSpec(memory_space=pltpu.SMEM)
    wide = pl.BlockSpec((tokens, TILE), lambda i: (0, i))
    deep = pl.BlockSpec((modes, GROUPS, LANES), lambda i: (0, i, 0))
    flat = pl.BlockSpec((None, tokens * GROUPS, LANES), lambda i: (i, 0, 0))
    f32 = jnp.float32
    qs, z, state = pl.pallas_call(
        local_kernel,
        grid=(tiles,),
        in_specs=[
            smem, smem, wide, wide, wide,
            pl.BlockSpec((kinds, ROWS, TILE), lambda i: (0, 0, i)),
            pl.BlockSpec((kinds * taps, TILE), lambda i: (0, i)),
            deep, deep,
            pl.BlockSpec((GROUPS, LANES), lambda i: (i, 0)),
        ],
        out_specs=[wide, flat, pl.BlockSpec((heads, GROUPS, LANES), lambda i: (0, i, 0))],
        out_shape=[
            jax.ShapeDtypeStruct((tokens, channels), jnp.bfloat16),
            jax.ShapeDtypeStruct((tiles, tokens * GROUPS, LANES), f32),
            jax.ShapeDtypeStruct((heads, channels // LANES, LANES), f32),
        ],
        scratch_shapes=[pltpu.VMEM((modes, GROUPS, LANES), f32)],
        cost_estimate=pl.CostEstimate(
            flops=tokens * channels * 80, bytes_accessed=tokens * channels * 12, transcendentals=0
        ),
        name="local_filter",
    )(doc_starts, reset_flags, q_feat, k_feat, v_feat, rim,
      short_taps.reshape(kinds * taps, channels), rates, residues, skips)

    part = channels // n
    sent = state.reshape(heads, n, part).transpose(1, 0, 2)
    pieces = lax.all_to_all(sent, "seq", 0, 0)
    my_rates = lax.dynamic_slice_in_dim(decay_rate, me * part, part, 1)
    chained = pl.pallas_call(
        functools.partial(scan_kernel, tokens),
        out_shape=jax.ShapeDtypeStruct((n, modes, part), f32),
        name="chain_states",
    )(pieces, my_rates)
    entering = lax.all_to_all(chained, "seq", 0, 0)
    entering = entering.transpose(1, 0, 2).reshape(modes, channels // LANES, LANES)

    mixed = pl.pallas_call(
        finish_kernel,
        grid=(tiles,),
        in_specs=[smem, smem, wide, flat, deep, deep, deep],
        out_specs=wide,
        out_shape=jax.ShapeDtypeStruct((tokens, channels), jnp.bfloat16),
        scratch_shapes=[
            pltpu.VMEM((modes, GROUPS, LANES), f32),
            pltpu.VMEM((tokens * GROUPS, LANES), f32),
        ],
        cost_estimate=pl.CostEstimate(
            flops=tokens * channels * 40, bytes_accessed=tokens * channels * 8, transcendentals=0
        ),
        name="finish_filter",
    )(doc_starts, reset_flags, qs, z, entering, rates, residues)

    projected = lax.dot_general(
        mixed, weight, (((1,), (1,)), ((), ())), preferred_element_type=f32
    ).astype(jnp.bfloat16)
    return lax.psum_scatter(projected, "ch", scatter_dimension=1, tiled=True)


def solution(mesh):
    placed = (
        P("seq", "ch"), P("seq", "ch"), P("seq", "ch"), P(None, None, "ch"), P(None, "ch"),
        P(None, "ch"), P("ch"), P("seq", "ch"), P("seq", None), P("seq", None),
    )
    direct = mesh.shape["ch"] == 1 and mesh.shape["seq"] in range(3 * PLANE, 2**16, PLANE)
    return jax.shard_map(
        fused if direct else local, mesh=mesh, in_specs=placed, out_specs=P("seq", "ch"), check_vma=False
    )
```
